32 devices in a mesh: seq: 16 (over z, y, x), head: 2 (over core).
Axes of the slice: x: 2, y: 2, z: 4, core: 2. Of those that a mesh axis runs over, the one named last changes fastest.
Arguments:
- x_in: bfloat16 [2, 2048, 8192], P(None, 'seq', 'head'), may hold values from -6 to 6
- target: bfloat16 [2, 2048, 8192], P(None, 'seq', 'head'), may hold values from -6 to 6
- b_in: bfloat16 [2, 2048, 1024], P(None, 'seq', 'head'), may hold values from -0.125 to 0.125
- c_in: bfloat16 [2, 2048, 1024], P(None, 'seq', 'head'), may hold values from -0.5 to 0.5
- dt_raw: float32 [2, 128, 2048], P(None, 'head', 'seq'), may hold values from -1 to 2.3
- resets: int32 [2, 2048], P(None, 'seq'), may hold values 0 or 1
- decay_rate: float32 [128], P('head'), may hold values from 0 to 1
- conv_w: float32 [4, 8192], P(None, 'head'), may hold values from -3 to 3
- label: int32 [1], replicated, may hold values from 0 to 1
Outputs:
- loss: float32 [], replicated
- grad_x: bfloat16 [2, 2048, 8192], P(None, 'seq', 'head')
- grad_dt: float32 [2, 128, 2048], P(None, 'head', 'seq')
The draws below stay inside these ranges and needn't reach their ends.
All inputs are finite; a program needn't handle non-finite values. No bound on the sum of `resets` on one device may be relied on, other than what follows from the above.
Results may differ from the reference program's by a relative error of at most 0.001.
Values may be sent and summed in bfloat16 or wider, within the bound.
A program may use at most 320 MiB of HBM per device.

```python
import math
import jax
import jax.numpy as jnp
from jax import lax

HEADS = 128
HEADDIM = 64
DSTATE = 128
GROUPS = 8
KERNEL = 4
SPAN = 128
INNER = 8192
LENGTH = 2048


def draw_decay_rate(key, part):
    pick_key, fast_key, slow_key = jax.random.split(key, 3)
    share = 0.5
    quick = jax.random.bernoulli(pick_key, share, (HEADS,))
    fast = jnp.exp(jax.random.uniform(fast_key, (HEADS,), jnp.float32, math.log(1.0 / 55.0), math.log(1.0 / 33.0)))
    slow = jnp.exp(jax.random.uniform(slow_key, (HEADS,), jnp.float32, math.log(0.2 / LENGTH), math.log(1.2 / LENGTH)))
    return jnp.where(quick, fast, slow).astype(jnp.float32)


def set_ends(values, own_key, least, largest):
    longest = values.shape.index(max(values.shape))
    spots = []
    for shift in (0, 1):
        where = [jax.random.randint(jax.random.fold_in(own_key, axis), (), 0, length) for axis, length in enumerate(values.shape)]
        where[longest] = (where[longest] + shift) % values.shape[longest]
        spots.append(tuple(where))
    return values.at[spots[0]].set(least).at[spots[1]].set(largest)


def level_of(own_key, shape, pieces, low, top_value):
    def one(position, parts):
        heights = jax.random.uniform(jax.random.fold_in(jax.random.fold_in(own_key, 6), position), (parts,), jnp.float32, low / len(pieces), top_value / len(pieces))
        return jnp.repeat(jnp.exp(heights), shape[position] // parts).reshape((-1,) + (1,) * (len(shape) - position - 1))

    factor_of = one(*pieces[0])
    for cut in pieces[1:]:
        factor_of = factor_of * one(*cut)
    return factor_of


def noise(rng, extent, scale, most, shards=(), held_as=jnp.bfloat16):
    drawn = jax.random.normal(rng, extent, jnp.float32) * scale
    if len(shards) > 0:
        drawn = level_of(rng, extent, shards, -0.22, 0.18) * drawn
    return jnp.clip(drawn, min=-most, max=most).astype(held_as)


def setup_inputs(seed: int = 0) -> dict:
    streams_of = jax.random.split(jax.random.key(seed), 10)
    return {
        "x_in": noise(streams_of[0], (2, LENGTH, INNER), 1.0, 6.0, ((1, 16), (2, 2))),
        "target": noise(streams_of[1], (2, LENGTH, INNER), 1.0, 6.0, ((1, 16), (2, 2))),
        "b_in": noise(streams_of[2], (2, LENGTH, GROUPS * DSTATE), LENGTH ** -0.5, 0.125, ((1, 16), (2, 2))),
        "c_in": noise(streams_of[3], (2, LENGTH, GROUPS * DSTATE), DSTATE ** -0.5, 0.5, ((1, 16), (2, 2))),
        "dt_raw": jnp.clip(-1.0 + 3.3 * jax.random.uniform(streams_of[4], (2, HEADS, LENGTH), jnp.float32) ** level_of(streams_of[4], (2, HEADS, LENGTH), ((1, 2), (2, 16)), -0.2, 0.2), -1.0, 2.3),
        "resets": set_ends((jax.random.randint(streams_of[5], (2, LENGTH), 0, LENGTH) < 3).astype(jnp.int32), jax.random.fold_in(streams_of[5], 1), 0, 1),
        "decay_rate": draw_decay_rate(jax.random.fold_in(streams_of[9], 71), 0),
        "conv_w": noise(streams_of[7], (KERNEL, INNER), KERNEL ** -0.5, 3.0, ((1, 2),), jnp.float32),
        "label": jax.random.randint(streams_of[8], (1,), 0, 2).astype(jnp.int32),
    }


HIGH = lax.Precision.HIGHEST

def conv_silu(x_ext, keep_ext, conv_w):
    keep_now = keep_ext[2:][:, None]
    keep_two = keep_now * keep_ext[1:-1][:, None]
    keep_three = keep_two * keep_ext[:-2][:, None]
    pre = conv_w[3] * x_ext[3:] + keep_now * conv_w[2] * x_ext[2:-1]
    pre = pre + keep_two * conv_w[1] * x_ext[1:-2] + keep_three * conv_w[0] * x_ext[:-3]
    return jax.nn.silu(pre)

def ssd_span(state, values, steps, logs, marks, b_rows, c_rows):
    size, heads, width = values.shape
    ratio = heads // b_rows.shape[1]
    running = jnp.cumsum(logs, axis=1)
    seen = jnp.cumsum(marks)
    order = jnp.arange(size)
    valid = (order[:, None] >= order[None, :]) & (seen[:, None] == seen[None, :])
    gap = jnp.where(valid[None], running[:, :, None] - running[:, None, :], 0.0)
    decay = jnp.where(valid[None], jnp.exp(gap), 0.0)
    scores = jnp.einsum('ign,jgn->gij', c_rows, b_rows, precision=HIGH)
    scores = jnp.repeat(scores, ratio, axis=0)
    mixing = decay * scores * steps[:, None, :]
    intra = jnp.einsum('hij,jhp->ihp', mixing, values, precision=HIGH)
    b_heads = jnp.repeat(b_rows, ratio, axis=1)
    c_heads = jnp.repeat(c_rows, ratio, axis=1)
    entry = jnp.exp(running) * (seen == 0.0).astype(running.dtype)[None, :]
    carried = jnp.einsum('ihn,hpn->ihp', c_heads, state, precision=HIGH) * entry.T[:, :, None]
    tail = jnp.exp(running[:, -1:] - running) * (seen[-1] == seen).astype(running.dtype)[None, :] * steps
    weighted = values * tail.T[:, :, None]
    final = entry[:, -1][:, None, None] * state + jnp.einsum('jhp,jhn->hpn', weighted, b_heads, precision=HIGH)
    return (final, intra + carried)

def mixer_rows(state, values, steps, logs, marks, b_rows, c_rows, saving):
    rows, heads, width = values.shape
    count = rows // SPAN

    def blocks(array):
        return array.reshape((count, SPAN) + array.shape[1:])

    def blocks_heads(array):
        return array.reshape(heads, count, SPAN).transpose(1, 0, 2)
    step_fn = jax.checkpoint(ssd_span) if saving else ssd_span

    def advance(carry, block):
        return step_fn(carry, *block)
    final, outs = lax.scan(advance, state, (blocks(values), blocks_heads(steps), blocks_heads(logs), blocks(marks), blocks(b_rows), blocks(c_rows)))
    return (outs.reshape(rows, heads * width), final)

def local_pass(x_ext, raw, state, keep_ext, marks, b_rows, c_rows, conv_w, decay_rate, saving):
    rows = x_ext.shape[0] - 3
    heads = raw.shape[0]
    values = conv_silu(x_ext, keep_ext, conv_w).reshape(rows, heads, -1)
    steps = jax.nn.softplus(raw)
    logs = -steps * decay_rate[:, None]
    return mixer_rows(state, values, steps, logs, marks, b_rows, c_rows, saving)

def reference(x_in, target, b_in, c_in, dt_raw, resets, decay_rate, conv_w, label):
    marks = resets.astype(jnp.float32)
    keep_ext = jnp.concatenate([jnp.ones((2, 2), jnp.float32), 1.0 - marks], axis=1)
    b_rows = b_in.astype(jnp.float32).reshape(2, LENGTH, GROUPS, DSTATE)
    c_rows = c_in.astype(jnp.float32).reshape(2, LENGTH, GROUPS, DSTATE)
    target_f = target.astype(jnp.float32)
    count = LENGTH * INNER
    sign = jnp.where(jnp.arange(2) == label[0], 1.0, -1.0).astype(jnp.float32)

    def single(x_one, raw_one, state_one, keep_one, marks_one, b_one, c_one):
        return local_pass(x_one, raw_one, state_one, keep_one, marks_one, b_one, c_one, conv_w, decay_rate, True)

    def objective(x_full, raw_full):
        x_ext = jnp.concatenate([jnp.zeros((2, 3, INNER), jnp.float32), x_full], axis=1)
        start = jnp.zeros((2, HEADS, HEADDIM, DSTATE), jnp.float32)
        outs, finals = jax.vmap(single)(x_ext, raw_full, start, keep_ext, marks, b_rows, c_rows)
        scores = lax.optimization_barrier(jnp.sum(outs * target_f, axis=(1, 2))) / math.sqrt(count)
        margin = jnp.sum(sign * scores)
        return jax.nn.softplus(-margin)
    loss, pullback = jax.vjp(objective, x_in.astype(jnp.float32), dt_raw)
    grad_x, grad_dt = pullback(jnp.ones_like(loss) * math.sqrt(count))
    return (loss, grad_x.astype(jnp.bfloat16), grad_dt)
```

```python
import functools
import math

import jax
import jax.numpy as jnp
from jax import lax
from jax.experimental import pallas as pl
from jax.experimental.pallas import tpu as pltpu
from jax.sharding import Mesh
from jax.sharding import PartitionSpec as P

DSTATE = 128
SPAN = 128
LANES = 128
TAPS = 4
CUTS = 4
HALO = 16
FAR = -1e30
HIGH = lax.Precision.HIGHEST
F32 = jnp.float32
BF16 = jnp.bfloat16


def split(value):
    high = value.astype(BF16)
    low = (value - high.astype(F32)).astype(BF16)
    return high, low


def mm(left, right):
    return lax.dot_general(left, right, (((1,), (0,)), ((), ())), preferred_element_type=F32)


def mm_exact_left(left, right):
    high, low = split(right)
    return mm(left, high) + mm(left, low)


def mm_exact_right(left, right):
    high, low = split(left)
    return mm(high, right) + mm(low, right)


def spread_matrix(offset, chans, width):
    row = lax.broadcasted_iota(jnp.int32, (LANES, chans), 0)
    head = lax.broadcasted_iota(jnp.int32, (LANES, chans), 1) // width
    return jnp.where(row == head + offset, 1.0, 0.0).astype(BF16)


def gather_matrix(chans, width):
    head = lax.broadcasted_iota(jnp.int32, (chans, LANES), 0) // width
    col = lax.broadcasted_iota(jnp.int32, (chans, LANES), 1)
    return jnp.where(col == head, 1.0, 0.0).astype(BF16)


def conv_of(x_ref, xe_scr, w_ref, tok, lane, first):
    xe_scr[...] = x_ref[pl.ds(first, SPAN + HALO), :].astype(F32)
    pre = w_ref[3:4, :] * xe_scr[pl.ds(HALO, SPAN), :]
    for back in range(1, TAPS):
        scale = tok[:, lane + back - 1 : lane + back] * w_ref[3 - back : 4 - back, :]
        pre = pre + scale * xe_scr[pl.ds(HALO - back, SPAN), :]
    return pre


def ends_kernel(heads, count, x_ref, t_ref, bt_ref, ct_ref, tok_ref, w_ref, alone_ref, seed_ref, xe_scr):
    chans = x_ref.shape[1]
    width = chans // heads
    spread_entry = spread_matrix(heads, chans, width)
    spread_tail = spread_matrix(3 * heads, chans, width)
    alone_ref[...] = jnp.zeros_like(alone_ref)
    seed_ref[...] = jnp.zeros_like(seed_ref)

    def forward(k, carry):
        first = pl.multiple_of(k * SPAN, SPAN)
        tok = tok_ref[pl.ds(first, SPAN), :]
        values = jax.nn.silu(conv_of(x_ref, xe_scr, w_ref, tok, 5 * heads, first))
        weighted = values * mm_exact_right(tok, spread_tail)
        through = mm_exact_right(tok[SPAN - 8 :, :], spread_entry)[7:8, :]
        added = mm_exact_left(bt_ref[:, pl.ds(first, SPAN)], weighted)
        alone_ref[...] = through * alone_ref[...] + added
        return carry

    lax.fori_loop(0, count, forward, 0)

    def backward(step, carry):
        first = pl.multiple_of((count - 1 - step) * SPAN, SPAN)
        tok = tok_ref[pl.ds(first, SPAN), :]
        entry = mm_exact_right(tok, spread_entry)
        weighted = entry * t_ref[pl.ds(first, SPAN), :].astype(F32)
        added = mm_exact_left(ct_ref[:, pl.ds(first, SPAN)], weighted)
        seed_ref[...] = entry[SPAN - 1 : SPAN, :] * seed_ref[...] + added
        return carry

    lax.fori_loop(0, count, backward, 0)


def main_kernel(
    heads, count, x_ref, t_ref, b_ref, c_ref, bt_ref, ct_ref, tok_ref, row_ref, w_ref, rate_ref,
    start_ref, later_ref, grad_ref, ddt_ref, score_ref, xe_scr, s_scr, g_scr, v_scr, y_scr, d_scr, cv_scr,
):
    chans = x_ref.shape[1]
    width = chans // heads
    per = LANES // width
    spread_steps = spread_matrix(0, chans, width)
    spread_entry = spread_matrix(heads, chans, width)
    spread_reach = spread_matrix(2 * heads, chans, width)
    spread_tail = spread_matrix(3 * heads, chans, width)
    gather = gather_matrix(chans, width)
    s_scr[0] = start_ref[...]
    g_scr[...] = later_ref[...]
    score_ref[...] = jnp.zeros_like(score_ref)
    cv_scr[...] = jnp.zeros_like(cv_scr)
    total = count * SPAN
    grad_ref[pl.ds(total, HALO), :] = jnp.zeros((HALO, chans), F32)

    def forward(k, carry):
        first = pl.multiple_of(k * SPAN, SPAN)
        tok = tok_ref[pl.ds(first, SPAN), :]
        pre = conv_of(x_ref, xe_scr, w_ref, tok, 5 * heads, first)
        v_scr[pl.ds(first, SPAN), :] = pre
        weighted = jax.nn.silu(pre) * mm_exact_right(tok, spread_tail)
        through = mm_exact_right(tok[SPAN - 8 :, :], spread_entry)[7:8, :]
        added = mm_exact_left(bt_ref[:, pl.ds(first, SPAN)], weighted)
        s_scr[k + 1] = through * s_scr[k] + added
        return carry

    lax.fori_loop(0, count, forward, 0)

    def backward(step, carry):
        k = count - 1 - step
        first = pl.multiple_of(k * SPAN, SPAN)
        here = pl.ds(first, SPAN)
        tok = tok_ref[here, :]
        pre = v_scr[here, :]
        sig = jax.nn.sigmoid(pre)
        values = pre * sig
        slope = sig * (1.0 + pre * (1.0 - sig))
        target = t_ref[here, :]
        b_rows = b_ref[here, :]
        c_rows = c_ref[here, :]
        bt = bt_ref[:, here]
        ct = ct_ref[:, here]
        steps = mm_exact_right(tok, spread_steps)
        entry = mm_exact_right(tok, spread_entry)
        reach = mm_exact_right(tok, spread_reach)
        y_scr[...] = entry * mm_exact_left(c_rows, s_scr[k])
        d_scr[...] = reach * mm_exact_left(b_rows, g_scr[...])
        u_high, u_low = split(steps * values)
        scores = mm(c_rows, bt)
        scores_t = mm(b_rows, ct)
        seen_col = tok[:, 5 * heads + 3 : 5 * heads + 4]
        seen_row = row_ref[5 * heads + 3 : 5 * heads + 4, here]
        order_row = lax.broadcasted_iota(jnp.int32, (SPAN, SPAN), 0)
        order_col = lax.broadcasted_iota(jnp.int32, (SPAN, SPAN), 1)
        same = seen_col == seen_row
        valid = same & (order_row >= order_col)
        valid_t = same & (order_row <= order_col)
        lane = lax.broadcasted_iota(jnp.int32, (SPAN, LANES), 1) // width
        for unit in range(heads // per):
            cols = slice(unit * LANES, (unit + 1) * LANES)
            t_unit = target[:, cols]
            both = jnp.concatenate([u_high[:, cols], u_low[:, cols]], axis=1)
            y_unit = jnp.zeros((SPAN, LANES), F32)
            d_unit = jnp.zeros((SPAN, LANES), F32)
            for part in range(per):
                h = 4 * heads + unit * per + part
                r_col = tok[:, h : h + 1]
                r_row = row_ref[h : h + 1, here]
                gap = r_col - r_row
                mix = jnp.exp(jnp.where(valid, gap, FAR)) * scores
                mix_t = jnp.exp(jnp.where(valid_t, -gap, FAR)) * scores_t
                m_high, m_low = split(mix)
                n_high, n_low = split(mix_t)
                wide = mm(m_high, both)
                y_part = wide[:, :LANES] + wide[:, LANES:] + mm(m_low, both[:, :LANES])
                d_part = mm(n_high, t_unit) + mm(n_low, t_unit)
                y_unit = jnp.where(lane == part, y_part, y_unit)
                d_unit = jnp.where(lane == part, d_part, d_unit)
            y_scr[:, cols] += y_unit
            d_scr[:, cols] += d_unit
        target_f = target.astype(F32)
        read = y_scr[...] * target_f
        score_ref[...] += jnp.sum(read.reshape(SPAN // 8, 8, chans), axis=0)
        du = d_scr[...]
        by_read = mm_exact_right(read, gather)
        by_step = mm_exact_right(values * du, gather)
        cross = jnp.sum((s_scr[k + 1] * g_scr[...]).reshape(DSTATE // 8, 8, chans), axis=0)
        crossed = jnp.sum(mm_exact_right(cross, gather), axis=0, keepdims=True)
        upper = jnp.where(order_row <= order_col, 1.0, 0.0).astype(BF16)
        d_log = mm_exact_left(upper, by_read - tok * by_step) + crossed
        ddt_ref[here, :] = by_step - rate_ref[...] * d_log
        d_pre = steps * du * slope
        cv_scr[0, pl.ds(HALO, SPAN), :] = w_ref[3:4, :] * d_pre
        for back in range(1, TAPS):
            scale = tok[:, 5 * heads + back - 1 : 5 * heads + back] * w_ref[3 - back : 4 - back, :]
            cv_scr[back, pl.ds(HALO, SPAN), :] = scale * d_pre
        top = cv_scr[0, pl.ds(0, SPAN), :]
        end = cv_scr[0, pl.ds(SPAN, HALO), :]
        for back in range(1, TAPS):
            top = top + cv_scr[back, pl.ds(back, SPAN), :]
            end = end + cv_scr[back, pl.ds(SPAN + back, HALO), :]
        grad_ref[here, :] = top
        tail = pl.ds(pl.multiple_of(first + SPAN, SPAN), HALO)
        grad_ref[tail, :] += end
        weighted = entry * target_f
        g_scr[...] = entry[SPAN - 1 : SPAN, :] * g_scr[...] + mm_exact_left(ct, weighted)
        return carry

    lax.fori_loop(0, count, backward, 0)


def per_pair(shape):
    return pl.BlockSpec((None,) + tuple(shape), lambda b: (b,) + (0,) * len(shape))


def whole(shape):
    return pl.BlockSpec(tuple(shape), lambda b: (0,) * len(shape))


def ends(x_ext, target, b_t, c_t, tok, taps, heads):
    pairs, rows, chans = target.shape
    out = jax.ShapeDtypeStruct((pairs, DSTATE, chans), F32)
    return pl.pallas_call(
        functools.partial(ends_kernel, heads, rows // SPAN),
        grid=(pairs,),
        out_shape=(out, out),
        in_specs=[per_pair(a.shape[1:]) for a in (x_ext, target, b_t, c_t, tok)] + [whole(taps.shape)],
        out_specs=(per_pair(out.shape[1:]),) * 2,
        scratch_shapes=[pltpu.VMEM((SPAN + HALO, chans), F32)],
        name="ends",
    )(x_ext, target, b_t, c_t, tok, taps)


def main(x_ext, target, b_rows, c_rows, b_t, c_t, tok, table, taps, rate, start, later, heads):
    pairs, rows, chans = target.shape
    count = rows // SPAN
    outs = (
        jax.ShapeDtypeStruct((pairs, rows + HALO, chans), F32),
        jax.ShapeDtypeStruct((pairs, rows, LANES), F32),
        jax.ShapeDtypeStruct((pairs, 8, chans), F32),
    )
    return pl.pallas_call(
        functools.partial(main_kernel, heads, count),
        grid=(pairs,),
        out_shape=outs,
        in_specs=[per_pair(a.shape[1:]) for a in (x_ext, target, b_rows, c_rows, b_t, c_t, tok, table)]
        + [whole(taps.shape), whole(rate.shape)]
        + [per_pair(start.shape[1:])] * 2,
        out_specs=tuple(per_pair(o.shape[1:]) for o in outs),
        scratch_shapes=[
            pltpu.VMEM((SPAN + HALO, chans), F32),
            pltpu.VMEM((count + 1, DSTATE, chans), F32),
            pltpu.VMEM((DSTATE, chans), F32),
            pltpu.VMEM((rows, chans), F32),
            pltpu.VMEM((SPAN, chans), F32),
            pltpu.VMEM((SPAN, chans), F32),
            pltpu.VMEM((TAPS, SPAN + 2 * HALO, chans), F32),
        ],
        name="main",
    )(x_ext, target, b_rows, c_rows, b_t, c_t, tok, table, taps, rate, start, later)


def send(source, goal, sent, got, where):
    return pltpu.make_async_remote_copy(
        src_ref=source,
        dst_ref=goal,
        send_sem=sent,
        recv_sem=got,
        device_id=where,
        device_id_type=pl.DeviceIdType.MESH,
    )


def greet(barrier, where):
    pl.semaphore_signal(barrier, inc=1, device_id=where, device_id_type=pl.DeviceIdType.MESH)


def chain_kernel(axis, through_ref, alone_ref, seed_ref, start_ref, later_ref, out_scr, in_scr, sent, got):
    count = lax.axis_size(axis)
    mine = lax.axis_index(axis)
    own_pieces, size, chans = alone_ref.shape
    has_less = mine > 0
    has_more = mine < count - 1
    less = lax.rem(mine + count - 1, count)
    more = lax.rem(mine + 1, count)
    barrier = pltpu.get_barrier_semaphore()

    @pl.when(has_less)
    def _():
        greet(barrier, {axis: less})

    @pl.when(has_more)
    def _():
        greet(barrier, {axis: more})

    pl.semaphore_wait(barrier, has_less.astype(jnp.int32) + has_more.astype(jnp.int32))
    ways = ((alone_ref, has_less, has_more, more), (seed_ref, has_more, has_less, less))
    for way, (_, arrives, _, _) in enumerate(ways):

        @pl.when(jnp.logical_not(arrives))
        def _():
            in_scr[way] = jnp.zeros((own_pieces, size, chans), F32)

    pieces = own_pieces

    def hop(time, carry):
        for way, (own, arrives, leaves, goal) in enumerate(ways):
            piece = time - (mine if way == 0 else count - 1 - mine)

            @pl.when((piece >= 0) & (piece < pieces))
            def _():
                copy = send(
                    out_scr.at[way, piece], in_scr.at[way, piece], sent.at[way, piece], got.at[way, piece], {axis: goal}
                )

                @pl.when(arrives)
                def _():
                    copy.wait_recv()

                @pl.when(leaves)
                def _():
                    through = through_ref[piece // CUTS]
                    out_scr[way, piece] = through * in_scr[way, piece] + own[piece]
                    copy.start()

        return carry

    lax.fori_loop(0, pieces + count - 1, hop, 0)
    start_ref[...] = in_scr[0]
    later_ref[...] = in_scr[1]

    def drain(piece, carry):
        for way, (_, _, leaves, goal) in enumerate(ways):

            @pl.when(leaves)
            def _():
                send(
                    out_scr.at[way, piece], in_scr.at[way, piece], sent.at[way, piece], got.at[way, piece], {axis: goal}
                ).wait_send()

        return carry

    lax.fori_loop(0, pieces, drain, 0)


def chain(through, alone, seed, axis):
    whole_shape = alone.shape
    pieces = whole_shape[0] * CUTS
    alone = alone.reshape(pieces, -1, whole_shape[2])
    seed = seed.reshape(alone.shape)
    shape = jax.ShapeDtypeStruct(alone.shape, F32)
    vmem = pl.BlockSpec(memory_space=pltpu.VMEM)
    start, later = pl.pallas_call(
        functools.partial(chain_kernel, axis),
        out_shape=(shape, shape),
        in_specs=[vmem] * 3,
        out_specs=(vmem, vmem),
        scratch_shapes=[
            pltpu.VMEM((2,) + alone.shape, F32),
            pltpu.VMEM((2,) + alone.shape, F32),
            pltpu.SemaphoreType.DMA((2, pieces)),
            pltpu.SemaphoreType.DMA((2, pieces)),
        ],
        compiler_params=pltpu.CompilerParams(collective_id=0, has_side_effects=True),
        name="chain",
    )(through, alone, seed)
    return start.reshape(whole_shape), later.reshape(whole_shape)


def finish_kernel(
    axes, size, grad_ref, score_ref, raw_ref, sign_ref, loss_ref, out_ref, slope_ref,
    part_scr, slot_scr, halo_scr, out_scr, raw_scr, psent, pgot, hsent, hgot, osent, ogot, rsent, rgot,
):
    outer, inner, _ = axes
    pairs, chans = grad_ref.shape[0], grad_ref.shape[2]
    heads = raw_ref.shape[1]
    rows = out_ref.shape[1]
    parts, planes = lax.axis_size(inner), lax.axis_size(outer)
    mine, plane = lax.axis_index(inner), lax.axis_index(outer)
    row = lax.broadcasted_iota(jnp.int32, (8, LANES), 0)
    own = [jnp.sum(jnp.sum(score_ref[b], axis=0, keepdims=True), axis=1, keepdims=True) for b in range(pairs)]
    part_scr[0] = jnp.where(row == 0, own[0], own[1])
    barrier = pltpu.get_barrier_semaphore()
    peers = 0
    for axis in axes:
        for away in range(1, lax.axis_size(axis)):
            greet(barrier, {axis: lax.rem(lax.axis_index(axis) + away, lax.axis_size(axis))})
            peers += 1
    pl.semaphore_wait(barrier, peers)
    has_less = plane > 0
    has_more = plane < planes - 1
    edge = send(
        grad_ref.at[:, pl.ds(0, HALO)], halo_scr, hsent, hgot, {outer: lax.rem(plane + planes - 1, planes)}
    )

    @pl.when(has_less)
    def _():
        edge.start()

    waits = []
    first = 0
    for turn, axis in enumerate(axes[::-1]):
        count = lax.axis_size(axis)
        me = lax.axis_index(axis)
        copies = []
        for away in range(1, count):
            goal = lax.rem(me + away, count)
            spot = first + away - 1
            copy = send(part_scr.at[turn], slot_scr.at[first + me], psent.at[spot], pgot.at[spot], {axis: goal})
            copy.start()
            copies.append(copy)
        slot_scr[first + me] = part_scr[turn]
        for copy in copies:
            copy.wait_recv()
        waits += copies
        subtotal = slot_scr[first]
        for i in range(1, count):
            subtotal = subtotal + slot_scr[first + i]
        part_scr[turn + 1] = subtotal
        first += count
    signed = subtotal * sign_ref[...] / math.sqrt(size)
    margin = signed[0:1, :] + signed[1:2, :]
    loss_ref[...] = jnp.broadcast_to(jax.nn.softplus(-margin), loss_ref.shape)
    factors = -jax.nn.sigmoid(-margin) * sign_ref[...]
    scale = [factors[b : b + 1, 0:1] for b in range(pairs)]

    @pl.when(has_more)
    def _():
        edge.wait_recv()

    @pl.when(jnp.logical_not(has_more))
    def _():
        halo_scr[...] = jnp.zeros_like(halo_scr)

    columns = pl.ds(pl.multiple_of(mine * chans, LANES), chans)
    lines = pl.ds(pl.multiple_of(mine * heads, 8), heads)
    for away in range(parts):
        goal = lax.rem(mine + away, parts) if parts > 1 else 0
        begin = pl.multiple_of(goal * rows, SPAN)
        last = jnp.where(goal == parts - 1, 1.0, 0.0).astype(F32)
        for b in range(pairs):
            body_rows = grad_ref[b, pl.ds(HALO + begin, rows - HALO), :]
            edge_rows = grad_ref[b, pl.ds(begin + rows, HALO), :] + last * halo_scr[b]
            above = (scale[b] * body_rows).astype(BF16)
            below = (scale[b] * edge_rows).astype(BF16)
            lean = scale[b] * raw_ref[b, :, pl.ds(begin, rows)]
            if away == 0:
                out_ref[b, pl.ds(0, rows - HALO), columns] = above
                out_ref[b, pl.ds(rows - HALO, HALO), columns] = below
                slope_ref[b, lines, :] = lean
                continue
            out_scr[away, b, pl.ds(0, rows - HALO), :] = above
            out_scr[away, b, pl.ds(rows - HALO, HALO), :] = below
            raw_scr[away, b] = lean
        if away > 0:
            wide = send(
                out_scr.at[away], out_ref.at[:, :, columns], osent.at[away], ogot.at[away], {inner: goal}
            )
            thin = send(raw_scr.at[away], slope_ref.at[:, lines], rsent.at[away], rgot.at[away], {inner: goal})
            thin.start()
            wide.start()
            waits += [thin, wide]
    for copy in waits[-2 * (parts - 1) :] if parts > 1 else []:
        copy.wait_recv()
    for copy in waits:
        copy.wait_send()

    @pl.when(has_less)
    def _():
        edge.wait_send()


def finish(grad, score, raw, sign, axes, size, rows):
    pairs, chans, heads = grad.shape[0], grad.shape[2], raw.shape[1]
    parts = lax.axis_size(axes[1])
    slots = sum(lax.axis_size(axis) for axis in axes)
    vmem = pl.BlockSpec(memory_space=pltpu.VMEM)
    dma = pltpu.SemaphoreType.DMA
    return pl.pallas_call(
        functools.partial(finish_kernel, axes, size),
        out_shape=(
            jax.ShapeDtypeStruct((8, LANES), F32),
            jax.ShapeDtypeStruct((pairs, rows, parts * chans), BF16),
            jax.ShapeDtypeStruct((pairs, parts * heads, rows), F32),
        ),
        in_specs=[vmem] * 4,
        out_specs=(vmem,) * 3,
        scratch_shapes=[
            pltpu.VMEM((len(axes) + 1, 8, LANES), F32),
            pltpu.VMEM((slots, 8, LANES), F32),
            pltpu.VMEM((pairs, HALO, chans), F32),
            pltpu.VMEM((parts, pairs, rows, chans), BF16),
            pltpu.VMEM((parts, pairs, heads, rows), F32),
            dma((slots,)),
            dma((slots,)),
            dma,
            dma,
            dma((parts,)),
            dma((parts,)),
            dma((parts,)),
            dma((parts,)),
        ],
        compiler_params=pltpu.CompilerParams(collective_id=1, has_side_effects=True),
        name="finish",
    )(grad, score, raw, sign)


def gather_kernel(axes, x_ref, t_ref, b_ref, c_ref, raw_ref, mark_ref, xo, to, bo, co, ro, mo, sent, got, kept, hsent, hgot):
    outer, inner = axes
    parts, planes = lax.axis_size(inner), lax.axis_size(outer)
    mine, plane = lax.axis_index(inner), lax.axis_index(outer)
    rows = x_ref.shape[1]
    chans, states, heads = xo.shape[2], bo.shape[2], ro.shape[1]
    has_less = plane > 0
    gives = (plane < planes - 1) & (mine == parts - 1)
    less, more = lax.rem(plane + planes - 1, planes), lax.rem(plane + 1, planes)
    barrier = pltpu.get_barrier_semaphore()
    for away in range(1, parts):
        greet(barrier, {inner: lax.rem(mine + away, parts)})

    @pl.when(has_less)
    def _():
        greet(barrier, {outer: less, inner: parts - 1})

    @pl.when(gives)
    def _():
        for j in range(parts):
            greet(barrier, {outer: more, inner: j})

    pl.semaphore_wait(barrier, parts - 1 + has_less.astype(jnp.int32) + parts * gives.astype(jnp.int32))

    def views(source, goal):
        wide = pl.ds(pl.multiple_of(goal * chans, LANES), chans)
        group = pl.ds(pl.multiple_of(goal * states, LANES), states)
        lines = pl.ds(pl.multiple_of(goal * heads, 8), heads)
        here = pl.ds(pl.multiple_of(source * rows, LANES), rows)
        below = pl.ds(pl.multiple_of(HALO + source * rows, HALO), rows)
        later = pl.ds(pl.multiple_of(rows + source * rows, LANES), rows)
        for b in range(2):
            yield x_ref.at[b, :, wide], xo.at[b, below]
            yield t_ref.at[b, :, wide], to.at[b, here]
            yield b_ref.at[b, :, group], bo.at[b, here]
            yield c_ref.at[b, :, group], co.at[b, here]
            yield raw_ref.at[b, lines], ro.at[b, :, here]
            yield mark_ref.at[b], mo.at[b, :, later]

    copies = []
    for away in range(1, parts):
        goal = lax.rem(mine + away, parts)
        for i, (source, target) in enumerate(views(mine, goal)):
            copy = send(source, target, sent.at[away, i], got.at[away, i], {inner: goal})
            copy.start()
            copies.append(copy)
    own = []
    for i, (source, target) in enumerate(views(mine, mine)):
        copy = pltpu.make_async_copy(source, target, kept.at[i])
        copy.start()
        own.append(copy)

    def edges(j):
        wide = pl.ds(j * chans, chans)
        end = pl.ds(rows - HALO, HALO)
        pairs = [(x_ref.at[:, end, wide], xo.at[:, pl.ds(0, HALO)]), (mark_ref, mo.at[:, :, pl.ds(0, rows)])]
        return [send(s, d, hsent.at[j, i], hgot.at[i], {outer: more, inner: j}) for i, (s, d) in enumerate(pairs)]

    @pl.when(gives)
    def _():
        for j in range(parts):
            for copy in edges(j):
                copy.start()

    @pl.when(has_less)
    def _():
        for copy in edges(0):
            copy.wait_recv()

    @pl.when(jnp.logical_not(has_less))
    def _():
        xo[:, pl.ds(0, HALO), :] = jnp.zeros((2, HALO, chans), BF16)
        mo[:, :, pl.ds(0, rows)] = jnp.zeros((2, 8, rows), F32)

    for copy in own:
        copy.wait()
    for copy in copies:
        copy.wait()

    @pl.when(gives)
    def _():
        for j in range(parts):
            for copy in edges(j):
                copy.wait_send()


def gather_all(x_in, target, b_in, c_in, dt_raw, marks, axes):
    parts = lax.axis_size(axes[1])
    rows = x_in.shape[1]
    tokens = parts * rows
    chans, states, heads = x_in.shape[2] // parts, b_in.shape[2] // parts, dt_raw.shape[1] // parts
    vmem = pl.BlockSpec(memory_space=pltpu.VMEM)
    dma = pltpu.SemaphoreType.DMA
    return pl.pallas_call(
        functools.partial(gather_kernel, axes),
        out_shape=(
            jax.ShapeDtypeStruct((2, tokens + HALO, chans), BF16),
            jax.ShapeDtypeStruct((2, tokens, chans), BF16),
            jax.ShapeDtypeStruct((2, tokens, states), BF16),
            jax.ShapeDtypeStruct((2, tokens, states), BF16),
            jax.ShapeDtypeStruct((2, heads, tokens), F32),
            jax.ShapeDtypeStruct((2, 8, rows + tokens), F32),
        ),
        in_specs=[pl.BlockSpec(memory_space=pl.ANY)] * 5 + [vmem],
        out_specs=(vmem,) * 6,
        scratch_shapes=[dma((parts, 12)), dma((parts, 12)), dma((12,)), dma((parts, 2)), dma((2,))],
        compiler_params=pltpu.CompilerParams(collective_id=2, has_side_effects=True),
        name="gather",
    )(x_in, target, b_in, c_in, dt_raw, marks)


def body(outer, inner, x_in, target, b_in, c_in, dt_raw, resets, decay_rate, conv_w, label):
    rows = x_in.shape[1]
    all_heads = dt_raw.shape[1]
    width = x_in.shape[2] // all_heads
    parts = lax.axis_size(inner)
    heads = all_heads // parts
    chans = heads * width
    tokens = rows * parts
    count = tokens // SPAN
    mine = lax.axis_index(inner)
    planes = lax.axis_size(outer)
    marks = jnp.broadcast_to(resets.astype(F32)[:, None], (2, 8, rows))
    x_ext, t_all, b_all, c_all, raw, marks = gather_all(x_in, target, b_in, c_in, dt_raw, marks, (outer, inner))
    keep = 1.0 - marks[:, 0, rows - 2 :]
    marks = marks[:, 0, rows:]
    keep_one = keep[:, 2:]
    keep_two = keep_one * keep[:, 1:-1]
    keep_three = keep_two * keep[:, :-2]
    rate = lax.dynamic_slice(decay_rate, (mine * heads,), (heads,))
    taps = lax.dynamic_slice(conv_w, (0, mine * chans), (TAPS, chans))
    steps = jax.nn.softplus(raw)
    logs = -steps * rate[None, :, None]
    upto = jnp.tril(jnp.ones((SPAN, SPAN), F32))
    both = jnp.concatenate([logs, marks[:, None]], axis=1).reshape(2, heads + 1, count, SPAN)
    sums = jnp.einsum("bhkj,ij->bhki", both, upto, precision=HIGH)
    running = sums[:, :heads]
    seen = jnp.round(sums[:, heads:])
    entry = jnp.exp(running) * (seen == 0.0).astype(F32)
    reach = jnp.exp(running[..., -1:] - running) * (seen[..., -1:] == seen).astype(F32)
    through = jnp.prod(entry[..., -1], axis=2)

    def flat(array):
        return array.reshape(2, -1, tokens)

    used = 5 * heads + 4
    table = jnp.concatenate(
        [
            steps,
            flat(entry),
            flat(reach),
            flat(reach) * steps,
            flat(running),
            keep_one[:, None],
            keep_two[:, None],
            keep_three[:, None],
            flat(seen),
            jnp.zeros((2, LANES - used, tokens), F32),
        ],
        axis=1,
    )
    tok = table.transpose(0, 2, 1)
    b_t = b_all.transpose(0, 2, 1)
    c_t = c_all.transpose(0, 2, 1)
    alone, seed = ends(x_ext, t_all, b_t, c_t, tok, taps, heads)
    wide = jnp.repeat(through, width, axis=1)[:, None, :]
    start, later = chain(wide, alone, seed, outer)
    rate_row = jnp.pad(rate, (0, LANES - heads))[None]
    grad, ddt, score = main(x_ext, t_all, b_all, c_all, b_t, c_t, tok, table, taps, rate_row, start, later, heads)
    sign = jnp.where(jnp.arange(2) == label[0], 1.0, -1.0).astype(F32)
    sign = jnp.broadcast_to(jnp.pad(sign, (0, 6))[:, None], (8, LANES))
    size = tokens * planes * x_in.shape[2] * lax.axis_size("head")
    lean = jax.nn.sigmoid(raw) * ddt[:, :, :heads].transpose(0, 2, 1)
    loss, grad, grad_raw = finish(grad, score, lean, sign, (outer, inner, "head"), size, rows)
    return (loss[0, 0], grad, grad_raw)


def solution(mesh):
    def program(*arrays):
        ways, across = mesh.shape["seq"], mesh.shape["head"]
        groups = arrays[2].shape[2] // DSTATE // across
        parts = math.gcd(groups, ways)
        devices = mesh.devices.reshape(ways // parts, parts, across)
        finer = Mesh(devices, ("outer", "inner", "head"))
        seq = ("outer", "inner")
        in_specs = (
            P(None, seq, "head"),
            P(None, seq, "head"),
            P(None, seq, "head"),
            P(None, seq, "head"),
            P(None, "head", seq),
            P(None, seq),
            P("head"),
            P(None, "head"),
            P(),
        )
        out_specs = (P(), P(None, seq, "head"), P(None, "head", seq))
        inner = functools.partial(body, "outer", "inner")
        mapped = jax.shard_map(inner, mesh=finer, in_specs=in_specs, out_specs=out_specs, check_vma=False)
        return mapped(*arrays)

    return program
```

```python
import functools
import math

import jax
import jax.numpy as jnp
from jax import lax
from jax.experimental import pallas as pl
from jax.experimental.pallas import tpu as pltpu
from jax.sharding import Mesh
from jax.sharding import PartitionSpec as P

DSTATE = 128
BLOCK = 128
CHUNK = 64
LANES = 128
TAPS = 4
HALO = 16
UNIT = 256
AHEAD = 2
F32 = jnp.float32
BF16 = jnp.bfloat16


def split(value):
    high = value.astype(BF16)
    low = (value - high.astype(F32)).astype(BF16)
    return high, low


def mm(left, right):
    return lax.dot_general(left, right, (((1,), (0,)), ((), ())), preferred_element_type=F32)


def mm_across(left, right):
    return lax.dot_general(left, right, (((1,), (1,)), ((), ())), preferred_element_type=F32)


def mm_three(left, right):
    high = left.astype(BF16)
    rest = left - high.astype(F32)
    low, least = split(rest)
    return mm(high, right) + mm(low, right) + mm(least, right)


def iota(shape, dim):
    return lax.broadcasted_iota(jnp.int32, shape, dim)


def side(*parts):
    return jnp.concatenate(parts, axis=1)


def stack(*parts):
    return jnp.concatenate(parts, axis=0)


def send(source, goal, sent, got, where):
    return pltpu.make_async_remote_copy(
        src_ref=source,
        dst_ref=goal,
        send_sem=sent,
        recv_sem=got,
        device_id=where,
        device_id_type=pl.DeviceIdType.MESH,
    )


def greet(barrier, where):
    pl.semaphore_signal(barrier, inc=1, device_id=where, device_id_type=pl.DeviceIdType.MESH)


def prepare(b, blk, heads, rows, raw_scr, mark_scr, rate, b_scr, c_scr, tok_scr, lm, rm, zc2, qb2, bt2, ct2):
    here = pl.ds(pl.multiple_of(blk * BLOCK, BLOCK), BLOCK)
    later = pl.ds(pl.multiple_of(rows + blk * BLOCK, BLOCK), BLOCK)
    before = pl.ds(pl.multiple_of(rows - BLOCK + blk * BLOCK, BLOCK), BLOCK)
    steps = jax.nn.softplus(raw_scr[b, :, here])
    logs = -steps * rate
    marks = mark_scr[b, :, later]
    keep = 1.0 - side(mark_scr[b, :, before], marks)
    keep_one = keep[:, BLOCK:]
    keep_two = keep_one * pltpu.roll(keep, 1, 1)[:, BLOCK:]
    keep_three = keep_two * pltpu.roll(keep, 2, 1)[:, BLOCK:]
    row = iota((BLOCK, BLOCK), 0)
    col = iota((BLOCK, BLOCK), 1)
    near = (row // CHUNK) == (col // CHUNK)
    upto = jnp.where(near & (row <= col), 1.0, 0.0).astype(BF16)
    full = jnp.where(near, 1.0, 0.0).astype(BF16)
    running = mm_three(logs, upto)
    total = mm_three(logs, full)
    seen = mm(marks.astype(BF16), upto)
    seen_all = mm(marks.astype(BF16), full)
    half = 0.5 * total
    grow = steps * jnp.exp(half - running)
    fall = jnp.exp(running - half)
    center = jnp.exp(half)
    open_all = jnp.where(seen_all == 0.0, 1.0, 0.0).astype(F32)
    through = jnp.exp(total) * open_all[0:1]
    opened = jnp.where(seen == 0.0, 1.0, 0.0).astype(F32)
    closing = jnp.where(seen == seen_all, 1.0, 0.0).astype(F32)
    line = iota((8, BLOCK), 0)
    extra = jnp.zeros((8, BLOCK), F32)
    for i, value in enumerate((keep_one, keep_two, keep_three, seen, opened, closing)):
        extra = jnp.where(line == i, value, extra)
    table = stack(grow, fall, center, through, extra, jnp.zeros((LANES - 4 * heads - 8, BLOCK), F32))
    tok = table.T
    tok_scr[b, here, :] = tok
    base = 4 * heads
    b_rows = b_scr[b, here, :]
    c_rows = c_scr[b, here, :]
    scores = mm_across(c_rows, b_rows)
    scores_t = mm_across(b_rows, c_rows)
    same = near & (tok[:, base + 3 : base + 4] == seen[0:1, :])
    m_high, m_low = split(jnp.where(same & (row >= col), scores, 0.0))
    n_high, n_low = split(jnp.where(same & (row <= col), scores_t, 0.0))
    lm[b, blk] = side(m_high, m_low, m_high)
    rm[b, blk] = side(n_high, n_low, n_high)
    for value, mask, twice, turned in ((c_rows, base + 4, zc2, ct2), (b_rows, base + 5, qb2, bt2)):
        masked = value.astype(F32) * tok[:, mask : mask + 1]
        short = masked.astype(BF16)
        twice[b, blk] = side(short, short)
        flipped = masked.T
        lane = iota((DSTATE, BLOCK), 1)
        one = jnp.where(lane < CHUNK, flipped, 0.0).astype(BF16)
        two = jnp.where(lane >= CHUNK, flipped, 0.0).astype(BF16)
        turned[b, blk] = stack(side(one, one), side(two, two))


def before_chain(
    u, b, q, heads, width, count, taps, x_scr, t_scr, tok_scr, bt2, ct2, xe_scr,
    wh, wl, vh, vl, pk, s_loc, g_loc, p_row, r_row, d_row, th_row,
):
    chans = UNIT
    per = chans // width
    row = iota((LANES, chans), 0)
    head = iota((LANES, chans), 1) // width + q * per

    def spread(offset):
        one = jnp.where(row == head + offset, 1.0, 0.0).astype(BF16)
        return stack(one, one)

    spread_grow, spread_fall = spread(0), spread(heads)
    spread_center, spread_through = spread(2 * heads), spread(3 * heads)
    base = 4 * heads
    s_loc[u, 0] = jnp.zeros((DSTATE, chans), F32)
    g_loc[u, 2 * count] = jnp.zeros((DSTATE, chans), F32)

    def forward(blk, through):
        first = pl.multiple_of(blk * BLOCK, BLOCK)
        here = pl.ds(first, BLOCK)
        tok = tok_scr[b, here, :]
        both = side(*split(tok))
        ends = stack(both[0:16], both[CHUNK : CHUNK + 16])
        grow = mm(both, spread_grow)
        fall = mm(both, spread_fall)
        center = mm(ends, spread_center)
        pass_by = mm(ends, spread_through)
        xe_scr[...] = x_scr[u, pl.ds(first, BLOCK + HALO), :].astype(F32)
        pre = taps[3:4, :] * xe_scr[pl.ds(HALO, BLOCK), :]
        for back in range(1, TAPS):
            scale = tok[:, base + back - 1 : base + back] * taps[3 - back : 4 - back, :]
            pre = pre + scale * xe_scr[pl.ds(HALO - back, BLOCK), :]
        sig = jax.nn.sigmoid(pre)
        values = pre * sig
        slope = sig + values * (1.0 - sig)
        w_high, w_low = split(grow * values)
        v_high, v_low = split(fall * t_scr[u, here, :].astype(F32))
        wh[u, here, :] = w_high
        wl[u, here, :] = w_low
        vh[u, here, :] = v_high
        vl[u, here, :] = v_low
        pk[u, here, :] = grow * slope
        added = mm(bt2[b, blk], stack(w_high, w_low))
        state = s_loc[u, 2 * blk]
        for sub in range(2):
            k = 2 * blk + sub
            c_one = center[16 * sub : 16 * sub + 1, :]
            t_one = pass_by[16 * sub : 16 * sub + 1, :]
            p_row[u, pl.ds(k, 1), :] = through
            d_row[u, pl.ds(k, 1), :] = c_one
            th_row[u, pl.ds(k, 1), :] = t_one
            through = through * t_one
            state = t_one * state + c_one * added[DSTATE * sub : DSTATE * (sub + 1), :]
            s_loc[u, k + 1] = state
        return through

    through = lax.fori_loop(0, count, forward, jnp.ones((1, chans), F32))
    p_row[u, 2 * count : 2 * count + 1, :] = through

    def backward(step, through):
        blk = count - 1 - step
        here = pl.ds(pl.multiple_of(blk * BLOCK, BLOCK), BLOCK)
        added = mm(ct2[b, blk], stack(vh[u, here, :], vl[u, here, :]))
        state = g_loc[u, 2 * blk + 2]
        for sub in (1, 0):
            k = 2 * blk + sub
            t_one = th_row[u, pl.ds(k, 1), :]
            r_row[u, pl.ds(k + 1, 1), :] = through
            through = through * t_one
            state = t_one * state + d_row[u, pl.ds(k, 1), :] * added[DSTATE * sub : DSTATE * (sub + 1), :]
            g_loc[u, k] = state
        return through

    lax.fori_loop(0, count, backward, jnp.ones((1, chans), F32))


def after_chain(
    u, b, q, heads, width, count, taps, tok_scr, lm, rm, zc2, qb2,
    wh, wl, vh, vl, pk, s_loc, g_loc, p_row, r_row, d_row, start_scr, later_scr, cv_scr, grad_scr, hd_scr, score_scr,
):
    chans = UNIT
    per = chans // width
    base = 4 * heads
    lane_head = iota((chans, LANES), 0) // width + q * per
    col = iota((chans, LANES), 1)
    pick_diff = jnp.where(col == lane_head, 1.0, 0.0).astype(BF16)
    pick_step = jnp.where(col == lane_head + heads, 1.0, 0.0).astype(BF16)
    pick = stack(pick_diff, pick_diff, pick_step, pick_step)
    tokens = count * BLOCK
    for back in range(TAPS):
        cv_scr[back, pl.ds(0, HALO), :] = jnp.zeros((HALO, chans), F32)
        cv_scr[back, pl.ds(HALO + tokens, HALO), :] = jnp.zeros((HALO, chans), F32)
    line = iota((BLOCK, chans), 0)

    def block(blk, carry):
        first = pl.multiple_of(blk * BLOCK, BLOCK)
        here = pl.ds(first, BLOCK)
        start = start_scr[u]
        later = later_scr[u]
        w_high, w_low = wh[u, here, :], wl[u, here, :]
        v_high, v_low = vh[u, here, :], vl[u, here, :]
        y_all, d_all, crossed = [], [], []
        state = s_loc[u, 2 * blk] + p_row[u, pl.ds(2 * blk, 1), :] * start
        for sub in range(2):
            k = 2 * blk + sub
            center = d_row[u, pl.ds(k, 1), :]
            rows = pl.ds(sub * CHUNK, CHUNK)
            slope = g_loc[u, k + 1] + r_row[u, pl.ds(k + 1, 1), :] * later
            after = s_loc[u, k + 1] + p_row[u, pl.ds(k + 1, 1), :] * start
            y_all.append(mm(zc2[b, blk, rows, :], stack(*split(center * state))))
            d_all.append(mm(qb2[b, blk, rows, :], stack(*split(center * slope))))
            crossed.append(jnp.sum(after * slope, axis=0, keepdims=True))
            state = after
        y_in = mm(lm[b, blk], stack(w_high, w_high, w_low)) + stack(*y_all)
        d_in = mm(rm[b, blk], stack(v_high, v_high, v_low)) + stack(*d_all)
        read = (v_high.astype(F32) + v_low.astype(F32)) * y_in
        stepped = (w_high.astype(F32) + w_low.astype(F32)) * d_in
        score_scr[b] += jnp.sum(read.reshape(BLOCK // 8, 8, chans), axis=0)
        diff = read - stepped
        diff = jnp.where(line == CHUNK - 1, diff + crossed[0], diff)
        diff = jnp.where(line == BLOCK - 1, diff + crossed[1], diff)
        hd_scr[b, here, :] += mm(side(*split(diff), *split(stepped)), pick)
        d_pre = pk[u, here, :] * d_in
        tok = tok_scr[b, here, :]
        below = pl.ds(pl.multiple_of(HALO + blk * BLOCK, HALO), BLOCK)
        cv_scr[0, below, :] = taps[3:4, :] * d_pre
        for back in range(1, TAPS):
            scale = tok[:, base + back - 1 : base + back] * taps[3 - back : 4 - back, :]
            cv_scr[back, below, :] = scale * d_pre
        return carry

    lax.fori_loop(0, count, block, 0)
    for begin, size in [(0, HALO)] + [(HALO + i * BLOCK, BLOCK) for i in range(count)]:
        total = cv_scr[0, pl.ds(begin, size), :]
        for back in range(1, TAPS):
            total = total + cv_scr[back, pl.ds(begin + back, size), :]
        grad_scr[u, pl.ds(begin, size), :] = total


def kernel(
    axes, size, width,
    x_ref, t_ref, b_ref, c_ref, raw_ref, mark_ref, rate_ref, w_ref, sign_ref,
    loss_ref, out_ref, slope_ref,
    x_scr, t_scr, b_scr, c_scr, raw_scr, mark_scr, tok_scr, lm, rm, zc2, qb2, bt2, ct2, xe_scr,
    wh, wl, vh, vl, pk, s_loc, g_loc, p_row, r_row, d_row, th_row, chain_out, start_scr, later_scr,
    cv_scr, grad_scr, hd_scr, score_scr, halo_scr, part_scr, slot_scr, out_scr, lean_scr,
    wsent, wgot, wkept, nsent, ngot, nkept, hsent, hgot, msent, mgot, csent, cgot,
    esent, egot, psent, pgot, osent, ogot, rsent, rgot,
):
    outer, inner, _ = axes
    units, tokens = t_scr.shape[0], t_scr.shape[1]
    rows = x_ref.shape[1]
    states, heads = b_scr.shape[2], raw_scr.shape[1]
    per_pair = units // 2
    chans = per_pair * UNIT
    count = tokens // BLOCK
    parts, planes = lax.axis_size(inner), lax.axis_size(outer)
    mine, plane = lax.axis_index(inner), lax.axis_index(outer)
    has_less = plane > 0
    has_more = plane < planes - 1
    gives = has_more & (mine == parts - 1)
    less, more = lax.rem(plane + planes - 1, planes), lax.rem(plane + 1, planes)
    barrier = pltpu.get_barrier_semaphore()
    peers = 0
    for axis in axes:
        for away in range(1, lax.axis_size(axis)):
            greet(barrier, {axis: lax.rem(lax.axis_index(axis) + away, lax.axis_size(axis))})
            peers += 1

    @pl.when(has_less)
    def _():
        greet(barrier, {outer: less, inner: parts - 1})

    @pl.when(gives)
    def _():
        for j in range(parts):
            greet(barrier, {outer: more, inner: j})

    pl.semaphore_wait(barrier, peers + has_less.astype(jnp.int32) + parts * gives.astype(jnp.int32))

    def wide_views(u, source, goal):
        b, q = u // per_pair, lax.rem(u, per_pair)
        wide = pl.ds(pl.multiple_of(goal * chans + q * UNIT, UNIT), UNIT)
        yield x_ref.at[b, :, wide], x_scr.at[u, pl.ds(pl.multiple_of(HALO + source * rows, HALO), rows)]
        yield t_ref.at[b, :, wide], t_scr.at[u, pl.ds(pl.multiple_of(source * rows, HALO), rows)]

    def thin_views(b, source, goal):
        group = pl.ds(pl.multiple_of(goal * states, LANES), states)
        lines = pl.ds(pl.multiple_of(goal * heads, 8), heads)
        here = pl.ds(pl.multiple_of(source * rows, LANES), rows)
        later = pl.ds(pl.multiple_of(rows + source * rows, LANES), rows)
        yield b_ref.at[b, :, group], b_scr.at[b, here]
        yield c_ref.at[b, :, group], c_scr.at[b, here]
        yield raw_ref.at[b, lines], raw_scr.at[b, :, here]
        yield mark_ref.at[b], mark_scr.at[b, :, later]

    def remote(views, index, sent, got):
        for away in range(1, parts):
            goal = lax.rem(mine + away, parts)
            for i, (source, target) in enumerate(views(index, mine, goal)):
                yield send(source, target, sent.at[away, index, i], got.at[away, index, i], {inner: goal})

    def local(views, index, kept):
        for i, (source, target) in enumerate(views(index, mine, mine)):
            yield pltpu.make_async_copy(source, target, kept.at[index, i])

    wides = functools.partial(remote, wide_views, sent=wsent, got=wgot)
    thins = functools.partial(remote, thin_views, sent=nsent, got=ngot)

    def edges(u, j):
        b, q = u // per_pair, lax.rem(u, per_pair)
        wide = pl.ds(pl.multiple_of(j * chans + q * UNIT, UNIT), UNIT)
        return send(
            x_ref.at[b, pl.ds(rows - HALO, HALO), wide], x_scr.at[u, pl.ds(0, HALO)],
            hsent.at[j, u], hgot.at[u], {outer: more, inner: j},
        )

    def edge_marks(j):
        return send(mark_ref, mark_scr.at[:, :, pl.ds(0, rows)], msent.at[j], mgot, {outer: more, inner: j})

    def issue(u):
        for copy in wides(u):
            copy.start()
        for copy in local(wide_views, u, wkept):
            copy.start()

    @pl.when(gives)
    def _():
        for j in range(parts):
            edge_marks(j).start()

    for b in range(2):
        for copy in thins(b):
            copy.start()
        for copy in local(thin_views, b, nkept):
            copy.start()
        if b == 0:
            for u in range(min(AHEAD, units)):
                issue(u)

    @pl.when(gives)
    def _():
        def one(u, carry):
            for j in range(parts):
                edges(u, j).start()
            return carry

        lax.fori_loop(0, units, one, 0)

    @pl.when(has_less)
    def _():
        edge_marks(0).wait_recv()

    @pl.when(jnp.logical_not(has_less))
    def _():
        x_scr[:, pl.ds(0, HALO), :] = jnp.zeros((units, HALO, UNIT), BF16)
        mark_scr[:, :, pl.ds(0, rows)] = jnp.zeros((2, 8, rows), F32)

    score_scr[...] = jnp.zeros_like(score_scr)
    hd_scr[...] = jnp.zeros_like(hd_scr)
    rate = rate_ref[pl.ds(pl.multiple_of(mine * heads, 8), heads), :]
    through_row = pl.ds(2 * count, 1)
    ways = ((s_loc, 2 * count, start_scr, has_less, has_more, more), (g_loc, 0, later_scr, has_more, has_less, less))
    for _, _, arrived, arrives, _, _ in ways:

        @pl.when(jnp.logical_not(arrives))
        def _():
            arrived[...] = jnp.zeros(arrived.shape, F32)

    def chain_copy(way, u, arrived, goal):
        return send(chain_out.at[way, u], arrived.at[u], csent.at[way, u], cgot.at[way, u], {outer: goal})

    def edge(u):
        return send(grad_scr.at[u, pl.ds(0, HALO)], halo_scr.at[u], esent.at[u], egot.at[u], {outer: less})

    def taps_of(q):
        return w_ref[:, pl.ds(pl.multiple_of(mine * chans + q * UNIT, UNIT), UNIT)]

    def turn(time, carry):
        @pl.when(time + AHEAD < units)
        def _():
            issue(time + AHEAD)

        @pl.when(time < units)
        def _():
            u = time
            b, q = u // per_pair, lax.rem(u, per_pair)

            @pl.when(q == 0)
            def _():
                for copy in thins(b):
                    copy.wait_recv()
                for copy in local(thin_views, b, nkept):
                    copy.wait()

                def one(blk, carry):
                    prepare(
                        b, blk, heads, rows, raw_scr, mark_scr, rate, b_scr, c_scr, tok_scr, lm, rm, zc2, qb2, bt2, ct2
                    )
                    return carry

                lax.fori_loop(0, count, one, 0)

            for copy in wides(u):
                copy.wait_recv()
            for copy in local(wide_views, u, wkept):
                copy.wait()

            @pl.when(has_less)
            def _():
                edges(u, 0).wait_recv()

            before_chain(
                u, b, q, heads, width, count, taps_of(q), x_scr, t_scr, tok_scr, bt2, ct2, xe_scr,
                wh, wl, vh, vl, pk, s_loc, g_loc, p_row, r_row, d_row, th_row,
            )

        for way, (own, end, arrived, arrives, leaves, goal) in enumerate(ways):
            u = time - (plane if way == 0 else planes - 1 - plane)

            @pl.when((u >= 0) & (u < units))
            def _():
                copy = chain_copy(way, u, arrived, goal)

                @pl.when(arrives)
                def _():
                    copy.wait_recv()

                @pl.when(leaves)
                def _():
                    chain_out[way, u] = p_row[u, through_row, :] * arrived[u] + own[u, end]
                    copy.start()

        u = time - (planes - 1)

        @pl.when(u >= 0)
        def _():
            b, q = u // per_pair, lax.rem(u, per_pair)
            after_chain(
                u, b, q, heads, width, count, taps_of(q), tok_scr, lm, rm, zc2, qb2,
                wh, wl, vh, vl, pk, s_loc, g_loc, p_row, r_row, d_row, start_scr, later_scr, cv_scr, grad_scr, hd_scr,
                score_scr,
            )

            @pl.when(has_less)
            def _():
                edge(u).start()

        return carry

    lax.fori_loop(0, units + planes - 1, turn, 0)

    row = iota((8, LANES), 0)
    own = [jnp.sum(jnp.sum(score_scr[b], axis=0, keepdims=True), axis=1, keepdims=True) for b in range(2)]
    part_scr[0] = jnp.where(row == 0, own[0], own[1])
    waits = []
    first = 0
    for level, axis in enumerate(axes[::-1]):
        span = lax.axis_size(axis)
        me = lax.axis_index(axis)
        copies = []
        for away in range(1, span):
            goal = lax.rem(me + away, span)
            spot = first + away - 1
            copy = send(part_scr.at[level], slot_scr.at[first + me], psent.at[spot], pgot.at[spot], {axis: goal})
            copy.start()
            copies.append(copy)
        if level == 0:
            back_row = iota((BLOCK, BLOCK), 0)
            back_col = iota((BLOCK, BLOCK), 1)
            near = (back_row // CHUNK) == (back_col // CHUNK)
            onward = jnp.where(near & (back_row >= back_col), 1.0, 0.0).astype(BF16)
            for b in range(2):
                for blk in range(count):
                    here = pl.ds(blk * BLOCK, BLOCK)
                    sums = hd_scr[b, here, :].T
                    raw = raw_scr[b, :, here]
                    d_log = mm_three(sums[0:heads], onward)
                    by_step = sums[heads : 2 * heads] / jax.nn.softplus(raw)
                    lean_scr[b, :, here] = jax.nn.sigmoid(raw) * (by_step - rate * d_log)
        slot_scr[first + me] = part_scr[level]
        for copy in copies:
            copy.wait_recv()
        waits += copies
        subtotal = slot_scr[first]
        for i in range(1, span):
            subtotal = subtotal + slot_scr[first + i]
        part_scr[level + 1] = subtotal
        first += span
    signed = subtotal * sign_ref[...] / math.sqrt(size)
    margin = signed[0:1, :] + signed[1:2, :]
    loss_ref[...] = jnp.broadcast_to(jax.nn.softplus(-margin), loss_ref.shape)
    factors = -jax.nn.sigmoid(-margin) * sign_ref[...]
    scale = [factors[b : b + 1, 0:1] for b in range(2)]

    @pl.when(jnp.logical_not(has_more))
    def _():
        halo_scr[...] = jnp.zeros_like(halo_scr)

    def out_view(u):
        b, q = u // per_pair, lax.rem(u, per_pair)
        return out_ref.at[b, :, pl.ds(pl.multiple_of(mine * chans + q * UNIT, UNIT), UNIT)]

    def wide_out(u, away):
        goal = lax.rem(mine + away, parts)
        return send(out_scr.at[away, u], out_view(u), osent.at[away, u], ogot.at[away, u], {inner: goal})

    lines = pl.ds(pl.multiple_of(mine * heads, 8), heads)

    def thin_out(away):
        goal = lax.rem(mine + away, parts)
        return send(out_lean(away), slope_ref.at[:, lines], rsent.at[away], rgot.at[away], {inner: goal})

    def out_lean(away):
        goal = lax.rem(mine + away, parts)
        return lean_scr.at[:, :, pl.ds(pl.multiple_of(goal * rows, LANES), rows)]

    for b in range(2):
        lean_scr[b] = scale[b] * lean_scr[b]
    for away in range(1, parts):
        thin_out(away).start()
    slope_ref[:, lines, :] = lean_scr[:, :, pl.ds(pl.multiple_of(mine * rows, LANES), rows)]

    def give(u, carry):
        b, q = u // per_pair, lax.rem(u, per_pair)
        factor = jnp.where(b == 0, scale[0], scale[1])

        @pl.when(has_more)
        def _():
            edge(u).wait_recv()

        for away in list(range(1, parts)) + [0]:
            goal = lax.rem(mine + away, parts)
            begin = pl.multiple_of(HALO + goal * rows, HALO)
            last = jnp.where(goal == parts - 1, 1.0, 0.0).astype(F32)
            body_rows = grad_scr[u, pl.ds(begin, rows - HALO), :]
            edge_rows = grad_scr[u, pl.ds(pl.multiple_of(begin + rows - HALO, HALO), HALO), :] + last * halo_scr[u]
            target = out_view(u) if away == 0 else out_scr.at[away, u]
            target[pl.ds(0, rows - HALO), :] = (factor * body_rows).astype(BF16)
            target[pl.ds(rows - HALO, HALO), :] = (factor * edge_rows).astype(BF16)
            if away > 0:
                wide_out(u, away).start()
        return carry

    lax.fori_loop(0, units, give, 0)

    def drain(u, carry):
        for away in range(1, parts):
            wide_out(u, away).wait()
        for copy in wides(u):
            copy.wait_send()
        for way, (_, _, arrived, _, leaves, goal) in enumerate(ways):

            @pl.when(leaves)
            def _():
                chain_copy(way, u, arrived, goal).wait_send()

        @pl.when(has_less)
        def _():
            edge(u).wait_send()

        @pl.when(gives)
        def _():
            for j in range(parts):
                edges(u, j).wait_send()

        return carry

    lax.fori_loop(0, units, drain, 0)
    for away in range(1, parts):
        thin_out(away).wait()
    for b in range(2):
        for copy in thins(b):
            copy.wait_send()
    for copy in waits:
        copy.wait_send()

    @pl.when(gives)
    def _():
        for j in range(parts):
            edge_marks(j).wait_send()


def everything(x_in, target, b_in, c_in, dt_raw, marks, rate, conv_w, sign, axes, size, width):
    parts = lax.axis_size(axes[1])
    rows = x_in.shape[1]
    tokens = parts * rows
    chans, states, heads = x_in.shape[2] // parts, b_in.shape[2] // parts, dt_raw.shape[1] // parts
    units = 2 * (chans // UNIT)
    count = tokens // BLOCK
    edge = 2 * count + 8
    slots = sum(lax.axis_size(axis) for axis in axes)
    vmem = pl.BlockSpec(memory_space=pltpu.VMEM)
    dma = pltpu.SemaphoreType.DMA

    def v(shape, kind=F32):
        return pltpu.VMEM(shape, kind)

    return pl.pallas_call(
        functools.partial(kernel, axes, size, width),
        out_shape=(
            jax.ShapeDtypeStruct((8, LANES), F32),
            jax.ShapeDtypeStruct(x_in.shape, BF16),
            jax.ShapeDtypeStruct(dt_raw.shape, F32),
        ),
        in_specs=[pl.BlockSpec(memory_space=pl.ANY)] * 5 + [vmem] * 4,
        out_specs=(vmem,) * 3,
        scratch_shapes=[
            v((units, tokens + HALO, UNIT), BF16),
            v((units, tokens, UNIT), BF16),
            v((2, tokens, states), BF16),
            v((2, tokens, states), BF16),
            v((2, heads, tokens)),
            v((2, 8, rows + tokens)),
            v((2, tokens, LANES)),
            v((2, count, BLOCK, 3 * BLOCK), BF16),
            v((2, count, BLOCK, 3 * BLOCK), BF16),
            v((2, count, BLOCK, 2 * DSTATE), BF16),
            v((2, count, BLOCK, 2 * DSTATE), BF16),
            v((2, count, 2 * DSTATE, 2 * BLOCK), BF16),
            v((2, count, 2 * DSTATE, 2 * BLOCK), BF16),
            v((BLOCK + HALO, UNIT)),
            v((units, tokens, UNIT), BF16),
            v((units, tokens, UNIT), BF16),
            v((units, tokens, UNIT), BF16),
            v((units, tokens, UNIT), BF16),
            v((units, tokens, UNIT)),
            v((units, 2 * count + 1, DSTATE, UNIT)),
            v((units, 2 * count + 1, DSTATE, UNIT)),
            v((units, edge, UNIT)),
            v((units, edge, UNIT)),
            v((units, edge, UNIT)),
            v((units, edge, UNIT)),
            v((2, units, DSTATE, UNIT)),
            v((units, DSTATE, UNIT)),
            v((units, DSTATE, UNIT)),
            v((TAPS, tokens + 2 * HALO, UNIT)),
            v((units, tokens + HALO, UNIT)),
            v((2, tokens, LANES)),
            v((2, 8, UNIT)),
            v((units, HALO, UNIT)),
            v((len(axes) + 1, 8, LANES)),
            v((slots, 8, LANES)),
            v((parts, units, rows, UNIT), BF16),
            v((2, heads, tokens)),
            dma((parts, units, 2)),
            dma((parts, units, 2)),
            dma((units, 2)),
            dma((parts, 2, 4)),
            dma((parts, 2, 4)),
            dma((2, 4)),
            dma((parts, units)),
            dma((units,)),
            dma((parts,)),
            dma,
            dma((2, units)),
            dma((2, units)),
            dma((units,)),
            dma((units,)),
            dma((slots,)),
            dma((slots,)),
            dma((parts, units)),
            dma((parts, units)),
            dma((parts,)),
            dma((parts,)),
        ],
        compiler_params=pltpu.CompilerParams(
            collective_id=0, has_side_effects=True, vmem_limit_bytes=60 * 1024 * 1024
        ),
        name="everything",
    )(x_in, target, b_in, c_in, dt_raw, marks, rate, conv_w, sign)


def body(outer, inner, x_in, target, b_in, c_in, dt_raw, resets, decay_rate, conv_w, label):
    rows = x_in.shape[1]
    width = x_in.shape[2] // dt_raw.shape[1]
    marks = jnp.broadcast_to(resets.astype(F32)[:, None], (2, 8, rows))
    sign = jnp.where(jnp.arange(2) == label[0], 1.0, -1.0).astype(F32)
    sign = jnp.broadcast_to(jnp.pad(sign, (0, 6))[:, None], (8, LANES))
    size = rows * lax.axis_size(outer) * lax.axis_size(inner) * x_in.shape[2] * lax.axis_size("head")
    axes = (outer, inner, "head")
    loss, grad, slope = everything(
        x_in, target, b_in, c_in, dt_raw, marks, decay_rate[:, None], conv_w, sign, axes, size, width
    )
    return (loss[0, 0], grad, slope)


def solution(mesh):
    def program(*arrays):
        ways, across = mesh.shape["seq"], mesh.shape["head"]
        groups = arrays[2].shape[2] // DSTATE // across
        parts = math.gcd(groups, ways)
        devices = mesh.devices.reshape(ways // parts, parts, across)
        finer = Mesh(devices, ("outer", "inner", "head"))
        seq = ("outer", "inner")
        in_specs = (
            P(None, seq, "head"),
            P(None, seq, "head"),
            P(None, seq, "head"),
            P(None, seq, "head"),
            P(None, "head", seq),
            P(None, seq),
            P("head"),
            P(None, "head"),
            P(),
        )
        out_specs = (P(), P(None, seq, "head"), P(None, "head", seq))
        inner = functools.partial(body, "outer", "inner")
        mapped = jax.shard_map(inner, mesh=finer, in_specs=in_specs, out_specs=out_specs, check_vma=False)
        return mapped(*arrays)

    return program
```

```python
import functools
import math

import jax
import jax.numpy as jnp
from jax import lax
from jax.experimental import pallas as pl
from jax.experimental.pallas import tpu as pltpu
from jax.sharding import Mesh
from jax.sharding import PartitionSpec as P

DSTATE = 128
BLOCK = 128
CHUNK = 64
LANES = 128
TAPS = 4
HALO = 16
UNIT = 256
AHEAD = 2
EARLY = 4
F32 = jnp.float32
BF16 = jnp.bfloat16


def split(value):
    high = value.astype(BF16)
    low = (value - high.astype(F32)).astype(BF16)
    return high, low


def mm(left, right):
    return lax.dot_general(left, right, (((1,), (0,)), ((), ())), preferred_element_type=F32)


def mm_across(left, right):
    return lax.dot_general(left, right, (((1,), (1,)), ((), ())), preferred_element_type=F32)


def mm_three(left, right):
    high = left.astype(BF16)
    rest = left - high.astype(F32)
    low, least = split(rest)
    return mm(high, right) + mm(low, right) + mm(least, right)


def iota(shape, dim):
    return lax.broadcasted_iota(jnp.int32, shape, dim)


def side(*parts):
    return jnp.concatenate(parts, axis=1)


def stack(*parts):
    return jnp.concatenate(parts, axis=0)


def send(source, goal, sent, got, where):
    return pltpu.make_async_remote_copy(
        src_ref=source,
        dst_ref=goal,
        send_sem=sent,
        recv_sem=got,
        device_id=where,
        device_id_type=pl.DeviceIdType.MESH,
    )


def greet(barrier, where):
    pl.semaphore_signal(barrier, inc=1, device_id=where, device_id_type=pl.DeviceIdType.MESH)


def fold(value):
    return jnp.sum(value.reshape(value.shape[0] // 8, 8, value.shape[1]), axis=0)


def prepare(b, blk, heads, rows, raw_scr, mark_scr, rate, b_scr, c_scr, tok_scr, lm, rm, zc2, qb2, bt2, ct2):
    here = pl.ds(pl.multiple_of(blk * BLOCK, BLOCK), BLOCK)
    later = pl.ds(pl.multiple_of(rows + blk * BLOCK, BLOCK), BLOCK)
    before = pl.ds(pl.multiple_of(rows - BLOCK + blk * BLOCK, BLOCK), BLOCK)
    steps = jax.nn.softplus(raw_scr[b, :, here])
    logs = -steps * rate
    marks = mark_scr[b, :, later]
    keep = 1.0 - side(mark_scr[b, :, before], marks)
    keep_one = keep[:, BLOCK:]
    keep_two = keep_one * pltpu.roll(keep, 1, 1)[:, BLOCK:]
    keep_three = keep_two * pltpu.roll(keep, 2, 1)[:, BLOCK:]
    row = iota((BLOCK, BLOCK), 0)
    col = iota((BLOCK, BLOCK), 1)
    near = (row // CHUNK) == (col // CHUNK)
    upto = jnp.where(near & (row <= col), 1.0, 0.0).astype(BF16)
    full = jnp.where(near, 1.0, 0.0).astype(BF16)
    running = mm_three(logs, upto)
    total = mm_three(logs, full)
    seen = mm(marks.astype(BF16), upto)
    seen_all = mm(marks.astype(BF16), full)
    half = 0.5 * total
    grow = steps * jnp.exp(half - running)
    fall = jnp.exp(running - half)
    center = jnp.exp(half)
    open_all = jnp.where(seen_all == 0.0, 1.0, 0.0).astype(F32)
    through = jnp.exp(total) * open_all[0:1]
    opened = jnp.where(seen == 0.0, 1.0, 0.0).astype(F32)
    closing = jnp.where(seen == seen_all, 1.0, 0.0).astype(F32)
    line = iota((8, BLOCK), 0)
    extra = jnp.zeros((8, BLOCK), F32)
    for i, value in enumerate((keep_one, keep_two, keep_three, seen, opened, closing)):
        extra = jnp.where(line == i, value, extra)
    table = stack(grow, fall, center, through, extra, jnp.zeros((LANES - 4 * heads - 8, BLOCK), F32))
    tok = table.T
    tok_scr[b, here, :] = tok
    base = 4 * heads
    b_rows = b_scr[b, here, :]
    c_rows = c_scr[b, here, :]
    scores = mm_across(c_rows, b_rows)
    scores_t = mm_across(b_rows, c_rows)
    same = near & (tok[:, base + 3 : base + 4] == seen[0:1, :])
    m_high, m_low = split(jnp.where(same & (row >= col), scores, 0.0))
    n_high, n_low = split(jnp.where(same & (row <= col), scores_t, 0.0))
    lm[b, blk] = side(m_high, m_low, m_high)
    rm[b, blk] = side(n_high, n_low, n_high)
    for value, mask, twice, turned in ((c_rows, base + 4, zc2, ct2), (b_rows, base + 5, qb2, bt2)):
        masked = value.astype(F32) * tok[:, mask : mask + 1]
        short = masked.astype(BF16)
        twice[b, blk] = side(short, short)
        flipped = masked.T
        lane = iota((DSTATE, BLOCK), 1)
        one = jnp.where(lane < CHUNK, flipped, 0.0).astype(BF16)
        two = jnp.where(lane >= CHUNK, flipped, 0.0).astype(BF16)
        turned[b, blk] = stack(side(one, one), side(two, two))


def before_chain(
    u, r, b, q, heads, width, count, taps, x_scr, t_scr, tok_scr, lm, bt2, ct2, xe_scr,
    wh, wl, vh, vl, pk, yi, s_loc, g_loc, p_row, r_row, d_row, th_row, score_scr,
):
    chans = UNIT
    per = chans // width
    row = iota((LANES, chans), 0)
    head = iota((LANES, chans), 1) // width + q * per

    def spread(offset):
        one = jnp.where(row == head + offset, 1.0, 0.0).astype(BF16)
        return stack(one, one)

    spread_grow, spread_fall = spread(0), spread(heads)
    spread_center, spread_through = spread(2 * heads), spread(3 * heads)
    base = 4 * heads
    s_loc[r, 0] = jnp.zeros((DSTATE, chans), F32)
    g_loc[r, 2 * count] = jnp.zeros((DSTATE, chans), F32)

    def forward(blk, through):
        first = pl.multiple_of(blk * BLOCK, BLOCK)
        here = pl.ds(first, BLOCK)
        tok = tok_scr[b, here, :]
        both = side(*split(tok))
        ends = stack(both[0:16], both[CHUNK : CHUNK + 16])
        grow = mm(both, spread_grow)
        fall = mm(both, spread_fall)
        center = mm(ends, spread_center)
        pass_by = mm(ends, spread_through)
        xe_scr[...] = x_scr[u, pl.ds(first, BLOCK + HALO), :].astype(F32)
        pre = taps[3:4, :] * xe_scr[pl.ds(HALO, BLOCK), :]
        for back in range(1, TAPS):
            scale = tok[:, base + back - 1 : base + back] * taps[3 - back : 4 - back, :]
            pre = pre + scale * xe_scr[pl.ds(HALO - back, BLOCK), :]
        sig = jax.nn.sigmoid(pre)
        values = pre * sig
        slope = sig + values * (1.0 - sig)
        w_high, w_low = split(grow * values)
        v = fall * t_scr[u, here, :].astype(F32)
        v_high, v_low = split(v)
        wh[r, here, :] = w_high
        wl[r, here, :] = w_low
        vh[r, here, :] = v_high
        vl[r, here, :] = v_low
        pk[r, here, :] = grow * slope
        inside = mm(lm[b, blk], stack(w_high, w_high, w_low))
        yi[r, here, :] = inside
        score_scr[b] += fold(v * inside)
        added = mm(bt2[b, blk], stack(w_high, w_low))
        state = s_loc[r, 2 * blk]
        for sub in range(2):
            k = 2 * blk + sub
            c_one = center[16 * sub : 16 * sub + 1, :]
            t_one = pass_by[16 * sub : 16 * sub + 1, :]
            p_row[u, pl.ds(k, 1), :] = through
            d_row[u, pl.ds(k, 1), :] = c_one
            th_row[u, pl.ds(k, 1), :] = t_one
            through = through * t_one
            state = t_one * state + c_one * added[DSTATE * sub : DSTATE * (sub + 1), :]
            s_loc[r, k + 1] = state
        return through

    through = lax.fori_loop(0, count, forward, jnp.ones((1, chans), F32))
    p_row[u, 2 * count : 2 * count + 1, :] = through

    def backward(step, through):
        blk = count - 1 - step
        here = pl.ds(pl.multiple_of(blk * BLOCK, BLOCK), BLOCK)
        added = mm(ct2[b, blk], stack(vh[r, here, :], vl[r, here, :]))
        state = g_loc[r, 2 * blk + 2]
        for sub in (1, 0):
            k = 2 * blk + sub
            t_one = th_row[u, pl.ds(k, 1), :]
            r_row[u, pl.ds(k + 1, 1), :] = through
            through = through * t_one
            fresh = d_row[u, pl.ds(k, 1), :] * added[DSTATE * sub : DSTATE * (sub + 1), :]
            score_scr[b] += fold(s_loc[r, k] * fresh)
            state = t_one * state + fresh
            g_loc[r, k] = state
        return through

    lax.fori_loop(0, count, backward, jnp.ones((1, chans), F32))


def after_chain(
    u, r, b, q, heads, width, count, taps, tok_scr, rm, zc2, qb2,
    wh, wl, vh, vl, pk, yi, s_loc, g_loc, p_row, r_row, d_row, start_scr, later_scr, cv_scr, grad_scr, hd_scr,
):
    chans = UNIT
    per = chans // width
    base = 4 * heads
    lane_head = iota((chans, LANES), 0) // width + q * per
    col = iota((chans, LANES), 1)
    pick_diff = jnp.where(col == lane_head, 1.0, 0.0).astype(BF16)
    pick_step = jnp.where(col == lane_head + heads, 1.0, 0.0).astype(BF16)
    pick = stack(pick_diff, pick_diff, pick_step, pick_step)
    tokens = count * BLOCK
    for back in range(TAPS):
        cv_scr[back, pl.ds(0, HALO), :] = jnp.zeros((HALO, chans), F32)
        cv_scr[back, pl.ds(HALO + tokens, HALO), :] = jnp.zeros((HALO, chans), F32)
    line = iota((BLOCK, chans), 0)

    def block(blk, carry):
        first = pl.multiple_of(blk * BLOCK, BLOCK)
        here = pl.ds(first, BLOCK)
        start = start_scr[u]
        later = later_scr[u]
        w_high, w_low = wh[r, here, :], wl[r, here, :]
        v_high, v_low = vh[r, here, :], vl[r, here, :]
        y_all, d_all, crossed = [], [], []
        state = s_loc[r, 2 * blk] + p_row[u, pl.ds(2 * blk, 1), :] * start
        for sub in range(2):
            k = 2 * blk + sub
            center = d_row[u, pl.ds(k, 1), :]
            rows = pl.ds(sub * CHUNK, CHUNK)
            slope = g_loc[r, k + 1] + r_row[u, pl.ds(k + 1, 1), :] * later
            after = s_loc[r, k + 1] + p_row[u, pl.ds(k + 1, 1), :] * start
            y_all.append(mm(zc2[b, blk, rows, :], stack(*split(center * state))))
            d_all.append(mm(qb2[b, blk, rows, :], stack(*split(center * slope))))
            crossed.append(jnp.sum(after * slope, axis=0, keepdims=True))
            state = after
        y_in = yi[r, here, :] + stack(*y_all)
        d_in = mm(rm[b, blk], stack(v_high, v_high, v_low)) + stack(*d_all)
        read = (v_high.astype(F32) + v_low.astype(F32)) * y_in
        stepped = (w_high.astype(F32) + w_low.astype(F32)) * d_in
        diff = read - stepped
        diff = jnp.where(line == CHUNK - 1, diff + crossed[0], diff)
        diff = jnp.where(line == BLOCK - 1, diff + crossed[1], diff)
        hd_scr[b, here, :] += mm(side(*split(diff), *split(stepped)), pick)
        d_pre = pk[r, here, :] * d_in
        tok = tok_scr[b, here, :]
        below = pl.ds(pl.multiple_of(HALO + blk * BLOCK, HALO), BLOCK)
        cv_scr[0, below, :] = taps[3:4, :] * d_pre
        for back in range(1, TAPS):
            scale = tok[:, base + back - 1 : base + back] * taps[3 - back : 4 - back, :]
            cv_scr[back, below, :] = scale * d_pre
        return carry

    lax.fori_loop(0, count, block, 0)
    for begin, size in [(0, HALO)] + [(HALO + i * BLOCK, BLOCK) for i in range(count)]:
        total = cv_scr[0, pl.ds(begin, size), :]
        for back in range(1, TAPS):
            total = total + cv_scr[back, pl.ds(begin + back, size), :]
        grad_scr[u, pl.ds(begin, size), :] = total


def kernel(
    axes, size, width,
    x_ref, t_ref, b_ref, c_ref, raw_ref, reset_ref, rate_ref, w_ref, label_ref,
    loss_ref, out_ref, slope_ref,
    x_scr, t_scr, b_scr, c_scr, raw_scr, mark_scr, tok_scr, lm, rm, zc2, qb2, bt2, ct2, xe_scr,
    wh, wl, vh, vl, pk, yi, s_loc, g_loc, p_row, r_row, d_row, th_row, chain_out, start_scr, later_scr,
    cv_scr, grad_scr, hd_scr, score_scr, halo_scr, part_scr, slot_scr, out_scr, lean_scr, mark_ref, wide_scr,
    wsent, wgot, wkept, nsent, ngot, nkept, hsent, hgot, msent, mgot, csent, cgot,
    esent, egot, psent, pgot, osent, ogot, rsent, rgot, fsent, fgot,
):
    outer, inner, cores = axes
    units, tokens = t_scr.shape[0], t_scr.shape[1]
    ring = wh.shape[0]
    rows = x_ref.shape[1]
    states, heads = b_scr.shape[2], raw_scr.shape[1]
    per_pair = units // 2
    chans = per_pair * UNIT
    count = tokens // BLOCK
    parts, planes = lax.axis_size(inner), lax.axis_size(outer)
    mine, plane = lax.axis_index(inner), lax.axis_index(outer)
    has_less = plane > 0
    has_more = plane < planes - 1
    gives = has_more & (mine == parts - 1)
    less, more = lax.rem(plane + planes - 1, planes), lax.rem(plane + 1, planes)
    barrier = pltpu.get_barrier_semaphore()
    across, core = lax.axis_size(cores), lax.axis_index(cores)
    mates = [(i, h) for i in range(parts) for h in range(across)][1:]

    def mate(i, h):
        return {inner: lax.rem(mine + i, parts), cores: lax.rem(core + h, across)}

    for i, h in mates:
        greet(barrier, mate(i, h))
    for away in range(1, planes):
        greet(barrier, {outer: lax.rem(plane + away, planes)})
    peers = len(mates) + planes - 1

    @pl.when(has_less)
    def _():
        greet(barrier, {outer: less, inner: parts - 1})

    @pl.when(gives)
    def _():
        for j in range(parts):
            greet(barrier, {outer: more, inner: j})

    pl.semaphore_wait(barrier, peers + has_less.astype(jnp.int32) + parts * gives.astype(jnp.int32))

    for b in range(2):
        mark_ref[b] = jnp.broadcast_to(reset_ref[b : b + 1, :].astype(F32), (8, rows))

    def wide_views(u, source, goal):
        b, q = u // per_pair, lax.rem(u, per_pair)
        wide = pl.ds(pl.multiple_of(goal * chans + q * UNIT, UNIT), UNIT)
        yield x_ref.at[b, :, wide], x_scr.at[u, pl.ds(pl.multiple_of(HALO + source * rows, HALO), rows)]
        yield t_ref.at[b, :, wide], t_scr.at[u, pl.ds(pl.multiple_of(source * rows, HALO), rows)]

    def thin_views(b, source, goal):
        group = pl.ds(pl.multiple_of(goal * states, LANES), states)
        lines = pl.ds(pl.multiple_of(goal * heads, 8), heads)
        here = pl.ds(pl.multiple_of(source * rows, LANES), rows)
        later = pl.ds(pl.multiple_of(rows + source * rows, LANES), rows)
        yield b_ref.at[b, :, group], b_scr.at[b, here]
        yield c_ref.at[b, :, group], c_scr.at[b, here]
        yield raw_ref.at[b, lines], raw_scr.at[b, :, here]
        yield mark_ref.at[b], mark_scr.at[b, :, later]

    def remote(views, index, sent, got):
        for away in range(1, parts):
            goal = lax.rem(mine + away, parts)
            for i, (source, target) in enumerate(views(index, mine, goal)):
                yield send(source, target, sent.at[away, index, i], got.at[away, index, i], {inner: goal})

    def local(views, index, kept):
        for i, (source, target) in enumerate(views(index, mine, mine)):
            yield pltpu.make_async_copy(source, target, kept.at[index, i])

    wides = functools.partial(remote, wide_views, sent=wsent, got=wgot)
    thins = functools.partial(remote, thin_views, sent=nsent, got=ngot)

    def edges(u, j):
        b, q = u // per_pair, lax.rem(u, per_pair)
        wide = pl.ds(pl.multiple_of(j * chans + q * UNIT, UNIT), UNIT)
        return send(
            x_ref.at[b, pl.ds(rows - HALO, HALO), wide], x_scr.at[u, pl.ds(0, HALO)],
            hsent.at[j, u], hgot.at[u], {outer: more, inner: j},
        )

    def edge_marks(j):
        return send(mark_ref, mark_scr.at[:, :, pl.ds(0, rows)], msent.at[j], mgot, {outer: more, inner: j})

    def issue(u):
        for copy in wides(u):
            copy.start()
        for copy in local(wide_views, u, wkept):
            copy.start()

    @pl.when(gives)
    def _():
        for j in range(parts):
            edge_marks(j).start()

    for b in range(2):
        for copy in thins(b):
            copy.start()
        for copy in local(thin_views, b, nkept):
            copy.start()
        if b == 0:
            for u in range(min(AHEAD, units)):
                issue(u)

    @pl.when(gives)
    def _():
        def one(u, carry):
            for j in range(parts):
                edges(u, j).start()
            return carry

        lax.fori_loop(0, units, one, 0)

    @pl.when(has_less)
    def _():
        edge_marks(0).wait_recv()

    @pl.when(jnp.logical_not(has_less))
    def _():
        x_scr[:, pl.ds(0, HALO), :] = jnp.zeros((units, HALO, UNIT), BF16)
        mark_scr[:, :, pl.ds(0, rows)] = jnp.zeros((2, 8, rows), F32)

    score_scr[...] = jnp.zeros_like(score_scr)
    hd_scr[...] = jnp.zeros_like(hd_scr)
    ours = iota((heads, rate_ref.shape[1]), 0) + mine * heads == iota((heads, rate_ref.shape[1]), 1)
    rate = jnp.sum(jnp.where(ours, rate_ref[...], 0.0), axis=1, keepdims=True)
    through_row = pl.ds(2 * count, 1)
    ways = ((s_loc, 2 * count, start_scr, has_less, has_more, more), (g_loc, 0, later_scr, has_more, has_less, less))
    for _, _, arrived, arrives, _, _ in ways:

        @pl.when(jnp.logical_not(arrives))
        def _():
            arrived[...] = jnp.zeros(arrived.shape, F32)

    def chain_copy(way, u, arrived, goal):
        return send(chain_out.at[way, u], arrived.at[u], csent.at[way, u], cgot.at[way, u], {outer: goal})

    def edge(u):
        return send(grad_scr.at[u, pl.ds(0, HALO)], halo_scr.at[u], esent.at[u], egot.at[u], {outer: less})

    def taps_of(q):
        return w_ref[:, pl.ds(pl.multiple_of(mine * chans + q * UNIT, UNIT), UNIT)]

    early = early_units(units, parts, planes)

    def early_out(u, away):
        goal = lax.rem(mine + away, parts)
        source = grad_scr.at[u, pl.ds(pl.multiple_of(HALO + goal * rows, HALO), rows)]
        return send(source, wide_scr.at[away, u], fsent.at[away, u], fgot.at[away, u], {inner: goal})

    def close(u):
        @pl.when(has_more)
        def _():
            edge(u).wait_recv()
            grad_scr[u, pl.ds(tokens, HALO), :] += halo_scr[u]

    def score_copy(spot):
        slot = slot_scr.at[mine * across + core]
        return send(part_scr.at[0], slot, psent.at[spot], pgot.at[spot], mate(*mates[spot]))

    def turn(time, carry):
        @pl.when(time + AHEAD < units)
        def _():
            issue(time + AHEAD)

        @pl.when(time < units)
        def _():
            u = time
            b, q = u // per_pair, lax.rem(u, per_pair)

            @pl.when(q == 0)
            def _():
                for copy in thins(b):
                    copy.wait_recv()
                for copy in local(thin_views, b, nkept):
                    copy.wait()

                def one(blk, carry):
                    prepare(
                        b, blk, heads, rows, raw_scr, mark_scr, rate, b_scr, c_scr, tok_scr, lm, rm, zc2, qb2, bt2, ct2
                    )
                    return carry

                lax.fori_loop(0, count, one, 0)

            for copy in wides(u):
                copy.wait_recv()
            for copy in local(wide_views, u, wkept):
                copy.wait()

            @pl.when(has_less)
            def _():
                edges(u, 0).wait_recv()

            if early > 0:

                @pl.when(u == units - 1)
                def _():
                    def one(i, carry):
                        close(i)
                        for away in range(1, parts):
                            early_out(i, away).start()
                        return carry

                    lax.fori_loop(0, early, one, 0)

            before_chain(
                u, lax.rem(u, ring), b, q, heads, width, count, taps_of(q), x_scr, t_scr, tok_scr, lm, bt2, ct2, xe_scr,
                wh, wl, vh, vl, pk, yi, s_loc, g_loc, p_row, r_row, d_row, th_row, score_scr,
            )

        for way, (own, end, arrived, arrives, leaves, goal) in enumerate(ways):
            u = time - (plane if way == 0 else planes - 1 - plane)

            @pl.when((u >= 0) & (u < units))
            def _():
                copy = chain_copy(way, u, arrived, goal)

                @pl.when(arrives)
                def _():
                    copy.wait_recv()

                @pl.when(leaves)
                def _():
                    chain_out[way, u] = p_row[u, through_row, :] * arrived[u] + own[lax.rem(u, ring), end]
                    copy.start()

        u = time - (planes - 1)

        @pl.when(u >= 0)
        def _():
            b, q = u // per_pair, lax.rem(u, per_pair)
            score_scr[b] += fold(start_scr[u] * g_loc[lax.rem(u, ring), 0])

            @pl.when(u == units - 1)
            def _():
                own = [jnp.sum(jnp.sum(score_scr[i], axis=0, keepdims=True), axis=1, keepdims=True) for i in range(2)]
                part = jnp.where(iota((8, LANES), 0) == 0, own[0], own[1])
                part_scr[0] = part
                slot_scr[mine * across + core] = part
                for spot in range(len(mates)):
                    score_copy(spot).start()

            after_chain(
                u, lax.rem(u, ring), b, q, heads, width, count, taps_of(q), tok_scr, rm, zc2, qb2,
                wh, wl, vh, vl, pk, yi, s_loc, g_loc, p_row, r_row, d_row, start_scr, later_scr, cv_scr, grad_scr,
                hd_scr,
            )

            @pl.when(has_less)
            def _():
                edge(u).start()

        return carry

    lax.fori_loop(0, units + planes - 1, turn, 0)

    for spot in range(len(mates)):
        score_copy(spot).wait_recv()
    subtotal = slot_scr[0]
    for i in range(1, parts * across):
        subtotal = subtotal + slot_scr[i]
    part_scr[1] = subtotal
    base = parts * across
    waits = []
    for away in range(1, planes):
        goal = lax.rem(plane + away, planes)
        spot = base + away - 1
        copy = send(part_scr.at[1], slot_scr.at[base + plane], psent.at[spot], pgot.at[spot], {outer: goal})
        copy.start()
        waits.append(copy)
    slot_scr[base + plane] = subtotal
    back_row = iota((BLOCK, BLOCK), 0)
    back_col = iota((BLOCK, BLOCK), 1)
    near = (back_row // CHUNK) == (back_col // CHUNK)
    onward = jnp.where(near & (back_row >= back_col), 1.0, 0.0).astype(BF16)
    for b in range(2):
        for blk in range(count):
            here = pl.ds(blk * BLOCK, BLOCK)
            sums = hd_scr[b, here, :].T
            raw = raw_scr[b, :, here]
            d_log = mm_three(sums[0:heads], onward)
            by_step = sums[heads : 2 * heads] / jax.nn.softplus(raw)
            lean_scr[b, :, here] = jax.nn.sigmoid(raw) * (by_step - rate * d_log)
    for copy in waits:
        copy.wait_recv()
    subtotal = slot_scr[base]
    for i in range(1, planes):
        subtotal = subtotal + slot_scr[base + i]
    row = iota((8, LANES), 0)
    sign = jnp.where(row == label_ref[0], 1.0, jnp.where(row < 2, -1.0, 0.0)).astype(F32)
    signed = subtotal * sign / math.sqrt(size)
    margin = signed[0:1, :] + signed[1:2, :]
    loss_ref[0, 0] = jax.nn.softplus(-margin)[0, 0]
    factors = -jax.nn.sigmoid(-margin) * sign
    scale = [factors[b : b + 1, 0:1] for b in range(2)]

    def out_view(u, owner):
        b, q = u // per_pair, lax.rem(u, per_pair)
        return out_ref.at[b, :, pl.ds(pl.multiple_of(owner * chans + q * UNIT, UNIT), UNIT)]

    def wide_out(u, away):
        goal = lax.rem(mine + away, parts)
        return send(out_scr.at[away, u], out_view(u, mine), osent.at[away, u], ogot.at[away, u], {inner: goal})

    lines = pl.ds(pl.multiple_of(mine * heads, 8), heads)

    def thin_out(away):
        goal = lax.rem(mine + away, parts)
        return send(out_lean(away), slope_ref.at[:, lines], rsent.at[away], rgot.at[away], {inner: goal})

    def out_lean(away):
        goal = lax.rem(mine + away, parts)
        return lean_scr.at[:, :, pl.ds(pl.multiple_of(goal * rows, LANES), rows)]

    for b in range(2):
        lean_scr[b] = scale[b] * lean_scr[b]
    for away in range(1, parts):
        thin_out(away).start()
    slope_ref[:, lines, :] = lean_scr[:, :, pl.ds(pl.multiple_of(mine * rows, LANES), rows)]

    def factor_of(u):
        return jnp.where(u // per_pair == 0, scale[0], scale[1])

    def block_of(u, away):
        goal = lax.rem(mine + away, parts)
        return grad_scr[u, pl.ds(pl.multiple_of(HALO + goal * rows, HALO), rows), :]

    def give(u, carry):
        close(u)
        for away in range(1, parts):
            out_scr[away, u] = (factor_of(u) * block_of(u, away)).astype(BF16)
            wide_out(u, away).start()
        return carry

    lax.fori_loop(early, units, give, 0)

    def keep_own(u, carry):
        out_view(u, mine)[...] = (factor_of(u) * block_of(u, 0)).astype(BF16)
        return carry

    lax.fori_loop(0, units, keep_own, 0)

    def take(u, carry):
        for away in range(1, parts):
            early_out(u, away).wait_recv()
            owner = lax.rem(mine + parts - away, parts)
            out_view(u, owner)[...] = (factor_of(u) * wide_scr[away, u]).astype(BF16)
        return carry

    if early > 0:
        lax.fori_loop(0, early, take, 0)

    def drain(u, carry):
        for copy in wides(u):
            copy.wait_send()
        for way, (_, _, arrived, _, leaves, goal) in enumerate(ways):

            @pl.when(leaves)
            def _():
                chain_copy(way, u, arrived, goal).wait_send()

        @pl.when(has_less)
        def _():
            edge(u).wait_send()

        @pl.when(gives)
        def _():
            for j in range(parts):
                edges(u, j).wait_send()

        return carry

    lax.fori_loop(0, units, drain, 0)

    def drain_early(u, carry):
        for away in range(1, parts):
            early_out(u, away).wait_send()
        return carry

    def drain_late(u, carry):
        for away in range(1, parts):
            wide_out(u, away).wait()
        return carry

    if early > 0:
        lax.fori_loop(0, early, drain_early, 0)
    lax.fori_loop(early, units, drain_late, 0)
    for spot in range(len(mates)):
        score_copy(spot).wait_send()
    for away in range(1, parts):
        thin_out(away).wait()
    for b in range(2):
        for copy in thins(b):
            copy.wait_send()
    for copy in waits:
        copy.wait_send()

    @pl.when(gives)
    def _():
        for j in range(parts):
            edge_marks(j).wait_send()


def early_units(units, parts, planes):
    return max(0, min(EARLY, units - planes)) if parts > 1 else 0


def everything(x_in, target, b_in, c_in, dt_raw, resets, rate, conv_w, label, axes, size, width):
    parts = lax.axis_size(axes[1])
    rows = x_in.shape[1]
    tokens = parts * rows
    chans, states, heads = x_in.shape[2] // parts, b_in.shape[2] // parts, dt_raw.shape[1] // parts
    units = 2 * (chans // UNIT)
    count = tokens // BLOCK
    edge = 2 * count + 8
    planes = lax.axis_size(axes[0])
    ring = min(units, planes)
    slots = planes + parts * lax.axis_size(axes[2])
    early = max(1, early_units(units, parts, planes))
    vmem = pl.BlockSpec(memory_space=pltpu.VMEM)
    dma = pltpu.SemaphoreType.DMA

    def v(shape, kind=F32):
        return pltpu.VMEM(shape, kind)

    return pl.pallas_call(
        functools.partial(kernel, axes, size, width),
        out_shape=(
            jax.ShapeDtypeStruct((1, 1), F32),
            jax.ShapeDtypeStruct(x_in.shape, BF16),
            jax.ShapeDtypeStruct(dt_raw.shape, F32),
        ),
        in_specs=[pl.BlockSpec(memory_space=pl.ANY)] * 5 + [vmem] * 3 + [pl.BlockSpec(memory_space=pltpu.SMEM)],
        out_specs=(pl.BlockSpec(memory_space=pltpu.SMEM), vmem, vmem),
        scratch_shapes=[
            v((units, tokens + HALO, UNIT), BF16),
            v((units, tokens, UNIT), BF16),
            v((2, tokens, states), BF16),
            v((2, tokens, states), BF16),
            v((2, heads, tokens)),
            v((2, 8, rows + tokens)),
            v((2, tokens, LANES)),
            v((2, count, BLOCK, 3 * BLOCK), BF16),
            v((2, count, BLOCK, 3 * BLOCK), BF16),
            v((2, count, BLOCK, 2 * DSTATE), BF16),
            v((2, count, BLOCK, 2 * DSTATE), BF16),
            v((2, count, 2 * DSTATE, 2 * BLOCK), BF16),
            v((2, count, 2 * DSTATE, 2 * BLOCK), BF16),
            v((BLOCK + HALO, UNIT)),
            v((ring, tokens, UNIT), BF16),
            v((ring, tokens, UNIT), BF16),
            v((ring, tokens, UNIT), BF16),
            v((ring, tokens, UNIT), BF16),
            v((ring, tokens, UNIT)),
            v((ring, tokens, UNIT)),
            v((ring, 2 * count + 1, DSTATE, UNIT)),
            v((ring, 2 * count + 1, DSTATE, UNIT)),
            v((units, edge, UNIT)),
            v((units, edge, UNIT)),
            v((units, edge, UNIT)),
            v((units, edge, UNIT)),
            v((2, units, DSTATE, UNIT)),
            v((units, DSTATE, UNIT)),
            v((units, DSTATE, UNIT)),
            v((TAPS, tokens + 2 * HALO, UNIT)),
            v((units, tokens + HALO, UNIT)),
            v((2, tokens, LANES)),
            v((2, 8, UNIT)),
            v((units, HALO, UNIT)),
            v((2, 8, LANES)),
            v((slots, 8, LANES)),
            v((parts, units, rows, UNIT), BF16),
            v((2, heads, tokens)),
            v((2, 8, rows)),
            v((parts, early, rows, UNIT)),
            dma((parts, units, 2)),
            dma((parts, units, 2)),
            dma((units, 2)),
            dma((parts, 2, 4)),
            dma((parts, 2, 4)),
            dma((2, 4)),
            dma((parts, units)),
            dma((units,)),
            dma((parts,)),
            dma,
            dma((2, units)),
            dma((2, units)),
            dma((units,)),
            dma((units,)),
            dma((slots,)),
            dma((slots,)),
            dma((parts, units)),
            dma((parts, units)),
            dma((parts,)),
            dma((parts,)),
            dma((parts, early)),
            dma((parts, early)),
        ],
        compiler_params=pltpu.CompilerParams(
            collective_id=0, has_side_effects=True, vmem_limit_bytes=60 * 1024 * 1024
        ),
        name="everything",
    )(x_in, target, b_in, c_in, dt_raw, resets, rate, conv_w, label)


def body(outer, inner, x_in, target, b_in, c_in, dt_raw, resets, decay_rate, conv_w, label):
    rows = x_in.shape[1]
    width = x_in.shape[2] // dt_raw.shape[1]
    size = rows * lax.axis_size(outer) * lax.axis_size(inner) * x_in.shape[2] * lax.axis_size("head")
    axes = (outer, inner, "head")
    loss, grad, slope = everything(
        x_in, target, b_in, c_in, dt_raw, resets, decay_rate[None], conv_w, label, axes, size, width
    )
    return (loss[0, 0], grad, slope)


def solution(mesh):
    def program(*arrays):
        ways, across = mesh.shape["seq"], mesh.shape["head"]
        groups = arrays[2].shape[2] // DSTATE // across
        parts = math.gcd(groups, ways)
        devices = mesh.devices.reshape(ways // parts, parts, across)
        finer = Mesh(devices, ("outer", "inner", "head"))
        seq = ("outer", "inner")
        in_specs = (
            P(None, seq, "head"),
            P(None, seq, "head"),
            P(None, seq, "head"),
            P(None, seq, "head"),
            P(None, "head", seq),
            P(None, seq),
            P("head"),
            P(None, "head"),
            P(),
        )
        out_specs = (P(), P(None, seq, "head"), P(None, "head", seq))
        inner = functools.partial(body, "outer", "inner")
        mapped = jax.shard_map(inner, mesh=finer, in_specs=in_specs, out_specs=out_specs, check_vma=False)
        return mapped(*arrays)

    return program
```

```python
import functools
import math

import jax
import jax.numpy as jnp
from jax import lax
from jax.experimental import pallas as pl
from jax.experimental.pallas import tpu as pltpu
from jax.sharding import Mesh
from jax.sharding import PartitionSpec as P

DSTATE = 128
BLOCK = 128
CHUNK = 64
LANES = 128
TAPS = 4
HALO = 16
UNIT = 256
AHEAD = 2
EARLY = 3
HOPS = 1
F32 = jnp.float32
BF16 = jnp.bfloat16


def split(value):
    high = value.astype(BF16)
    low = (value - high.astype(F32)).astype(BF16)
    return high, low


def mm(left, right):
    return lax.dot_general(left, right, (((1,), (0,)), ((), ())), preferred_element_type=F32)


def mm_across(left, right):
    return lax.dot_general(left, right, (((1,), (1,)), ((), ())), preferred_element_type=F32)


def mm_three(left, right):
    high = left.astype(BF16)
    rest = left - high.astype(F32)
    low, least = split(rest)
    return mm(high, right) + mm(low, right) + mm(least, right)


def iota(shape, dim):
    return lax.broadcasted_iota(jnp.int32, shape, dim)


def side(*parts):
    return jnp.concatenate(parts, axis=1)


def stack(*parts):
    return jnp.concatenate(parts, axis=0)


def send(source, goal, sent, got, where):
    return pltpu.make_async_remote_copy(
        src_ref=source,
        dst_ref=goal,
        send_sem=sent,
        recv_sem=got,
        device_id=where,
        device_id_type=pl.DeviceIdType.MESH,
    )


def greet(barrier, where):
    pl.semaphore_signal(barrier, inc=1, device_id=where, device_id_type=pl.DeviceIdType.MESH)


def fold(value):
    return jnp.sum(value.reshape(value.shape[0] // 8, 8, value.shape[1]), axis=0)


def prepare(b, blk, heads, rows, raw_scr, mark_scr, rate, b_scr, c_scr, tok_scr, lm, rm, zc2, qb2, bt2, ct2):
    here = pl.ds(pl.multiple_of(blk * BLOCK, BLOCK), BLOCK)
    later = pl.ds(pl.multiple_of(rows + blk * BLOCK, BLOCK), BLOCK)
    before = pl.ds(pl.multiple_of(rows - BLOCK + blk * BLOCK, BLOCK), BLOCK)
    steps = jax.nn.softplus(raw_scr[b, :, here])
    logs = -steps * rate
    marks = mark_scr[b, :, later]
    keep = 1.0 - side(mark_scr[b, :, before], marks)
    keep_one = keep[:, BLOCK:]
    keep_two = keep_one * pltpu.roll(keep, 1, 1)[:, BLOCK:]
    keep_three = keep_two * pltpu.roll(keep, 2, 1)[:, BLOCK:]
    row = iota((BLOCK, BLOCK), 0)
    col = iota((BLOCK, BLOCK), 1)
    near = (row // CHUNK) == (col // CHUNK)
    upto = jnp.where(near & (row <= col), 1.0, 0.0).astype(BF16)
    full = jnp.where(near, 1.0, 0.0).astype(BF16)
    running = mm_three(logs, upto)
    total = mm_three(logs, full)
    seen = mm(marks.astype(BF16), upto)
    seen_all = mm(marks.astype(BF16), full)
    half = 0.5 * total
    grow = steps * jnp.exp(half - running)
    fall = jnp.exp(running - half)
    center = jnp.exp(half)
    open_all = jnp.where(seen_all == 0.0, 1.0, 0.0).astype(F32)
    through = jnp.exp(total) * open_all[0:1]
    opened = jnp.where(seen == 0.0, 1.0, 0.0).astype(F32)
    closing = jnp.where(seen == seen_all, 1.0, 0.0).astype(F32)
    line = iota((8, BLOCK), 0)
    extra = jnp.zeros((8, BLOCK), F32)
    for i, value in enumerate((keep_one, keep_two, keep_three, seen, opened, closing)):
        extra = jnp.where(line == i, value, extra)
    table = stack(grow, fall, center, through, extra, jnp.zeros((LANES - 4 * heads - 8, BLOCK), F32))
    tok = table.T
    tok_scr[b, here, :] = tok
    base = 4 * heads
    b_rows = b_scr[b, here, :]
    c_rows = c_scr[b, here, :]
    scores = mm_across(c_rows, b_rows)
    scores_t = mm_across(b_rows, c_rows)
    same = near & (tok[:, base + 3 : base + 4] == seen[0:1, :])
    m_high, m_low = split(jnp.where(same & (row >= col), scores, 0.0))
    n_high, n_low = split(jnp.where(same & (row <= col), scores_t, 0.0))
    lm[b, blk] = side(m_high, m_low, m_high)
    rm[b, blk] = side(n_high, n_low, n_high)
    for value, mask, twice, turned in ((c_rows, base + 4, zc2, ct2), (b_rows, base + 5, qb2, bt2)):
        masked = value.astype(F32) * tok[:, mask : mask + 1]
        short = masked.astype(BF16)
        twice[b, blk] = side(short, short)
        flipped = masked.T
        lane = iota((DSTATE, BLOCK), 1)
        one = jnp.where(lane < CHUNK, flipped, 0.0).astype(BF16)
        two = jnp.where(lane >= CHUNK, flipped, 0.0).astype(BF16)
        turned[b, blk] = stack(side(one, one), side(two, two))


def before_chain(
    u, r, b, q, heads, width, count, taps, x_scr, t_scr, tok_scr, lm, bt2, ct2, xe_scr,
    wh, wl, vh, vl, pk, yi, s_loc, g_loc, p_row, r_row, d_row, th_row, score_scr,
):
    chans = UNIT
    per = chans // width
    row = iota((LANES, chans), 0)
    head = iota((LANES, chans), 1) // width + q * per

    def spread(offset):
        one = jnp.where(row == head + offset, 1.0, 0.0).astype(BF16)
        return stack(one, one)

    spread_grow, spread_fall = spread(0), spread(heads)
    spread_center, spread_through = spread(2 * heads), spread(3 * heads)
    base = 4 * heads
    s_loc[r, 0] = jnp.zeros((DSTATE, chans), F32)
    g_loc[r, 2 * count] = jnp.zeros((DSTATE, chans), F32)

    def forward(blk, through):
        first = pl.multiple_of(blk * BLOCK, BLOCK)
        here = pl.ds(first, BLOCK)
        tok = tok_scr[b, here, :]
        both = side(*split(tok))
        ends = stack(both[0:16], both[CHUNK : CHUNK + 16])
        grow = mm(both, spread_grow)
        fall = mm(both, spread_fall)
        center = mm(ends, spread_center)
        pass_by = mm(ends, spread_through)
        xe_scr[...] = x_scr[u, pl.ds(first, BLOCK + HALO), :].astype(F32)
        pre = taps[3:4, :] * xe_scr[pl.ds(HALO, BLOCK), :]
        for back in range(1, TAPS):
            scale = tok[:, base + back - 1 : base + back] * taps[3 - back : 4 - back, :]
            pre = pre + scale * xe_scr[pl.ds(HALO - back, BLOCK), :]
        sig = jax.nn.sigmoid(pre)
        values = pre * sig
        slope = sig + values * (1.0 - sig)
        w_high, w_low = split(grow * values)
        v = fall * t_scr[u, here, :].astype(F32)
        v_high, v_low = split(v)
        wh[r, here, :] = w_high
        wl[r, here, :] = w_low
        vh[r, here, :] = v_high
        vl[r, here, :] = v_low
        pk[r, here, :] = grow * slope
        inside = mm(lm[b, blk], stack(w_high, w_high, w_low))
        yi[r, here, :] = inside
        score_scr[b] += fold(v * inside)
        added = mm(bt2[b, blk], stack(w_high, w_low))
        state = s_loc[r, 2 * blk]
        for sub in range(2):
            k = 2 * blk + sub
            c_one = center[16 * sub : 16 * sub + 1, :]
            t_one = pass_by[16 * sub : 16 * sub + 1, :]
            p_row[u, pl.ds(k, 1), :] = through
            d_row[u, pl.ds(k, 1), :] = c_one
            th_row[u, pl.ds(k, 1), :] = t_one
            through = through * t_one
            state = t_one * state + c_one * added[DSTATE * sub : DSTATE * (sub + 1), :]
            s_loc[r, k + 1] = state
        return through

    through = lax.fori_loop(0, count, forward, jnp.ones((1, chans), F32))
    p_row[u, 2 * count : 2 * count + 1, :] = through

    def backward(step, through):
        blk = count - 1 - step
        here = pl.ds(pl.multiple_of(blk * BLOCK, BLOCK), BLOCK)
        added = mm(ct2[b, blk], stack(vh[r, here, :], vl[r, here, :]))
        state = g_loc[r, 2 * blk + 2]
        for sub in (1, 0):
            k = 2 * blk + sub
            t_one = th_row[u, pl.ds(k, 1), :]
            r_row[u, pl.ds(k + 1, 1), :] = through
            through = through * t_one
            fresh = d_row[u, pl.ds(k, 1), :] * added[DSTATE * sub : DSTATE * (sub + 1), :]
            score_scr[b] += fold(s_loc[r, k] * fresh)
            state = t_one * state + fresh
            g_loc[r, k] = state
        return through

    lax.fori_loop(0, count, backward, jnp.ones((1, chans), F32))


def after_chain(
    u, r, b, q, heads, width, count, taps, tok_scr, rm, zc2, qb2,
    wh, wl, vh, vl, pk, yi, s_loc, g_loc, p_row, r_row, d_row, start_scr, later_scr, cv_scr, grad_scr, hd_scr,
    between,
):
    chans = UNIT
    per = chans // width
    base = 4 * heads
    lane_head = iota((chans, LANES), 0) // width + q * per
    col = iota((chans, LANES), 1)
    pick_diff = jnp.where(col == lane_head, 1.0, 0.0).astype(BF16)
    pick_step = jnp.where(col == lane_head + heads, 1.0, 0.0).astype(BF16)
    pick = stack(pick_diff, pick_diff, pick_step, pick_step)
    tokens = count * BLOCK
    for back in range(TAPS):
        cv_scr[back, pl.ds(0, HALO), :] = jnp.zeros((HALO, chans), F32)
        cv_scr[back, pl.ds(HALO + tokens, HALO), :] = jnp.zeros((HALO, chans), F32)
    line = iota((BLOCK, chans), 0)

    def block(blk, carry):
        if between is not None:
            pl.when(blk == count - 1)(between)

        first = pl.multiple_of(blk * BLOCK, BLOCK)
        here = pl.ds(first, BLOCK)
        start = start_scr[u]
        later = later_scr[u]
        w_high, w_low = wh[r, here, :], wl[r, here, :]
        v_high, v_low = vh[r, here, :], vl[r, here, :]
        y_all, d_all, crossed = [], [], []
        state = s_loc[r, 2 * blk] + p_row[u, pl.ds(2 * blk, 1), :] * start
        for sub in range(2):
            k = 2 * blk + sub
            center = d_row[u, pl.ds(k, 1), :]
            rows = pl.ds(sub * CHUNK, CHUNK)
            slope = g_loc[r, k + 1] + r_row[u, pl.ds(k + 1, 1), :] * later
            after = s_loc[r, k + 1] + p_row[u, pl.ds(k + 1, 1), :] * start
            y_all.append(mm(zc2[b, blk, rows, :], stack(*split(center * state))))
            d_all.append(mm(qb2[b, blk, rows, :], stack(*split(center * slope))))
            crossed.append(jnp.sum(after * slope, axis=0, keepdims=True))
            state = after
        y_in = yi[r, here, :] + stack(*y_all)
        d_in = mm(rm[b, blk], stack(v_high, v_high, v_low)) + stack(*d_all)
        read = (v_high.astype(F32) + v_low.astype(F32)) * y_in
        stepped = (w_high.astype(F32) + w_low.astype(F32)) * d_in
        diff = read - stepped
        diff = jnp.where(line == CHUNK - 1, diff + crossed[0], diff)
        diff = jnp.where(line == BLOCK - 1, diff + crossed[1], diff)
        hd_scr[b, here, :] += mm(side(*split(diff), *split(stepped)), pick)
        d_pre = pk[r, here, :] * d_in
        tok = tok_scr[b, here, :]
        below = pl.ds(pl.multiple_of(HALO + blk * BLOCK, HALO), BLOCK)
        cv_scr[0, below, :] = taps[3:4, :] * d_pre
        for back in range(1, TAPS):
            scale = tok[:, base + back - 1 : base + back] * taps[3 - back : 4 - back, :]
            cv_scr[back, below, :] = scale * d_pre
        return carry

    lax.fori_loop(0, count, block, 0)
    for begin, size in [(0, HALO)] + [(HALO + i * BLOCK, BLOCK) for i in range(count)]:
        total = cv_scr[0, pl.ds(begin, size), :]
        for back in range(1, TAPS):
            total = total + cv_scr[back, pl.ds(begin + back, size), :]
        grad_scr[u, pl.ds(begin, size), :] = total


def kernel(
    axes, size, width,
    x_ref, t_ref, b_ref, c_ref, raw_ref, reset_ref, rate_ref, w_ref, label_ref,
    loss_ref, out_ref, slope_ref,
    x_scr, t_scr, b_scr, c_scr, raw_scr, mark_scr, tok_scr, lm, rm, zc2, qb2, bt2, ct2, xe_scr,
    wh, wl, vh, vl, pk, yi, s_loc, g_loc, p_row, r_row, d_row, th_row, chain_out, start_scr, later_scr,
    cv_scr, grad_scr, hd_scr, score_scr, halo_scr, part_scr, slot_scr, out_scr, lean_scr, mark_ref, wide_scr,
    wsent, wgot, wkept, nsent, ngot, nkept, hsent, hgot, msent, mgot, csent, cgot,
    esent, egot, psent, pgot, osent, ogot, rsent, rgot, fsent, fgot,
):
    outer, inner, cores = axes
    units, tokens = t_scr.shape[0], t_scr.shape[1]
    ring = wh.shape[0]
    rows = x_ref.shape[1]
    states, heads = b_scr.shape[2], raw_scr.shape[1]
    per_pair = units // 2
    chans = per_pair * UNIT
    count = tokens // BLOCK
    parts, planes = lax.axis_size(inner), lax.axis_size(outer)
    mine, plane = lax.axis_index(inner), lax.axis_index(outer)
    has_less = plane > 0
    has_more = plane < planes - 1
    gives = has_more & (mine == parts - 1)
    less, more = lax.rem(plane + planes - 1, planes), lax.rem(plane + 1, planes)
    barrier = pltpu.get_barrier_semaphore()
    across, core = lax.axis_size(cores), lax.axis_index(cores)
    mates = [(i, h) for i in range(parts) for h in range(across)][1:]

    def mate(i, h):
        return {inner: lax.rem(mine + i, parts), cores: lax.rem(core + h, across)}

    for i, h in mates:
        greet(barrier, mate(i, h))
    for away in range(1, planes):
        greet(barrier, {outer: lax.rem(plane + away, planes)})
    peers = len(mates) + planes - 1

    @pl.when(has_less)
    def _():
        greet(barrier, {outer: less, inner: parts - 1})

    @pl.when(gives)
    def _():
        for j in range(parts):
            greet(barrier, {outer: more, inner: j})

    pl.semaphore_wait(barrier, peers + has_less.astype(jnp.int32) + parts * gives.astype(jnp.int32))

    for b in range(2):
        mark_ref[b] = jnp.broadcast_to(reset_ref[b : b + 1, :].astype(F32), (8, rows))

    def wide_views(u, source, goal):
        b, q = u // per_pair, lax.rem(u, per_pair)
        wide = pl.ds(pl.multiple_of(goal * chans + q * UNIT, UNIT), UNIT)
        yield x_ref.at[b, :, wide], x_scr.at[u, pl.ds(pl.multiple_of(HALO + source * rows, HALO), rows)]
        yield t_ref.at[b, :, wide], t_scr.at[u, pl.ds(pl.multiple_of(source * rows, HALO), rows)]

    def thin_views(b, source, goal):
        group = pl.ds(pl.multiple_of(goal * states, LANES), states)
        lines = pl.ds(pl.multiple_of(goal * heads, 8), heads)
        here = pl.ds(pl.multiple_of(source * rows, LANES), rows)
        later = pl.ds(pl.multiple_of(rows + source * rows, LANES), rows)
        yield b_ref.at[b, :, group], b_scr.at[b, here]
        yield c_ref.at[b, :, group], c_scr.at[b, here]
        yield raw_ref.at[b, lines], raw_scr.at[b, :, here]
        yield mark_ref.at[b], mark_scr.at[b, :, later]

    def remote(views, index, sent, got):
        for away in range(1, parts):
            goal = lax.rem(mine + away, parts)
            for i, (source, target) in enumerate(views(index, mine, goal)):
                yield send(source, target, sent.at[away, index, i], got.at[away, index, i], {inner: goal})

    def local(views, index, kept):
        for i, (source, target) in enumerate(views(index, mine, mine)):
            yield pltpu.make_async_copy(source, target, kept.at[index, i])

    wides = functools.partial(remote, wide_views, sent=wsent, got=wgot)
    thins = functools.partial(remote, thin_views, sent=nsent, got=ngot)

    def edges(u, j):
        b, q = u // per_pair, lax.rem(u, per_pair)
        wide = pl.ds(pl.multiple_of(j * chans + q * UNIT, UNIT), UNIT)
        return send(
            x_ref.at[b, pl.ds(rows - HALO, HALO), wide], x_scr.at[u, pl.ds(0, HALO)],
            hsent.at[j, u], hgot.at[u], {outer: more, inner: j},
        )

    def edge_marks(j):
        return send(mark_ref, mark_scr.at[:, :, pl.ds(0, rows)], msent.at[j], mgot, {outer: more, inner: j})

    def issue(u):
        for copy in wides(u):
            copy.start()
        for copy in local(wide_views, u, wkept):
            copy.start()

    @pl.when(gives)
    def _():
        for j in range(parts):
            edge_marks(j).start()

    for b in range(2):
        for copy in thins(b):
            copy.start()
        for copy in local(thin_views, b, nkept):
            copy.start()
        if b == 0:
            for u in range(min(AHEAD, units)):
                issue(u)

    @pl.when(gives)
    def _():
        def one(u, carry):
            for j in range(parts):
                edges(u, j).start()
            return carry

        lax.fori_loop(0, units, one, 0)

    @pl.when(has_less)
    def _():
        edge_marks(0).wait_recv()

    @pl.when(jnp.logical_not(has_less))
    def _():
        x_scr[:, pl.ds(0, HALO), :] = jnp.zeros((units, HALO, UNIT), BF16)
        mark_scr[:, :, pl.ds(0, rows)] = jnp.zeros((2, 8, rows), F32)

    score_scr[...] = jnp.zeros_like(score_scr)
    hd_scr[...] = jnp.zeros_like(hd_scr)
    ours = iota((heads, rate_ref.shape[1]), 0) + mine * heads == iota((heads, rate_ref.shape[1]), 1)
    rate = jnp.sum(jnp.where(ours, rate_ref[...], 0.0), axis=1, keepdims=True)
    through_row = pl.ds(2 * count, 1)
    ways = ((s_loc, 2 * count, start_scr, has_less, has_more, more), (g_loc, 0, later_scr, has_more, has_less, less))
    for _, _, arrived, arrives, _, _ in ways:

        @pl.when(jnp.logical_not(arrives))
        def _():
            arrived[...] = jnp.zeros(arrived.shape, F32)

    def piece_rows(piece):
        return pl.ds(piece * (DSTATE // HOPS), DSTATE // HOPS)

    def chain_copy(way, u, piece, arrived, goal):
        lines = piece_rows(piece)
        source, target = chain_out.at[way, u, lines], arrived.at[u, lines]
        return send(source, target, csent.at[way, u, piece], cgot.at[way, u, piece], {outer: goal})

    def edge(u):
        return send(grad_scr.at[u, pl.ds(0, HALO)], halo_scr.at[u], esent.at[u], egot.at[u], {outer: less})

    def taps_of(q):
        return w_ref[:, pl.ds(pl.multiple_of(mine * chans + q * UNIT, UNIT), UNIT)]

    early = early_units(units, parts, planes)

    def early_out(u, away):
        goal = lax.rem(mine + away, parts)
        source = grad_scr.at[u, pl.ds(pl.multiple_of(HALO + goal * rows, HALO), rows)]
        return send(source, wide_scr.at[away, u], fsent.at[away, u], fgot.at[away, u], {inner: goal})

    def close(u):
        @pl.when(has_more)
        def _():
            edge(u).wait_recv()
            grad_scr[u, pl.ds(tokens, HALO), :] += halo_scr[u]

    def score_copy(spot):
        slot = slot_scr.at[mine * across + core]
        return send(part_scr.at[0], slot, psent.at[spot], pgot.at[spot], mate(*mates[spot]))

    base = parts * across

    def far_copy(away):
        goal = lax.rem(plane + away, planes)
        spot = base + away - 1
        return send(part_scr.at[1], slot_scr.at[base + plane], psent.at[spot], pgot.at[spot], {outer: goal})

    def sum_mates():
        for spot in range(len(mates)):
            score_copy(spot).wait_recv()
        subtotal = slot_scr[0]
        for i in range(1, parts * across):
            subtotal = subtotal + slot_scr[i]
        part_scr[1] = subtotal
        slot_scr[base + plane] = subtotal
        for away in range(1, planes):
            far_copy(away).start()

    def post(u, between=None):
        b, q = u // per_pair, lax.rem(u, per_pair)
        after_chain(
            u, lax.rem(u, ring), b, q, heads, width, count, taps_of(q), tok_scr, rm, zc2, qb2,
            wh, wl, vh, vl, pk, yi, s_loc, g_loc, p_row, r_row, d_row, start_scr, later_scr, cv_scr, grad_scr,
            hd_scr, between,
        )

        @pl.when(has_less)
        def _():
            edge(u).start()

    middle = (planes + 1) // 2

    def hop(time, carry):
        for piece, way in [(piece, way) for piece in range(HOPS) for way in range(2)]:
            own, end, arrived, arrives, leaves, goal = ways[way]
            lines = piece_rows(piece)
            u = time - (plane if way == 0 else planes - 1 - plane)

            @pl.when((u >= 0) & (u < units))
            def _():
                copy = chain_copy(way, u, piece, arrived, goal)

                @pl.when(arrives)
                def _():
                    copy.wait_recv()

                    @pl.when(plane < middle if way == 0 else plane >= middle)
                    def _():
                        far = g_loc if way == 0 else s_loc
                        end_now = 0 if way == 0 else 2 * count
                        met = far[lax.rem(u, ring), end_now, lines, :]
                        score_scr[u // per_pair] += fold(arrived[u, lines, :] * met)

                    if way == 0:

                        @pl.when(plane == middle)
                        def _():
                            score_scr[u // per_pair] += fold(arrived[u, lines, :] * chain_out[1, u, lines, :])

                @pl.when(leaves)
                def _():
                    mine_now = own[lax.rem(u, ring), end, lines, :]
                    chain_out[way, u, lines, :] = p_row[u, through_row, :] * arrived[u, lines, :] + mine_now
                    copy.start()

        return carry

    def turn(time, carry):
        @pl.when(time + AHEAD < units)
        def _():
            issue(time + AHEAD)

        @pl.when(time < units)
        def _():
            u = time
            b, q = u // per_pair, lax.rem(u, per_pair)

            @pl.when(q == 0)
            def _():
                for copy in thins(b):
                    copy.wait_recv()
                for copy in local(thin_views, b, nkept):
                    copy.wait()

                def one(blk, carry):
                    prepare(
                        b, blk, heads, rows, raw_scr, mark_scr, rate, b_scr, c_scr, tok_scr, lm, rm, zc2, qb2, bt2, ct2
                    )
                    return carry

                lax.fori_loop(0, count, one, 0)

            for copy in wides(u):
                copy.wait_recv()
            for copy in local(wide_views, u, wkept):
                copy.wait()

            @pl.when(has_less)
            def _():
                edges(u, 0).wait_recv()

            if early > 0:

                @pl.when(u == units - 1)
                def _():
                    def one(i, carry):
                        close(i)
                        for away in range(1, parts):
                            early_out(i, away).start()
                        return carry

                    lax.fori_loop(0, early, one, 0)

            before_chain(
                u, lax.rem(u, ring), b, q, heads, width, count, taps_of(q), x_scr, t_scr, tok_scr, lm, bt2, ct2, xe_scr,
                wh, wl, vh, vl, pk, yi, s_loc, g_loc, p_row, r_row, d_row, th_row, score_scr,
            )

        hop(time, 0)
        u = time - (planes - 1)

        @pl.when((u >= 0) & (time < units))
        def _():
            post(u)

        return carry

    known = min(units + middle, units + planes - 1)
    lax.fori_loop(0, known, turn, 0)
    own = [jnp.sum(jnp.sum(score_scr[i], axis=0, keepdims=True), axis=1, keepdims=True) for i in range(2)]
    part = jnp.where(iota((8, LANES), 0) == 0, own[0], own[1])
    part_scr[0] = part
    slot_scr[mine * across + core] = part
    for spot in range(len(mates)):
        score_copy(spot).start()
    done = max(0, units - planes + 1)
    ready = done + planes - 1 < known
    if not ready:
        lax.fori_loop(known, units + planes - 1, hop, 0)
    if done < units:
        post(jnp.int32(done), sum_mates)
    else:
        sum_mates()
    if ready:
        lax.fori_loop(known, units + planes - 1, hop, 0)
    for away in range(1, planes):
        far_copy(away).wait_recv()
    subtotal = slot_scr[base]
    for i in range(1, planes):
        subtotal = subtotal + slot_scr[base + i]
    row = iota((8, LANES), 0)
    sign = jnp.where(row == label_ref[0], 1.0, jnp.where(row < 2, -1.0, 0.0)).astype(F32)
    signed = subtotal * sign / math.sqrt(size)
    margin = signed[0:1, :] + signed[1:2, :]
    loss_ref[0, 0] = jax.nn.softplus(-margin)[0, 0]
    factors = -jax.nn.sigmoid(-margin) * sign
    scale = [factors[b : b + 1, 0:1] for b in range(2)]

    def out_view(u, owner):
        b, q = u // per_pair, lax.rem(u, per_pair)
        return out_ref.at[b, :, pl.ds(pl.multiple_of(owner * chans + q * UNIT, UNIT), UNIT)]

    def wide_out(u, away):
        goal = lax.rem(mine + away, parts)
        return send(out_scr.at[away, u], out_view(u, mine), osent.at[away, u], ogot.at[away, u], {inner: goal})

    lines = pl.ds(pl.multiple_of(mine * heads, 8), heads)

    def thin_out(away):
        goal = lax.rem(mine + away, parts)
        return send(out_lean(away), slope_ref.at[:, lines], rsent.at[away], rgot.at[away], {inner: goal})

    def out_lean(away):
        goal = lax.rem(mine + away, parts)
        return lean_scr.at[:, :, pl.ds(pl.multiple_of(goal * rows, LANES), rows)]

    def factor_of(u):
        return jnp.where(u // per_pair == 0, scale[0], scale[1])

    def block_of(u, away):
        goal = lax.rem(mine + away, parts)
        return grad_scr[u, pl.ds(pl.multiple_of(HALO + goal * rows, HALO), rows), :]

    def give(u, carry):
        close(u)
        for away in range(1, parts):
            out_scr[away, u] = (factor_of(u) * block_of(u, away)).astype(BF16)
            wide_out(u, away).start()
        return carry

    def late(u, carry):
        post(u)
        give(u - 1, 0)
        return carry

    lax.fori_loop(early, done, give, 0)
    if done < units:
        lax.fori_loop(done + 1, units, late, 0)
        give(jnp.int32(units - 1), 0)
    back_row = iota((BLOCK, BLOCK), 0)
    back_col = iota((BLOCK, BLOCK), 1)
    near = (back_row // CHUNK) == (back_col // CHUNK)
    onward = jnp.where(near & (back_row >= back_col), 1.0, 0.0).astype(BF16)
    for b in range(2):
        for blk in range(count):
            here = pl.ds(blk * BLOCK, BLOCK)
            sums = hd_scr[b, here, :].T
            raw = raw_scr[b, :, here]
            d_log = mm_three(sums[0:heads], onward)
            by_step = sums[heads : 2 * heads] / jax.nn.softplus(raw)
            lean_scr[b, :, here] = scale[b] * jax.nn.sigmoid(raw) * (by_step - rate * d_log)
    for away in range(1, parts):
        thin_out(away).start()
    slope_ref[:, lines, :] = lean_scr[:, :, pl.ds(pl.multiple_of(mine * rows, LANES), rows)]

    def keep_own(u, carry):
        out_view(u, mine)[...] = (factor_of(u) * block_of(u, 0)).astype(BF16)
        return carry

    lax.fori_loop(0, units, keep_own, 0)

    def take(u, carry):
        for away in range(1, parts):
            early_out(u, away).wait_recv()
            owner = lax.rem(mine + parts - away, parts)
            out_view(u, owner)[...] = (factor_of(u) * wide_scr[away, u]).astype(BF16)
        return carry

    if early > 0:
        lax.fori_loop(0, early, take, 0)

    def drain(u, carry):
        for copy in wides(u):
            copy.wait_send()
        for way, (_, _, arrived, _, leaves, goal) in enumerate(ways):

            @pl.when(leaves)
            def _():
                for piece in range(HOPS):
                    chain_copy(way, u, piece, arrived, goal).wait_send()

        @pl.when(has_less)
        def _():
            edge(u).wait_send()

        @pl.when(gives)
        def _():
            for j in range(parts):
                edges(u, j).wait_send()

        return carry

    lax.fori_loop(0, units, drain, 0)

    def drain_early(u, carry):
        for away in range(1, parts):
            early_out(u, away).wait_send()
        return carry

    def drain_late(u, carry):
        for away in range(1, parts):
            wide_out(u, away).wait()
        return carry

    if early > 0:
        lax.fori_loop(0, early, drain_early, 0)
    lax.fori_loop(early, units, drain_late, 0)
    for spot in range(len(mates)):
        score_copy(spot).wait_send()
    for away in range(1, parts):
        thin_out(away).wait()
    for b in range(2):
        for copy in thins(b):
            copy.wait_send()
    for away in range(1, planes):
        far_copy(away).wait_send()

    @pl.when(gives)
    def _():
        for j in range(parts):
            edge_marks(j).wait_send()


def early_units(units, parts, planes):
    return max(0, min(EARLY, units - planes)) if parts > 1 else 0


def everything(x_in, target, b_in, c_in, dt_raw, resets, rate, conv_w, label, axes, size, width):
    parts = lax.axis_size(axes[1])
    rows = x_in.shape[1]
    tokens = parts * rows
    chans, states, heads = x_in.shape[2] // parts, b_in.shape[2] // parts, dt_raw.shape[1] // parts
    units = 2 * (chans // UNIT)
    count = tokens // BLOCK
    edge = 2 * count + 8
    planes = lax.axis_size(axes[0])
    ring = min(units, planes)
    slots = planes + parts * lax.axis_size(axes[2])
    early = max(1, early_units(units, parts, planes))
    vmem = pl.BlockSpec(memory_space=pltpu.VMEM)
    dma = pltpu.SemaphoreType.DMA

    def v(shape, kind=F32):
        return pltpu.VMEM(shape, kind)

    return pl.pallas_call(
        functools.partial(kernel, axes, size, width),
        out_shape=(
            jax.ShapeDtypeStruct((1, 1), F32),
            jax.ShapeDtypeStruct(x_in.shape, BF16),
            jax.ShapeDtypeStruct(dt_raw.shape, F32),
        ),
        in_specs=[pl.BlockSpec(memory_space=pl.ANY)] * 5 + [vmem] * 3 + [pl.BlockSpec(memory_space=pltpu.SMEM)],
        out_specs=(pl.BlockSpec(memory_space=pltpu.SMEM), vmem, vmem),
        scratch_shapes=[
            v((units, tokens + HALO, UNIT), BF16),
            v((units, tokens, UNIT), BF16),
            v((2, tokens, states), BF16),
            v((2, tokens, states), BF16),
            v((2, heads, tokens)),
            v((2, 8, rows + tokens)),
            v((2, tokens, LANES)),
            v((2, count, BLOCK, 3 * BLOCK), BF16),
            v((2, count, BLOCK, 3 * BLOCK), BF16),
            v((2, count, BLOCK, 2 * DSTATE), BF16),
            v((2, count, BLOCK, 2 * DSTATE), BF16),
            v((2, count, 2 * DSTATE, 2 * BLOCK), BF16),
            v((2, count, 2 * DSTATE, 2 * BLOCK), BF16),
            v((BLOCK + HALO, UNIT)),
            v((ring, tokens, UNIT), BF16),
            v((ring, tokens, UNIT), BF16),
            v((ring, tokens, UNIT), BF16),
            v((ring, tokens, UNIT), BF16),
            v((ring, tokens, UNIT)),
            v((ring, tokens, UNIT)),
            v((ring, 2 * count + 1, DSTATE, UNIT)),
            v((ring, 2 * count + 1, DSTATE, UNIT)),
            v((units, edge, UNIT)),
            v((units, edge, UNIT)),
            v((units, edge, UNIT)),
            v((units, edge, UNIT)),
            v((2, units, DSTATE, UNIT)),
            v((units, DSTATE, UNIT)),
            v((units, DSTATE, UNIT)),
            v((TAPS, tokens + 2 * HALO, UNIT)),
            v((units, tokens + HALO, UNIT)),
            v((2, tokens, LANES)),
            v((2, 8, UNIT)),
            v((units, HALO, UNIT)),
            v((2, 8, LANES)),
            v((slots, 8, LANES)),
            v((parts, units, rows, UNIT), BF16),
            v((2, heads, tokens)),
            v((2, 8, rows)),
            v((parts, early, rows, UNIT)),
            dma((parts, units, 2)),
            dma((parts, units, 2)),
            dma((units, 2)),
            dma((parts, 2, 4)),
            dma((parts, 2, 4)),
            dma((2, 4)),
            dma((parts, units)),
            dma((units,)),
            dma((parts,)),
            dma,
            dma((2, units, HOPS)),
            dma((2, units, HOPS)),
            dma((units,)),
            dma((units,)),
            dma((slots,)),
            dma((slots,)),
            dma((parts, units)),
            dma((parts, units)),
            dma((parts,)),
            dma((parts,)),
            dma((parts, early)),
            dma((parts, early)),
        ],
        compiler_params=pltpu.CompilerParams(
            collective_id=0, has_side_effects=True, vmem_limit_bytes=60 * 1024 * 1024
        ),
        name="everything",
    )(x_in, target, b_in, c_in, dt_raw, resets, rate, conv_w, label)


def body(outer, inner, x_in, target, b_in, c_in, dt_raw, resets, decay_rate, conv_w, label):
    rows = x_in.shape[1]
    width = x_in.shape[2] // dt_raw.shape[1]
    size = rows * lax.axis_size(outer) * lax.axis_size(inner) * x_in.shape[2] * lax.axis_size("head")
    axes = (outer, inner, "head")
    loss, grad, slope = everything(
        x_in, target, b_in, c_in, dt_raw, resets, decay_rate[None], conv_w, label, axes, size, width
    )
    return (loss[0, 0], grad, slope)


def solution(mesh):
    def program(*arrays):
        ways, across = mesh.shape["seq"], mesh.shape["head"]
        groups = arrays[2].shape[2] // DSTATE // across
        parts = math.gcd(groups, ways)
        devices = mesh.devices.reshape(ways // parts, parts, across)
        finer = Mesh(devices, ("outer", "inner", "head"))
        seq = ("outer", "inner")
        in_specs = (
            P(None, seq, "head"),
            P(None, seq, "head"),
            P(None, seq, "head"),
            P(None, seq, "head"),
            P(None, "head", seq),
            P(None, seq),
            P("head"),
            P(None, "head"),
            P(),
        )
        out_specs = (P(), P(None, seq, "head"), P(None, "head", seq))
        inner = functools.partial(body, "outer", "inner")
        mapped = jax.shard_map(inner, mesh=finer, in_specs=in_specs, out_specs=out_specs, check_vma=False)
        return mapped(*arrays)

    return program
```

```python
import functools
import math

import jax
import jax.numpy as jnp
from jax import lax
from jax.experimental import pallas as pl
from jax.experimental.pallas import tpu as pltpu
from jax.sharding import Mesh
from jax.sharding import PartitionSpec as P

DSTATE = 128
BLOCK = 128
CHUNK = 64
LANES = 128
TAPS = 4
HALO = 16
UNIT = 256
AHEAD = 2
EARLY = 3
HOPS = 1
F32 = jnp.float32
BF16 = jnp.bfloat16


def split(value):
    high = value.astype(BF16)
    low = (value - high.astype(F32)).astype(BF16)
    return high, low


def mm(left, right):
    return lax.dot_general(left, right, (((1,), (0,)), ((), ())), preferred_element_type=F32)


def mm_across(left, right):
    return lax.dot_general(left, right, (((1,), (1,)), ((), ())), preferred_element_type=F32)


def mm_three(left, right):
    high = left.astype(BF16)
    rest = left - high.astype(F32)
    low, least = split(rest)
    return mm(high, right) + mm(low, right) + mm(least, right)


def iota(shape, dim):
    return lax.broadcasted_iota(jnp.int32, shape, dim)


def side(*parts):
    return jnp.concatenate(parts, axis=1)


def stack(*parts):
    return jnp.concatenate(parts, axis=0)


def send(source, goal, sent, got, where):
    return pltpu.make_async_remote_copy(
        src_ref=source,
        dst_ref=goal,
        send_sem=sent,
        recv_sem=got,
        device_id=where,
        device_id_type=pl.DeviceIdType.MESH,
    )


def greet(barrier, where):
    pl.semaphore_signal(barrier, inc=1, device_id=where, device_id_type=pl.DeviceIdType.MESH)


def fold(value):
    return jnp.sum(value.reshape(value.shape[0] // 8, 8, value.shape[1]), axis=0)


def prepare(b, blk, heads, rows, raw_scr, mark_scr, rate, b_scr, c_scr, tok_scr, lm, rm, zc2, qb2, bt2, ct2):
    here = pl.ds(pl.multiple_of(blk * BLOCK, BLOCK), BLOCK)
    later = pl.ds(pl.multiple_of(rows + blk * BLOCK, BLOCK), BLOCK)
    before = pl.ds(pl.multiple_of(rows - BLOCK + blk * BLOCK, BLOCK), BLOCK)
    steps = jax.nn.softplus(raw_scr[b, :, here])
    logs = -steps * rate
    marks = mark_scr[b, :, later]
    keep = 1.0 - side(mark_scr[b, :, before], marks)
    keep_one = keep[:, BLOCK:]
    keep_two = keep_one * pltpu.roll(keep, 1, 1)[:, BLOCK:]
    keep_three = keep_two * pltpu.roll(keep, 2, 1)[:, BLOCK:]
    row = iota((BLOCK, BLOCK), 0)
    col = iota((BLOCK, BLOCK), 1)
    near = (row // CHUNK) == (col // CHUNK)
    upto = jnp.where(near & (row <= col), 1.0, 0.0).astype(BF16)
    full = jnp.where(near, 1.0, 0.0).astype(BF16)
    running = mm_three(logs, upto)
    total = mm_three(logs, full)
    seen = mm(marks.astype(BF16), upto)
    seen_all = mm(marks.astype(BF16), full)
    half = 0.5 * total
    grow = steps * jnp.exp(half - running)
    fall = jnp.exp(running - half)
    center = jnp.exp(half)
    open_all = jnp.where(seen_all == 0.0, 1.0, 0.0).astype(F32)
    through = jnp.exp(total) * open_all[0:1]
    opened = jnp.where(seen == 0.0, 1.0, 0.0).astype(F32)
    closing = jnp.where(seen == seen_all, 1.0, 0.0).astype(F32)
    line = iota((8, BLOCK), 0)
    extra = jnp.zeros((8, BLOCK), F32)
    for i, value in enumerate((keep_one, keep_two, keep_three, seen, opened, closing)):
        extra = jnp.where(line == i, value, extra)
    table = stack(grow, fall, center, through, extra, jnp.zeros((LANES - 4 * heads - 8, BLOCK), F32))
    tok = table.T
    tok_scr[b, here, :] = tok
    base = 4 * heads
    b_rows = b_scr[b, here, :]
    c_rows = c_scr[b, here, :]
    scores = mm_across(c_rows, b_rows)
    scores_t = mm_across(b_rows, c_rows)
    same = near & (tok[:, base + 3 : base + 4] == seen[0:1, :])
    m_high, m_low = split(jnp.where(same & (row >= col), scores, 0.0))
    n_high, n_low = split(jnp.where(same & (row <= col), scores_t, 0.0))
    lm[b, blk] = side(m_high, m_low, m_high)
    rm[b, blk] = side(n_high, n_low, n_high)
    for value, mask, twice, turned in ((c_rows, base + 4, zc2, ct2), (b_rows, base + 5, qb2, bt2)):
        masked = value.astype(F32) * tok[:, mask : mask + 1]
        short = masked.astype(BF16)
        twice[b, blk] = side(short, short)
        flipped = masked.T
        lane = iota((DSTATE, BLOCK), 1)
        one = jnp.where(lane < CHUNK, flipped, 0.0).astype(BF16)
        two = jnp.where(lane >= CHUNK, flipped, 0.0).astype(BF16)
        turned[b, blk] = stack(side(one, one), side(two, two))


def before_chain(
    u, r, b, q, heads, width, count, taps, x_scr, t_scr, tok_scr, lm, bt2, ct2, xe_scr,
    wh, wl, vh, vl, pk, yi, s_loc, g_loc, p_row, r_row, d_row, th_row, score_scr,
):
    chans = UNIT
    per = chans // width
    row = iota((LANES, chans), 0)
    head = iota((LANES, chans), 1) // width + q * per

    def spread(offset):
        one = jnp.where(row == head + offset, 1.0, 0.0).astype(BF16)
        return stack(one, one)

    spread_grow, spread_fall = spread(0), spread(heads)
    spread_center, spread_through = spread(2 * heads), spread(3 * heads)
    base = 4 * heads
    s_loc[r, 0] = jnp.zeros((DSTATE, chans), F32)
    g_loc[r, 2 * count] = jnp.zeros((DSTATE, chans), F32)

    def forward(blk, through):
        first = pl.multiple_of(blk * BLOCK, BLOCK)
        here = pl.ds(first, BLOCK)
        tok = tok_scr[b, here, :]
        both = side(*split(tok))
        ends = stack(both[0:16], both[CHUNK : CHUNK + 16])
        grow = mm(both, spread_grow)
        fall = mm(both, spread_fall)
        center = mm(ends, spread_center)
        pass_by = mm(ends, spread_through)
        xe_scr[...] = x_scr[u, pl.ds(first, BLOCK + HALO), :].astype(F32)
        pre = taps[3:4, :] * xe_scr[pl.ds(HALO, BLOCK), :]
        for back in range(1, TAPS):
            scale = tok[:, base + back - 1 : base + back] * taps[3 - back : 4 - back, :]
            pre = pre + scale * xe_scr[pl.ds(HALO - back, BLOCK), :]
        sig = jax.nn.sigmoid(pre)
        values = pre * sig
        slope = sig + values * (1.0 - sig)
        w_high, w_low = split(grow * values)
        v = fall * t_scr[u, here, :].astype(F32)
        v_high, v_low = split(v)
        wh[r, here, :] = w_high
        wl[r, here, :] = w_low
        vh[r, here, :] = v_high
        vl[r, here, :] = v_low
        pk[r, here, :] = grow * slope
        inside = mm(lm[b, blk], stack(w_high, w_high, w_low))
        yi[r, here, :] = inside
        score_scr[b] += fold(v * inside)
        added = mm(bt2[b, blk], stack(w_high, w_low))
        state = s_loc[r, 2 * blk]
        for sub in range(2):
            k = 2 * blk + sub
            c_one = center[16 * sub : 16 * sub + 1, :]
            t_one = pass_by[16 * sub : 16 * sub + 1, :]
            p_row[u, pl.ds(k, 1), :] = through
            d_row[u, pl.ds(k, 1), :] = c_one
            th_row[u, pl.ds(k, 1), :] = t_one
            through = through * t_one
            state = t_one * state + c_one * added[DSTATE * sub : DSTATE * (sub + 1), :]
            s_loc[r, k + 1] = state
        return through

    through = lax.fori_loop(0, count, forward, jnp.ones((1, chans), F32))
    p_row[u, 2 * count : 2 * count + 1, :] = through

    def backward(step, through):
        blk = count - 1 - step
        here = pl.ds(pl.multiple_of(blk * BLOCK, BLOCK), BLOCK)
        added = mm(ct2[b, blk], stack(vh[r, here, :], vl[r, here, :]))
        state = g_loc[r, 2 * blk + 2]
        for sub in (1, 0):
            k = 2 * blk + sub
            t_one = th_row[u, pl.ds(k, 1), :]
            r_row[u, pl.ds(k + 1, 1), :] = through
            through = through * t_one
            fresh = d_row[u, pl.ds(k, 1), :] * added[DSTATE * sub : DSTATE * (sub + 1), :]
            score_scr[b] += fold(s_loc[r, k] * fresh)
            state = t_one * state + fresh
            g_loc[r, k] = state
        return through

    lax.fori_loop(0, count, backward, jnp.ones((1, chans), F32))


def after_chain(
    u, r, b, q, heads, width, count, taps, tok_scr, rm, zc2, qb2,
    wh, wl, vh, vl, pk, yi, s_loc, g_loc, p_row, r_row, d_row, start_scr, later_scr, cv_scr, grad_scr, hd_scr,
    between,
):
    chans = UNIT
    per = chans // width
    base = 4 * heads
    lane_head = iota((chans, LANES), 0) // width + q * per
    col = iota((chans, LANES), 1)
    pick_diff = jnp.where(col == lane_head, 1.0, 0.0).astype(BF16)
    pick_step = jnp.where(col == lane_head + heads, 1.0, 0.0).astype(BF16)
    pick = stack(pick_diff, pick_diff, pick_step, pick_step)
    tokens = count * BLOCK
    for back in range(TAPS):
        cv_scr[back, pl.ds(0, HALO), :] = jnp.zeros((HALO, chans), F32)
        cv_scr[back, pl.ds(HALO + tokens, HALO), :] = jnp.zeros((HALO, chans), F32)
    line = iota((BLOCK, chans), 0)

    def block(blk, carry):
        if between is not None:
            pl.when(blk == count - 1)(between)

        first = pl.multiple_of(blk * BLOCK, BLOCK)
        here = pl.ds(first, BLOCK)
        start = start_scr[u]
        later = later_scr[u]
        w_high, w_low = wh[r, here, :], wl[r, here, :]
        v_high, v_low = vh[r, here, :], vl[r, here, :]
        y_all, d_all, crossed = [], [], []
        state = s_loc[r, 2 * blk] + p_row[u, pl.ds(2 * blk, 1), :] * start
        for sub in range(2):
            k = 2 * blk + sub
            center = d_row[u, pl.ds(k, 1), :]
            rows = pl.ds(sub * CHUNK, CHUNK)
            slope = g_loc[r, k + 1] + r_row[u, pl.ds(k + 1, 1), :] * later
            after = s_loc[r, k + 1] + p_row[u, pl.ds(k + 1, 1), :] * start
            y_all.append(mm(zc2[b, blk, rows, :], stack(*split(center * state))))
            d_all.append(mm(qb2[b, blk, rows, :], stack(*split(center * slope))))
            crossed.append(jnp.sum(after * slope, axis=0, keepdims=True))
            state = after
        y_in = yi[r, here, :] + stack(*y_all)
        d_in = mm(rm[b, blk], stack(v_high, v_high, v_low)) + stack(*d_all)
        read = (v_high.astype(F32) + v_low.astype(F32)) * y_in
        stepped = (w_high.astype(F32) + w_low.astype(F32)) * d_in
        diff = read - stepped
        diff = jnp.where(line == CHUNK - 1, diff + crossed[0], diff)
        diff = jnp.where(line == BLOCK - 1, diff + crossed[1], diff)
        hd_scr[b, here, :] += mm(side(*split(diff), *split(stepped)), pick)
        d_pre = pk[r, here, :] * d_in
        tok = tok_scr[b, here, :]
        below = pl.ds(pl.multiple_of(HALO + blk * BLOCK, HALO), BLOCK)
        cv_scr[0, below, :] = taps[3:4, :] * d_pre
        for back in range(1, TAPS):
            scale = tok[:, base + back - 1 : base + back] * taps[3 - back : 4 - back, :]
            cv_scr[back, below, :] = scale * d_pre
        return carry

    lax.fori_loop(0, count, block, 0)
    for begin, size in [(0, HALO)] + [(HALO + i * BLOCK, BLOCK) for i in range(count)]:
        total = cv_scr[0, pl.ds(begin, size), :]
        for back in range(1, TAPS):
            total = total + cv_scr[back, pl.ds(begin + back, size), :]
        grad_scr[u, pl.ds(begin, size), :] = total


def kernel(
    axes, size, width,
    x_ref, t_ref, b_ref, c_ref, raw_ref, reset_ref, rate_ref, w_ref, label_ref,
    loss_ref, out_ref, slope_ref,
    x_scr, t_scr, b_scr, c_scr, raw_scr, mark_scr, tok_scr, lm, rm, zc2, qb2, bt2, ct2, xe_scr,
    wh, wl, vh, vl, pk, yi, s_loc, g_loc, p_row, r_row, d_row, th_row, chain_out, start_scr, later_scr,
    cv_scr, grad_scr, hd_scr, score_scr, halo_scr, part_scr, slot_scr, out_scr, lean_scr, mark_ref, wide_scr, take_scr,
    wsent, wgot, wkept, nsent, ngot, nkept, hsent, hgot, msent, mgot, csent, cgot,
    esent, egot, psent, pgot, osent, ogot, rsent, rgot, fsent, fgot, stored,
):
    outer, inner, cores = axes
    units, tokens = t_scr.shape[0], t_scr.shape[1]
    ring = wh.shape[0]
    rows = x_ref.shape[1]
    states, heads = b_scr.shape[2], raw_scr.shape[1]
    per_pair = units // 2
    chans = per_pair * UNIT
    count = tokens // BLOCK
    parts, planes = lax.axis_size(inner), lax.axis_size(outer)
    mine, plane = lax.axis_index(inner), lax.axis_index(outer)
    has_less = plane > 0
    has_more = plane < planes - 1
    gives = has_more & (mine == parts - 1)
    less, more = lax.rem(plane + planes - 1, planes), lax.rem(plane + 1, planes)
    barrier = pltpu.get_barrier_semaphore()
    across, core = lax.axis_size(cores), lax.axis_index(cores)
    mates = [(i, h) for i in range(parts) for h in range(across)][1:]

    def mate(i, h):
        return {inner: lax.rem(mine + i, parts), cores: lax.rem(core + h, across)}

    for i, h in mates:
        greet(barrier, mate(i, h))
    for away in range(1, planes):
        greet(barrier, {outer: lax.rem(plane + away, planes)})
    peers = len(mates) + planes - 1

    @pl.when(has_less)
    def _():
        greet(barrier, {outer: less, inner: parts - 1})

    @pl.when(gives)
    def _():
        for j in range(parts):
            greet(barrier, {outer: more, inner: j})

    pl.semaphore_wait(barrier, peers + has_less.astype(jnp.int32) + parts * gives.astype(jnp.int32))

    for b in range(2):
        mark_ref[b] = jnp.broadcast_to(reset_ref[b : b + 1, :].astype(F32), (8, rows))

    def wide_views(u, source, goal):
        b, q = u // per_pair, lax.rem(u, per_pair)
        wide = pl.ds(pl.multiple_of(goal * chans + q * UNIT, UNIT), UNIT)
        yield x_ref.at[b, :, wide], x_scr.at[u, pl.ds(pl.multiple_of(HALO + source * rows, HALO), rows)]
        yield t_ref.at[b, :, wide], t_scr.at[u, pl.ds(pl.multiple_of(source * rows, HALO), rows)]

    def thin_views(b, source, goal):
        group = pl.ds(pl.multiple_of(goal * states, LANES), states)
        lines = pl.ds(pl.multiple_of(goal * heads, 8), heads)
        here = pl.ds(pl.multiple_of(source * rows, LANES), rows)
        later = pl.ds(pl.multiple_of(rows + source * rows, LANES), rows)
        yield b_ref.at[b, :, group], b_scr.at[b, here]
        yield c_ref.at[b, :, group], c_scr.at[b, here]
        yield raw_ref.at[b, lines], raw_scr.at[b, :, here]
        yield mark_ref.at[b], mark_scr.at[b, :, later]

    def remote(views, index, sent, got):
        for away in range(1, parts):
            goal = lax.rem(mine + away, parts)
            for i, (source, target) in enumerate(views(index, mine, goal)):
                yield send(source, target, sent.at[away, index, i], got.at[away, index, i], {inner: goal})

    def local(views, index, kept):
        for i, (source, target) in enumerate(views(index, mine, mine)):
            yield pltpu.make_async_copy(source, target, kept.at[index, i])

    wides = functools.partial(remote, wide_views, sent=wsent, got=wgot)
    thins = functools.partial(remote, thin_views, sent=nsent, got=ngot)

    def edges(u, j):
        b, q = u // per_pair, lax.rem(u, per_pair)
        wide = pl.ds(pl.multiple_of(j * chans + q * UNIT, UNIT), UNIT)
        return send(
            x_ref.at[b, pl.ds(rows - HALO, HALO), wide], x_scr.at[u, pl.ds(0, HALO)],
            hsent.at[j, u], hgot.at[u], {outer: more, inner: j},
        )

    def edge_marks(j):
        return send(mark_ref, mark_scr.at[:, :, pl.ds(0, rows)], msent.at[j], mgot, {outer: more, inner: j})

    def issue(u):
        for copy in wides(u):
            copy.start()
        for copy in local(wide_views, u, wkept):
            copy.start()

    @pl.when(gives)
    def _():
        for j in range(parts):
            edge_marks(j).start()

    for b in range(2):
        for copy in thins(b):
            copy.start()
        for copy in local(thin_views, b, nkept):
            copy.start()
        if b == 0:
            for u in range(min(AHEAD, units)):
                issue(u)

    @pl.when(gives)
    def _():
        def one(u, carry):
            for j in range(parts):
                edges(u, j).start()
            return carry

        lax.fori_loop(0, units, one, 0)

    @pl.when(has_less)
    def _():
        edge_marks(0).wait_recv()

    @pl.when(jnp.logical_not(has_less))
    def _():
        x_scr[:, pl.ds(0, HALO), :] = jnp.zeros((units, HALO, UNIT), BF16)
        mark_scr[:, :, pl.ds(0, rows)] = jnp.zeros((2, 8, rows), F32)

    score_scr[...] = jnp.zeros_like(score_scr)
    hd_scr[...] = jnp.zeros_like(hd_scr)
    ours = iota((heads, rate_ref.shape[1]), 0) + mine * heads == iota((heads, rate_ref.shape[1]), 1)
    rate = jnp.sum(jnp.where(ours, rate_ref[...], 0.0), axis=1, keepdims=True)
    through_row = pl.ds(2 * count, 1)
    ways = ((s_loc, 2 * count, start_scr, has_less, has_more, more), (g_loc, 0, later_scr, has_more, has_less, less))
    for _, _, arrived, arrives, _, _ in ways:

        @pl.when(jnp.logical_not(arrives))
        def _():
            arrived[...] = jnp.zeros(arrived.shape, F32)

    def piece_rows(piece):
        return pl.ds(piece * (DSTATE // HOPS), DSTATE // HOPS)

    def chain_copy(way, u, piece, arrived, goal):
        lines = piece_rows(piece)
        source, target = chain_out.at[way, u, lines], arrived.at[u, lines]
        return send(source, target, csent.at[way, u, piece], cgot.at[way, u, piece], {outer: goal})

    def edge(u):
        return send(grad_scr.at[u, pl.ds(0, HALO)], halo_scr.at[u], esent.at[u], egot.at[u], {outer: less})

    def taps_of(q):
        return w_ref[:, pl.ds(pl.multiple_of(mine * chans + q * UNIT, UNIT), UNIT)]

    early = early_units(units, parts, planes)

    def early_out(u, away):
        goal = lax.rem(mine + away, parts)
        source = grad_scr.at[u, pl.ds(pl.multiple_of(HALO + goal * rows, HALO), rows)]
        return send(source, wide_scr.at[away, u], fsent.at[away, u], fgot.at[away, u], {inner: goal})

    def close(u):
        @pl.when(has_more)
        def _():
            edge(u).wait_recv()
            grad_scr[u, pl.ds(tokens, HALO), :] += halo_scr[u]

    def score_copy(spot):
        slot = slot_scr.at[mine * across + core]
        return send(part_scr.at[0], slot, psent.at[spot], pgot.at[spot], mate(*mates[spot]))

    base = parts * across

    def far_copy(away):
        goal = lax.rem(plane + away, planes)
        spot = base + away - 1
        return send(part_scr.at[1], slot_scr.at[base + plane], psent.at[spot], pgot.at[spot], {outer: goal})

    def sum_mates():
        for spot in range(len(mates)):
            score_copy(spot).wait_recv()
        subtotal = slot_scr[0]
        for i in range(1, parts * across):
            subtotal = subtotal + slot_scr[i]
        part_scr[1] = subtotal
        slot_scr[base + plane] = subtotal
        for away in range(1, planes):
            far_copy(away).start()

    def post(u, between=None):
        b, q = u // per_pair, lax.rem(u, per_pair)
        after_chain(
            u, lax.rem(u, ring), b, q, heads, width, count, taps_of(q), tok_scr, rm, zc2, qb2,
            wh, wl, vh, vl, pk, yi, s_loc, g_loc, p_row, r_row, d_row, start_scr, later_scr, cv_scr, grad_scr,
            hd_scr, between,
        )

        @pl.when(has_less)
        def _():
            edge(u).start()

    middle = (planes + 1) // 2

    def hop(time, carry):
        for piece, way in [(piece, way) for piece in range(HOPS) for way in range(2)]:
            own, end, arrived, arrives, leaves, goal = ways[way]
            lines = piece_rows(piece)
            u = time - (plane if way == 0 else planes - 1 - plane)

            @pl.when((u >= 0) & (u < units))
            def _():
                copy = chain_copy(way, u, piece, arrived, goal)

                @pl.when(arrives)
                def _():
                    copy.wait_recv()

                    @pl.when(plane < middle if way == 0 else plane >= middle)
                    def _():
                        far = g_loc if way == 0 else s_loc
                        end_now = 0 if way == 0 else 2 * count
                        met = far[lax.rem(u, ring), end_now, lines, :]
                        score_scr[u // per_pair] += fold(arrived[u, lines, :] * met)

                    if way == 0:

                        @pl.when(plane == middle)
                        def _():
                            score_scr[u // per_pair] += fold(arrived[u, lines, :] * chain_out[1, u, lines, :])

                @pl.when(leaves)
                def _():
                    mine_now = own[lax.rem(u, ring), end, lines, :]
                    chain_out[way, u, lines, :] = p_row[u, through_row, :] * arrived[u, lines, :] + mine_now
                    copy.start()

        return carry

    def turn(time, carry):
        @pl.when(time + AHEAD < units)
        def _():
            issue(time + AHEAD)

        @pl.when(time < units)
        def _():
            u = time
            b, q = u // per_pair, lax.rem(u, per_pair)

            @pl.when(q == 0)
            def _():
                for copy in thins(b):
                    copy.wait_recv()
                for copy in local(thin_views, b, nkept):
                    copy.wait()

                def one(blk, carry):
                    prepare(
                        b, blk, heads, rows, raw_scr, mark_scr, rate, b_scr, c_scr, tok_scr, lm, rm, zc2, qb2, bt2, ct2
                    )
                    return carry

                lax.fori_loop(0, count, one, 0)

            for copy in wides(u):
                copy.wait_recv()
            for copy in local(wide_views, u, wkept):
                copy.wait()

            @pl.when(has_less)
            def _():
                edges(u, 0).wait_recv()

            if early > 0:

                @pl.when(u == units - 1)
                def _():
                    def one(i, carry):
                        close(i)
                        for away in range(1, parts):
                            early_out(i, away).start()
                        return carry

                    lax.fori_loop(0, early, one, 0)

            before_chain(
                u, lax.rem(u, ring), b, q, heads, width, count, taps_of(q), x_scr, t_scr, tok_scr, lm, bt2, ct2, xe_scr,
                wh, wl, vh, vl, pk, yi, s_loc, g_loc, p_row, r_row, d_row, th_row, score_scr,
            )

        hop(time, 0)
        u = time - (planes - 1)

        @pl.when((u >= 0) & (time < units))
        def _():
            post(u)

        return carry

    known = min(units + middle, units + planes - 1)
    lax.fori_loop(0, known, turn, 0)
    own = [jnp.sum(jnp.sum(score_scr[i], axis=0, keepdims=True), axis=1, keepdims=True) for i in range(2)]
    part = jnp.where(iota((8, LANES), 0) == 0, own[0], own[1])
    part_scr[0] = part
    slot_scr[mine * across + core] = part
    for spot in range(len(mates)):
        score_copy(spot).start()
    done = max(0, units - planes + 1)
    ready = done + planes - 1 < known
    if not ready:
        lax.fori_loop(known, units + planes - 1, hop, 0)
    if done < units:
        post(jnp.int32(done), sum_mates)
    else:
        sum_mates()
    if ready:
        lax.fori_loop(known, units + planes - 1, hop, 0)
    for away in range(1, planes):
        far_copy(away).wait_recv()
    subtotal = slot_scr[base]
    for i in range(1, planes):
        subtotal = subtotal + slot_scr[base + i]
    row = iota((8, LANES), 0)
    sign = jnp.where(row == label_ref[0], 1.0, jnp.where(row < 2, -1.0, 0.0)).astype(F32)
    signed = subtotal * sign / math.sqrt(size)
    margin = signed[0:1, :] + signed[1:2, :]
    loss_ref[0, 0] = jax.nn.softplus(-margin)[0, 0]
    factors = -jax.nn.sigmoid(-margin) * sign
    scale = [factors[b : b + 1, 0:1] for b in range(2)]

    def out_view(u, owner):
        b, q = u // per_pair, lax.rem(u, per_pair)
        return out_ref.at[b, :, pl.ds(pl.multiple_of(owner * chans + q * UNIT, UNIT), UNIT)]

    def wide_out(u, away):
        goal = lax.rem(mine + away, parts)
        return send(out_scr.at[away, u], out_view(u, mine), osent.at[away, u], ogot.at[away, u], {inner: goal})

    lines = pl.ds(pl.multiple_of(mine * heads, 8), heads)

    def thin_out(away):
        goal = lax.rem(mine + away, parts)
        return send(out_lean(away), slope_ref.at[:, lines], rsent.at[away], rgot.at[away], {inner: goal})

    def out_lean(away):
        goal = lax.rem(mine + away, parts)
        return lean_scr.at[:, :, pl.ds(pl.multiple_of(goal * rows, LANES), rows)]

    def factor_of(u):
        return jnp.where(u // per_pair == 0, scale[0], scale[1])

    def block_of(u, away):
        goal = lax.rem(mine + away, parts)
        return grad_scr[u, pl.ds(pl.multiple_of(HALO + goal * rows, HALO), rows), :]

    def give(u, carry):
        close(u)
        for away in range(1, parts):
            out_scr[away, u] = (factor_of(u) * block_of(u, away)).astype(BF16)
            wide_out(u, away).start()
        return carry

    def late(u, carry):
        post(u)
        give(u - 1, 0)
        return carry

    lax.fori_loop(early, done, give, 0)
    if done < units:
        lax.fori_loop(done + 1, units, late, 0)
        give(jnp.int32(units - 1), 0)
    back_row = iota((BLOCK, BLOCK), 0)
    back_col = iota((BLOCK, BLOCK), 1)
    near = (back_row // CHUNK) == (back_col // CHUNK)
    onward = jnp.where(near & (back_row >= back_col), 1.0, 0.0).astype(BF16)
    for b in range(2):
        for blk in range(count):
            here = pl.ds(blk * BLOCK, BLOCK)
            sums = hd_scr[b, here, :].T
            raw = raw_scr[b, :, here]
            d_log = mm_three(sums[0:heads], onward)
            by_step = sums[heads : 2 * heads] / jax.nn.softplus(raw)
            lean_scr[b, :, here] = scale[b] * jax.nn.sigmoid(raw) * (by_step - rate * d_log)
    for away in range(1, parts):
        thin_out(away).start()
    slope_ref[:, lines, :] = lean_scr[:, :, pl.ds(pl.multiple_of(mine * rows, LANES), rows)]

    def own_store(u):
        return pltpu.make_async_copy(out_scr.at[0, u], out_view(u, mine), stored.at[0, u])

    def take_store(u, away):
        owner = lax.rem(mine + parts - away, parts)
        return pltpu.make_async_copy(take_scr.at[away, u], out_view(u, owner), stored.at[away, u])

    def keep_own(u, carry):
        out_scr[0, u] = (factor_of(u) * block_of(u, 0)).astype(BF16)
        own_store(u).start()
        return carry

    lax.fori_loop(0, units, keep_own, 0)

    def take(u, carry):
        for away in range(1, parts):
            early_out(u, away).wait_recv()
            take_scr[away, u] = (factor_of(u) * wide_scr[away, u]).astype(BF16)
            take_store(u, away).start()
        return carry

    if early > 0:
        lax.fori_loop(0, early, take, 0)

    def drain(u, carry):
        own_store(u).wait()
        for copy in wides(u):
            copy.wait_send()
        for way, (_, _, arrived, _, leaves, goal) in enumerate(ways):

            @pl.when(leaves)
            def _():
                for piece in range(HOPS):
                    chain_copy(way, u, piece, arrived, goal).wait_send()

        @pl.when(has_less)
        def _():
            edge(u).wait_send()

        @pl.when(gives)
        def _():
            for j in range(parts):
                edges(u, j).wait_send()

        return carry

    lax.fori_loop(0, units, drain, 0)

    def drain_early(u, carry):
        for away in range(1, parts):
            early_out(u, away).wait_send()
            take_store(u, away).wait()
        return carry

    def drain_late(u, carry):
        for away in range(1, parts):
            wide_out(u, away).wait()
        return carry

    if early > 0:
        lax.fori_loop(0, early, drain_early, 0)
    lax.fori_loop(early, units, drain_late, 0)
    for spot in range(len(mates)):
        score_copy(spot).wait_send()
    for away in range(1, parts):
        thin_out(away).wait()
    for b in range(2):
        for copy in thins(b):
            copy.wait_send()
    for away in range(1, planes):
        far_copy(away).wait_send()

    @pl.when(gives)
    def _():
        for j in range(parts):
            edge_marks(j).wait_send()


def early_units(units, parts, planes):
    return max(0, min(EARLY, units - planes)) if parts > 1 else 0


def everything(x_in, target, b_in, c_in, dt_raw, resets, rate, conv_w, label, axes, size, width):
    parts = lax.axis_size(axes[1])
    rows = x_in.shape[1]
    tokens = parts * rows
    chans, states, heads = x_in.shape[2] // parts, b_in.shape[2] // parts, dt_raw.shape[1] // parts
    units = 2 * (chans // UNIT)
    count = tokens // BLOCK
    edge = 2 * count + 8
    planes = lax.axis_size(axes[0])
    ring = min(units, planes)
    slots = planes + parts * lax.axis_size(axes[2])
    early = max(1, early_units(units, parts, planes))
    vmem = pl.BlockSpec(memory_space=pltpu.VMEM)
    dma = pltpu.SemaphoreType.DMA

    def v(shape, kind=F32):
        return pltpu.VMEM(shape, kind)

    return pl.pallas_call(
        functools.partial(kernel, axes, size, width),
        out_shape=(
            jax.ShapeDtypeStruct((1, 1), F32),
            jax.ShapeDtypeStruct(x_in.shape, BF16),
            jax.ShapeDtypeStruct(dt_raw.shape, F32),
        ),
        in_specs=[pl.BlockSpec(memory_space=pl.ANY)] * 5 + [vmem] * 3 + [pl.BlockSpec(memory_space=pltpu.SMEM)],
        out_specs=(pl.BlockSpec(memory_space=pltpu.SMEM), pl.BlockSpec(memory_space=pl.ANY), vmem),
        scratch_shapes=[
            v((units, tokens + HALO, UNIT), BF16),
            v((units, tokens, UNIT), BF16),
            v((2, tokens, states), BF16),
            v((2, tokens, states), BF16),
            v((2, heads, tokens)),
            v((2, 8, rows + tokens)),
            v((2, tokens, LANES)),
            v((2, count, BLOCK, 3 * BLOCK), BF16),
            v((2, count, BLOCK, 3 * BLOCK), BF16),
            v((2, count, BLOCK, 2 * DSTATE), BF16),
            v((2, count, BLOCK, 2 * DSTATE), BF16),
            v((2, count, 2 * DSTATE, 2 * BLOCK), BF16),
            v((2, count, 2 * DSTATE, 2 * BLOCK), BF16),
            v((BLOCK + HALO, UNIT)),
            v((ring, tokens, UNIT), BF16),
            v((ring, tokens, UNIT), BF16),
            v((ring, tokens, UNIT), BF16),
            v((ring, tokens, UNIT), BF16),
            v((ring, tokens, UNIT)),
            v((ring, tokens, UNIT)),
            v((ring, 2 * count + 1, DSTATE, UNIT)),
            v((ring, 2 * count + 1, DSTATE, UNIT)),
            v((units, edge, UNIT)),
            v((units, edge, UNIT)),
            v((units, edge, UNIT)),
            v((units, edge, UNIT)),
            v((2, units, DSTATE, UNIT)),
            v((units, DSTATE, UNIT)),
            v((units, DSTATE, UNIT)),
            v((TAPS, tokens + 2 * HALO, UNIT)),
            v((units, tokens + HALO, UNIT)),
            v((2, tokens, LANES)),
            v((2, 8, UNIT)),
            v((units, HALO, UNIT)),
            v((2, 8, LANES)),
            v((slots, 8, LANES)),
            v((parts, units, rows, UNIT), BF16),
            v((2, heads, tokens)),
            v((2, 8, rows)),
            v((parts, early, rows, UNIT)),
            v((parts, early, rows, UNIT), BF16),
            dma((parts, units, 2)),
            dma((parts, units, 2)),
            dma((units, 2)),
            dma((parts, 2, 4)),
            dma((parts, 2, 4)),
            dma((2, 4)),
            dma((parts, units)),
            dma((units,)),
            dma((parts,)),
            dma,
            dma((2, units, HOPS)),
            dma((2, units, HOPS)),
            dma((units,)),
            dma((units,)),
            dma((slots,)),
            dma((slots,)),
            dma((parts, units)),
            dma((parts, units)),
            dma((parts,)),
            dma((parts,)),
            dma((parts, early)),
            dma((parts, early)),
            dma((parts, units)),
        ],
        compiler_params=pltpu.CompilerParams(
            collective_id=0, has_side_effects=True, vmem_limit_bytes=60 * 1024 * 1024
        ),
        name="everything",
    )(x_in, target, b_in, c_in, dt_raw, resets, rate, conv_w, label)


def hand_kernel(pieces, grad_ref, slope_ref, grad_out, slope_out, grad_scr, slope_scr, came, went):
    size = grad_ref.shape[1] // pieces

    def views(b, i):
        here = pl.ds(i * size, size)
        return grad_ref.at[b, here], grad_scr.at[b, here], grad_out.at[b, here]

    chain = [views(b, i) for b in range(2) for i in range(pieces)] + [(slope_ref, slope_scr, slope_out)]
    reads = [pltpu.make_async_copy(a, m, came.at[i]) for i, (a, m, _) in enumerate(chain)]
    writes = [pltpu.make_async_copy(m, c, went.at[i]) for i, (_, m, c) in enumerate(chain)]
    for copy in reads:
        copy.start()
    for read, write in zip(reads, writes):
        read.wait()
        write.start()
    for copy in writes:
        copy.wait()


def hand_over(grad, slope):
    pieces = max(1, grad.shape[1] // (2 * HALO))
    anywhere = pl.BlockSpec(memory_space=pl.ANY)
    dma = pltpu.SemaphoreType.DMA((2 * pieces + 1,))
    return pl.pallas_call(
        functools.partial(hand_kernel, pieces),
        out_shape=(jax.ShapeDtypeStruct(grad.shape, grad.dtype), jax.ShapeDtypeStruct(slope.shape, slope.dtype)),
        in_specs=[anywhere] * 2,
        out_specs=(anywhere,) * 2,
        scratch_shapes=[pltpu.VMEM(grad.shape, grad.dtype), pltpu.VMEM(slope.shape, slope.dtype), dma, dma],
        name="hand_over",
    )(grad, slope)


def body(outer, inner, x_in, target, b_in, c_in, dt_raw, resets, decay_rate, conv_w, label):
    rows = x_in.shape[1]
    width = x_in.shape[2] // dt_raw.shape[1]
    size = rows * lax.axis_size(outer) * lax.axis_size(inner) * x_in.shape[2] * lax.axis_size("head")
    axes = (outer, inner, "head")
    loss, grad, slope = everything(
        x_in, target, b_in, c_in, dt_raw, resets, decay_rate[None], conv_w, label, axes, size, width
    )
    grad, slope = hand_over(grad, slope)
    return (loss[0, 0], grad, slope)


def solution(mesh):
    def program(*arrays):
        ways, across = mesh.shape["seq"], mesh.shape["head"]
        groups = arrays[2].shape[2] // DSTATE // across
        parts = math.gcd(groups, ways)
        devices = mesh.devices.reshape(ways // parts, parts, across)
        finer = Mesh(devices, ("outer", "inner", "head"))
        seq = ("outer", "inner")
        in_specs = (
            P(None, seq, "head"),
            P(None, seq, "head"),
            P(None, seq, "head"),
            P(None, seq, "head"),
            P(None, "head", seq),
            P(None, seq),
            P("head"),
            P(None, "head"),
            P(),
        )
        out_specs = (P(), P(None, seq, "head"), P(None, "head", seq))
        inner = functools.partial(body, "outer", "inner")
        mapped = jax.shard_map(inner, mesh=finer, in_specs=in_specs, out_specs=out_specs, check_vma=False)
        return mapped(*arrays)

    return program
```

```python
import functools
import math

import jax
import jax.numpy as jnp
from jax import lax
from jax.experimental import pallas as pl
from jax.experimental.pallas import tpu as pltpu
from jax.sharding import Mesh
from jax.sharding import PartitionSpec as P

DSTATE = 128
BLOCK = 128
CHUNK = 64
LANES = 128
TAPS = 4
HALO = 16
UNIT = 256
AHEAD = 2
EARLY = 3
HOPS = 1
F32 = jnp.float32
BF16 = jnp.bfloat16


def split(value):
    high = value.astype(BF16)
    low = (value - high.astype(F32)).astype(BF16)
    return high, low


def mm(left, right):
    return lax.dot_general(left, right, (((1,), (0,)), ((), ())), preferred_element_type=F32)


def mm_across(left, right):
    return lax.dot_general(left, right, (((1,), (1,)), ((), ())), preferred_element_type=F32)


def mm_three(left, right):
    high = left.astype(BF16)
    rest = left - high.astype(F32)
    low, least = split(rest)
    return mm(high, right) + mm(low, right) + mm(least, right)


def iota(shape, dim):
    return lax.broadcasted_iota(jnp.int32, shape, dim)


def side(*parts):
    return jnp.concatenate(parts, axis=1)


def stack(*parts):
    return jnp.concatenate(parts, axis=0)


def send(source, goal, sent, got, where):
    return pltpu.make_async_remote_copy(
        src_ref=source,
        dst_ref=goal,
        send_sem=sent,
        recv_sem=got,
        device_id=where,
        device_id_type=pl.DeviceIdType.MESH,
    )


def greet(barrier, where):
    pl.semaphore_signal(barrier, inc=1, device_id=where, device_id_type=pl.DeviceIdType.MESH)


def fold(value):
    return jnp.sum(value.reshape(value.shape[0] // 8, 8, value.shape[1]), axis=0)


def prepare(b, blk, heads, rows, raw_scr, mark_scr, rate, b_scr, c_scr, tok_scr, lm, rm, zc2, qb2, bt2, ct2):
    here = pl.ds(pl.multiple_of(blk * BLOCK, BLOCK), BLOCK)
    later = pl.ds(pl.multiple_of(rows + blk * BLOCK, BLOCK), BLOCK)
    before = pl.ds(pl.multiple_of(rows - BLOCK + blk * BLOCK, BLOCK), BLOCK)
    steps = jax.nn.softplus(raw_scr[b, :, here])
    logs = -steps * rate
    marks = mark_scr[b, :, later]
    keep = 1.0 - side(mark_scr[b, :, before], marks)
    keep_one = keep[:, BLOCK:]
    keep_two = keep_one * pltpu.roll(keep, 1, 1)[:, BLOCK:]
    keep_three = keep_two * pltpu.roll(keep, 2, 1)[:, BLOCK:]
    row = iota((BLOCK, BLOCK), 0)
    col = iota((BLOCK, BLOCK), 1)
    near = (row // CHUNK) == (col // CHUNK)
    upto = jnp.where(near & (row <= col), 1.0, 0.0).astype(BF16)
    full = jnp.where(near, 1.0, 0.0).astype(BF16)
    running = mm_three(logs, upto)
    total = mm_three(logs, full)
    seen = mm(marks.astype(BF16), upto)
    seen_all = mm(marks.astype(BF16), full)
    half = 0.5 * total
    grow = steps * jnp.exp(half - running)
    fall = jnp.exp(running - half)
    center = jnp.exp(half)
    open_all = jnp.where(seen_all == 0.0, 1.0, 0.0).astype(F32)
    through = jnp.exp(total) * open_all[0:1]
    opened = jnp.where(seen == 0.0, 1.0, 0.0).astype(F32)
    closing = jnp.where(seen == seen_all, 1.0, 0.0).astype(F32)
    line = iota((8, BLOCK), 0)
    extra = jnp.zeros((8, BLOCK), F32)
    for i, value in enumerate((keep_one, keep_two, keep_three, seen, opened, closing)):
        extra = jnp.where(line == i, value, extra)
    table = stack(grow, fall, center, through, extra, jnp.zeros((LANES - 4 * heads - 8, BLOCK), F32))
    tok = table.T
    tok_scr[b, here, :] = tok
    base = 4 * heads
    b_rows = b_scr[b, here, :]
    c_rows = c_scr[b, here, :]
    scores = mm_across(c_rows, b_rows)
    scores_t = mm_across(b_rows, c_rows)
    same = near & (tok[:, base + 3 : base + 4] == seen[0:1, :])
    m_high, m_low = split(jnp.where(same & (row >= col), scores, 0.0))
    n_high, n_low = split(jnp.where(same & (row <= col), scores_t, 0.0))
    lm[b, blk] = side(m_high, m_low, m_high)
    rm[b, blk] = side(n_high, n_low, n_high)
    for value, mask, twice, turned in ((c_rows, base + 4, zc2, ct2), (b_rows, base + 5, qb2, bt2)):
        masked = value.astype(F32) * tok[:, mask : mask + 1]
        short = masked.astype(BF16)
        twice[b, blk] = side(short, short)
        flipped = masked.T
        lane = iota((DSTATE, BLOCK), 1)
        one = jnp.where(lane < CHUNK, flipped, 0.0).astype(BF16)
        two = jnp.where(lane >= CHUNK, flipped, 0.0).astype(BF16)
        turned[b, blk] = stack(side(one, one), side(two, two))


def before_chain(
    u, r, b, q, heads, width, count, taps, x_scr, t_scr, tok_scr, lm, bt2, ct2, xe_scr,
    wh, wl, vh, vl, pk, yi, s_loc, g_loc, p_row, r_row, d_row, th_row, score_scr,
):
    chans = UNIT
    per = chans // width
    row = iota((LANES, chans), 0)
    head = iota((LANES, chans), 1) // width + q * per

    def spread(offset):
        one = jnp.where(row == head + offset, 1.0, 0.0).astype(BF16)
        return stack(one, one)

    spread_grow, spread_fall = spread(0), spread(heads)
    spread_center, spread_through = spread(2 * heads), spread(3 * heads)
    base = 4 * heads
    s_loc[r, 0] = jnp.zeros((DSTATE, chans), F32)
    g_loc[r, 2 * count] = jnp.zeros((DSTATE, chans), F32)

    def forward(blk, through):
        first = pl.multiple_of(blk * BLOCK, BLOCK)
        here = pl.ds(first, BLOCK)
        tok = tok_scr[b, here, :]
        both = side(*split(tok))
        ends = stack(both[0:16], both[CHUNK : CHUNK + 16])
        grow = mm(both, spread_grow)
        fall = mm(both, spread_fall)
        center = mm(ends, spread_center)
        pass_by = mm(ends, spread_through)
        xe_scr[...] = x_scr[u, pl.ds(first, BLOCK + HALO), :].astype(F32)
        pre = taps[3:4, :] * xe_scr[pl.ds(HALO, BLOCK), :]
        for back in range(1, TAPS):
            scale = tok[:, base + back - 1 : base + back] * taps[3 - back : 4 - back, :]
            pre = pre + scale * xe_scr[pl.ds(HALO - back, BLOCK), :]
        sig = jax.nn.sigmoid(pre)
        values = pre * sig
        slope = sig + values * (1.0 - sig)
        w_high, w_low = split(grow * values)
        v = fall * t_scr[u, here, :].astype(F32)
        v_high, v_low = split(v)
        wh[r, here, :] = w_high
        wl[r, here, :] = w_low
        vh[r, here, :] = v_high
        vl[r, here, :] = v_low
        pk[r, here, :] = grow * slope
        inside = mm(lm[b, blk], stack(w_high, w_high, w_low))
        yi[r, here, :] = inside
        score_scr[b] += fold(v * inside)
        added = mm(bt2[b, blk], stack(w_high, w_low))
        state = s_loc[r, 2 * blk]
        for sub in range(2):
            k = 2 * blk + sub
            c_one = center[16 * sub : 16 * sub + 1, :]
            t_one = pass_by[16 * sub : 16 * sub + 1, :]
            p_row[u, pl.ds(k, 1), :] = through
            d_row[u, pl.ds(k, 1), :] = c_one
            th_row[u, pl.ds(k, 1), :] = t_one
            through = through * t_one
            state = t_one * state + c_one * added[DSTATE * sub : DSTATE * (sub + 1), :]
            s_loc[r, k + 1] = state
        return through

    through = lax.fori_loop(0, count, forward, jnp.ones((1, chans), F32))
    p_row[u, 2 * count : 2 * count + 1, :] = through

    def backward(step, through):
        blk = count - 1 - step
        here = pl.ds(pl.multiple_of(blk * BLOCK, BLOCK), BLOCK)
        added = mm(ct2[b, blk], stack(vh[r, here, :], vl[r, here, :]))
        state = g_loc[r, 2 * blk + 2]
        for sub in (1, 0):
            k = 2 * blk + sub
            t_one = th_row[u, pl.ds(k, 1), :]
            r_row[u, pl.ds(k + 1, 1), :] = through
            through = through * t_one
            fresh = d_row[u, pl.ds(k, 1), :] * added[DSTATE * sub : DSTATE * (sub + 1), :]
            score_scr[b] += fold(s_loc[r, k] * fresh)
            state = t_one * state + fresh
            g_loc[r, k] = state
        return through

    lax.fori_loop(0, count, backward, jnp.ones((1, chans), F32))


def after_chain(
    u, r, b, q, heads, width, count, taps, tok_scr, rm, zc2, qb2,
    wh, wl, vh, vl, pk, yi, s_loc, g_loc, p_row, r_row, d_row, start_scr, later_scr, cv_scr, grad_scr, hd_scr,
    between,
):
    chans = UNIT
    per = chans // width
    base = 4 * heads
    lane_head = iota((chans, LANES), 0) // width + q * per
    col = iota((chans, LANES), 1)
    pick_diff = jnp.where(col == lane_head, 1.0, 0.0).astype(BF16)
    pick_step = jnp.where(col == lane_head + heads, 1.0, 0.0).astype(BF16)
    pick = stack(pick_diff, pick_diff, pick_step, pick_step)
    tokens = count * BLOCK
    for back in range(TAPS):
        cv_scr[back, pl.ds(0, HALO), :] = jnp.zeros((HALO, chans), F32)
        cv_scr[back, pl.ds(HALO + tokens, HALO), :] = jnp.zeros((HALO, chans), F32)
    line = iota((BLOCK, chans), 0)

    def block(blk, carry):
        if between is not None:
            pl.when(blk == count - 1)(between)

        first = pl.multiple_of(blk * BLOCK, BLOCK)
        here = pl.ds(first, BLOCK)
        start = start_scr[u]
        later = later_scr[u]
        w_high, w_low = wh[r, here, :], wl[r, here, :]
        v_high, v_low = vh[r, here, :], vl[r, here, :]
        y_all, d_all, crossed = [], [], []
        state = s_loc[r, 2 * blk] + p_row[u, pl.ds(2 * blk, 1), :] * start
        for sub in range(2):
            k = 2 * blk + sub
            center = d_row[u, pl.ds(k, 1), :]
            rows = pl.ds(sub * CHUNK, CHUNK)
            slope = g_loc[r, k + 1] + r_row[u, pl.ds(k + 1, 1), :] * later
            after = s_loc[r, k + 1] + p_row[u, pl.ds(k + 1, 1), :] * start
            y_all.append(mm(zc2[b, blk, rows, :], stack(*split(center * state))))
            d_all.append(mm(qb2[b, blk, rows, :], stack(*split(center * slope))))
            crossed.append(jnp.sum(after * slope, axis=0, keepdims=True))
            state = after
        y_in = yi[r, here, :] + stack(*y_all)
        d_in = mm(rm[b, blk], stack(v_high, v_high, v_low)) + stack(*d_all)
        read = (v_high.astype(F32) + v_low.astype(F32)) * y_in
        stepped = (w_high.astype(F32) + w_low.astype(F32)) * d_in
        diff = read - stepped
        diff = jnp.where(line == CHUNK - 1, diff + crossed[0], diff)
        diff = jnp.where(line == BLOCK - 1, diff + crossed[1], diff)
        hd_scr[b, here, :] += mm(side(*split(diff), *split(stepped)), pick)
        d_pre = pk[r, here, :] * d_in
        tok = tok_scr[b, here, :]
        below = pl.ds(pl.multiple_of(HALO + blk * BLOCK, HALO), BLOCK)
        cv_scr[0, below, :] = taps[3:4, :] * d_pre
        for back in range(1, TAPS):
            scale = tok[:, base + back - 1 : base + back] * taps[3 - back : 4 - back, :]
            cv_scr[back, below, :] = scale * d_pre
        return carry

    lax.fori_loop(0, count, block, 0)
    for begin, size in [(0, HALO)] + [(HALO + i * BLOCK, BLOCK) for i in range(count)]:
        total = cv_scr[0, pl.ds(begin, size), :]
        for back in range(1, TAPS):
            total = total + cv_scr[back, pl.ds(begin + back, size), :]
        grad_scr[u, pl.ds(begin, size), :] = total


def kernel(
    axes, size, width,
    x_ref, t_ref, b_ref, c_ref, raw_ref, reset_ref, rate_ref, w_ref, label_ref,
    loss_ref, out_ref, slope_ref,
    x_scr, t_scr, b_scr, c_scr, raw_scr, mark_scr, tok_scr, lm, rm, zc2, qb2, bt2, ct2, xe_scr,
    wh, wl, vh, vl, pk, yi, s_loc, g_loc, p_row, r_row, d_row, th_row, chain_out, start_scr, later_scr,
    cv_scr, grad_scr, hd_scr, score_scr, halo_scr, part_scr, slot_scr, out_scr, lean_scr, mark_ref, wide_scr, take_scr,
    wsent, wgot, wkept, nsent, ngot, nkept, hsent, hgot, msent, mgot, csent, cgot,
    esent, egot, psent, pgot, osent, ogot, rsent, rgot, fsent, fgot, stored,
):
    outer, inner, cores = axes
    units, tokens = t_scr.shape[0], t_scr.shape[1]
    ring = wh.shape[0]
    rows = x_ref.shape[1]
    states, heads = b_scr.shape[2], raw_scr.shape[1]
    per_pair = units // 2
    chans = per_pair * UNIT
    count = tokens // BLOCK
    parts, planes = lax.axis_size(inner), lax.axis_size(outer)
    mine, plane = lax.axis_index(inner), lax.axis_index(outer)
    has_less = plane > 0
    has_more = plane < planes - 1
    gives = has_more & (mine == parts - 1)
    less, more = lax.rem(plane + planes - 1, planes), lax.rem(plane + 1, planes)
    barrier = pltpu.get_barrier_semaphore()
    across, core = lax.axis_size(cores), lax.axis_index(cores)
    mates = [(i, h) for i in range(parts) for h in range(across)][1:]

    def mate(i, h):
        return {inner: lax.rem(mine + i, parts), cores: lax.rem(core + h, across)}

    for i, h in mates:
        greet(barrier, mate(i, h))
    for away in range(1, planes):
        greet(barrier, {outer: lax.rem(plane + away, planes)})
    peers = len(mates) + planes - 1

    @pl.when(has_less)
    def _():
        greet(barrier, {outer: less, inner: parts - 1})

    @pl.when(gives)
    def _():
        for j in range(parts):
            greet(barrier, {outer: more, inner: j})

    pl.semaphore_wait(barrier, peers + has_less.astype(jnp.int32) + parts * gives.astype(jnp.int32))

    for b in range(2):
        mark_ref[b] = jnp.broadcast_to(reset_ref[b : b + 1, :].astype(F32), (8, rows))

    def wide_views(u, source, goal):
        b, q = u // per_pair, lax.rem(u, per_pair)
        wide = pl.ds(pl.multiple_of(goal * chans + q * UNIT, UNIT), UNIT)
        yield x_ref.at[b, :, wide], x_scr.at[u, pl.ds(pl.multiple_of(HALO + source * rows, HALO), rows)]
        yield t_ref.at[b, :, wide], t_scr.at[u, pl.ds(pl.multiple_of(source * rows, HALO), rows)]

    def thin_views(b, source, goal):
        group = pl.ds(pl.multiple_of(goal * states, LANES), states)
        lines = pl.ds(pl.multiple_of(goal * heads, 8), heads)
        here = pl.ds(pl.multiple_of(source * rows, LANES), rows)
        later = pl.ds(pl.multiple_of(rows + source * rows, LANES), rows)
        yield b_ref.at[b, :, group], b_scr.at[b, here]
        yield c_ref.at[b, :, group], c_scr.at[b, here]
        yield raw_ref.at[b, lines], raw_scr.at[b, :, here]
        yield mark_ref.at[b], mark_scr.at[b, :, later]

    def remote(views, index, sent, got):
        for away in range(1, parts):
            goal = lax.rem(mine + away, parts)
            for i, (source, target) in enumerate(views(index, mine, goal)):
                yield send(source, target, sent.at[away, index, i], got.at[away, index, i], {inner: goal})

    def local(views, index, kept):
        for i, (source, target) in enumerate(views(index, mine, mine)):
            yield pltpu.make_async_copy(source, target, kept.at[index, i])

    wides = functools.partial(remote, wide_views, sent=wsent, got=wgot)
    thins = functools.partial(remote, thin_views, sent=nsent, got=ngot)

    def edges(u, j):
        b, q = u // per_pair, lax.rem(u, per_pair)
        wide = pl.ds(pl.multiple_of(j * chans + q * UNIT, UNIT), UNIT)
        return send(
            x_ref.at[b, pl.ds(rows - HALO, HALO), wide], x_scr.at[u, pl.ds(0, HALO)],
            hsent.at[j, u], hgot.at[u], {outer: more, inner: j},
        )

    def edge_marks(j):
        return send(mark_ref, mark_scr.at[:, :, pl.ds(0, rows)], msent.at[j], mgot, {outer: more, inner: j})

    def issue(u):
        for copy in wides(u):
            copy.start()
        for copy in local(wide_views, u, wkept):
            copy.start()

    @pl.when(gives)
    def _():
        for j in range(parts):
            edge_marks(j).start()

    def issue_thin(b):
        for copy in thins(b):
            copy.start()
        for copy in local(thin_views, b, nkept):
            copy.start()

    for b in range(1):
        issue_thin(b)
        if b == 0:
            for u in range(min(AHEAD, units)):
                issue(u)

    @pl.when(gives)
    def _():
        def one(u, carry):
            for j in range(parts):
                edges(u, j).start()
            return carry

        lax.fori_loop(0, units, one, 0)

    @pl.when(has_less)
    def _():
        edge_marks(0).wait_recv()

    @pl.when(jnp.logical_not(has_less))
    def _():
        x_scr[:, pl.ds(0, HALO), :] = jnp.zeros((units, HALO, UNIT), BF16)
        mark_scr[:, :, pl.ds(0, rows)] = jnp.zeros((2, 8, rows), F32)

    score_scr[...] = jnp.zeros_like(score_scr)
    hd_scr[...] = jnp.zeros_like(hd_scr)
    ours = iota((heads, rate_ref.shape[1]), 0) + mine * heads == iota((heads, rate_ref.shape[1]), 1)
    rate = jnp.sum(jnp.where(ours, rate_ref[...], 0.0), axis=1, keepdims=True)
    through_row = pl.ds(2 * count, 1)
    ways = ((s_loc, 2 * count, start_scr, has_less, has_more, more), (g_loc, 0, later_scr, has_more, has_less, less))
    for _, _, arrived, arrives, _, _ in ways:

        @pl.when(jnp.logical_not(arrives))
        def _():
            arrived[...] = jnp.zeros(arrived.shape, F32)

    def piece_rows(piece):
        return pl.ds(piece * (DSTATE // HOPS), DSTATE // HOPS)

    def chain_copy(way, u, piece, arrived, goal):
        lines = piece_rows(piece)
        source, target = chain_out.at[way, u, lines], arrived.at[u, lines]
        return send(source, target, csent.at[way, u, piece], cgot.at[way, u, piece], {outer: goal})

    def edge(u):
        return send(grad_scr.at[u, pl.ds(0, HALO)], halo_scr.at[u], esent.at[u], egot.at[u], {outer: less})

    def taps_of(q):
        return w_ref[:, pl.ds(pl.multiple_of(mine * chans + q * UNIT, UNIT), UNIT)]

    early = early_units(units, parts, planes)

    def early_out(u, away):
        goal = lax.rem(mine + away, parts)
        source = grad_scr.at[u, pl.ds(pl.multiple_of(HALO + goal * rows, HALO), rows)]
        return send(source, wide_scr.at[away, u], fsent.at[away, u], fgot.at[away, u], {inner: goal})

    def close(u):
        @pl.when(has_more)
        def _():
            edge(u).wait_recv()
            grad_scr[u, pl.ds(tokens, HALO), :] += halo_scr[u]

    def score_copy(spot):
        slot = slot_scr.at[mine * across + core]
        return send(part_scr.at[0], slot, psent.at[spot], pgot.at[spot], mate(*mates[spot]))

    base = parts * across

    def far_copy(away):
        goal = lax.rem(plane + away, planes)
        spot = base + away - 1
        return send(part_scr.at[1], slot_scr.at[base + plane], psent.at[spot], pgot.at[spot], {outer: goal})

    def sum_mates():
        for spot in range(len(mates)):
            score_copy(spot).wait_recv()
        subtotal = slot_scr[0]
        for i in range(1, parts * across):
            subtotal = subtotal + slot_scr[i]
        part_scr[1] = subtotal
        slot_scr[base + plane] = subtotal
        for away in range(1, planes):
            far_copy(away).start()

    def post(u, between=None):
        b, q = u // per_pair, lax.rem(u, per_pair)
        after_chain(
            u, lax.rem(u, ring), b, q, heads, width, count, taps_of(q), tok_scr, rm, zc2, qb2,
            wh, wl, vh, vl, pk, yi, s_loc, g_loc, p_row, r_row, d_row, start_scr, later_scr, cv_scr, grad_scr,
            hd_scr, between,
        )

        @pl.when(has_less)
        def _():
            edge(u).start()

    middle = (planes + 1) // 2

    def hop(time, carry):
        for piece, way in [(piece, way) for piece in range(HOPS) for way in range(2)]:
            own, end, arrived, arrives, leaves, goal = ways[way]
            lines = piece_rows(piece)
            u = time - (plane if way == 0 else planes - 1 - plane)

            @pl.when((u >= 0) & (u < units))
            def _():
                copy = chain_copy(way, u, piece, arrived, goal)

                @pl.when(arrives)
                def _():
                    copy.wait_recv()

                    @pl.when(plane < middle if way == 0 else plane >= middle)
                    def _():
                        far = g_loc if way == 0 else s_loc
                        end_now = 0 if way == 0 else 2 * count
                        met = far[lax.rem(u, ring), end_now, lines, :]
                        score_scr[u // per_pair] += fold(arrived[u, lines, :] * met)

                    if way == 0:

                        @pl.when(plane == middle)
                        def _():
                            score_scr[u // per_pair] += fold(arrived[u, lines, :] * chain_out[1, u, lines, :])

                @pl.when(leaves)
                def _():
                    mine_now = own[lax.rem(u, ring), end, lines, :]
                    chain_out[way, u, lines, :] = p_row[u, through_row, :] * arrived[u, lines, :] + mine_now
                    copy.start()

        return carry

    def turn(time, carry):
        @pl.when(time == max(0, per_pair - AHEAD))
        def _():
            issue_thin(1)

        @pl.when(time + AHEAD < units)
        def _():
            issue(time + AHEAD)

        @pl.when(time < units)
        def _():
            u = time
            b, q = u // per_pair, lax.rem(u, per_pair)

            @pl.when(q == 0)
            def _():
                for copy in thins(b):
                    copy.wait_recv()
                for copy in local(thin_views, b, nkept):
                    copy.wait()

                def one(blk, carry):
                    prepare(
                        b, blk, heads, rows, raw_scr, mark_scr, rate, b_scr, c_scr, tok_scr, lm, rm, zc2, qb2, bt2, ct2
                    )
                    return carry

                lax.fori_loop(0, count, one, 0)

            for copy in wides(u):
                copy.wait_recv()
            for copy in local(wide_views, u, wkept):
                copy.wait()

            @pl.when(has_less)
            def _():
                edges(u, 0).wait_recv()

            if early > 0:

                @pl.when(u == units - 1)
                def _():
                    def one(i, carry):
                        close(i)
                        for away in range(1, parts):
                            early_out(i, away).start()
                        return carry

                    lax.fori_loop(0, early, one, 0)

            before_chain(
                u, lax.rem(u, ring), b, q, heads, width, count, taps_of(q), x_scr, t_scr, tok_scr, lm, bt2, ct2, xe_scr,
                wh, wl, vh, vl, pk, yi, s_loc, g_loc, p_row, r_row, d_row, th_row, score_scr,
            )

        hop(time, 0)
        u = time - (planes - 1)

        @pl.when((u >= 0) & (time < units))
        def _():
            post(u)

        return carry

    known = min(units + middle, units + planes - 1)
    lax.fori_loop(0, known, turn, 0)
    own = [jnp.sum(jnp.sum(score_scr[i], axis=0, keepdims=True), axis=1, keepdims=True) for i in range(2)]
    part = jnp.where(iota((8, LANES), 0) == 0, own[0], own[1])
    part_scr[0] = part
    slot_scr[mine * across + core] = part
    for spot in range(len(mates)):
        score_copy(spot).start()
    done = max(0, units - planes + 1)
    ready = done + planes - 1 < known
    if not ready:
        lax.fori_loop(known, units + planes - 1, hop, 0)
    if done < units:
        post(jnp.int32(done), sum_mates)
    else:
        sum_mates()
    if ready:
        lax.fori_loop(known, units + planes - 1, hop, 0)
    for away in range(1, planes):
        far_copy(away).wait_recv()
    subtotal = slot_scr[base]
    for i in range(1, planes):
        subtotal = subtotal + slot_scr[base + i]
    row = iota((8, LANES), 0)
    sign = jnp.where(row == label_ref[0], 1.0, jnp.where(row < 2, -1.0, 0.0)).astype(F32)
    signed = subtotal * sign / math.sqrt(size)
    margin = signed[0:1, :] + signed[1:2, :]
    loss_ref[0, 0] = jax.nn.softplus(-margin)[0, 0]
    factors = -jax.nn.sigmoid(-margin) * sign
    scale = [factors[b : b + 1, 0:1] for b in range(2)]

    def out_view(u, owner):
        b, q = u // per_pair, lax.rem(u, per_pair)
        return out_ref.at[b, :, pl.ds(pl.multiple_of(owner * chans + q * UNIT, UNIT), UNIT)]

    def wide_out(u, away):
        goal = lax.rem(mine + away, parts)
        return send(out_scr.at[away, u], out_view(u, mine), osent.at[away, u], ogot.at[away, u], {inner: goal})

    lines = pl.ds(pl.multiple_of(mine * heads, 8), heads)

    def thin_out(away):
        goal = lax.rem(mine + away, parts)
        return send(out_lean(away), slope_ref.at[:, lines], rsent.at[away], rgot.at[away], {inner: goal})

    def out_lean(away):
        goal = lax.rem(mine + away, parts)
        return lean_scr.at[:, :, pl.ds(pl.multiple_of(goal * rows, LANES), rows)]

    def factor_of(u):
        return jnp.where(u // per_pair == 0, scale[0], scale[1])

    def block_of(u, away):
        goal = lax.rem(mine + away, parts)
        return grad_scr[u, pl.ds(pl.multiple_of(HALO + goal * rows, HALO), rows), :]

    def give(u, carry):
        close(u)
        for away in range(1, parts):
            out_scr[away, u] = (factor_of(u) * block_of(u, away)).astype(BF16)
            wide_out(u, away).start()
        return carry

    def late(u, carry):
        post(u)
        give(u - 1, 0)
        return carry

    lax.fori_loop(early, done, give, 0)
    if done < units:
        lax.fori_loop(done + 1, units, late, 0)
        give(jnp.int32(units - 1), 0)
    back_row = iota((BLOCK, BLOCK), 0)
    back_col = iota((BLOCK, BLOCK), 1)
    near = (back_row // CHUNK) == (back_col // CHUNK)
    onward = jnp.where(near & (back_row >= back_col), 1.0, 0.0).astype(BF16)
    for b in range(2):
        for blk in range(count):
            here = pl.ds(blk * BLOCK, BLOCK)
            sums = hd_scr[b, here, :].T
            raw = raw_scr[b, :, here]
            d_log = mm_three(sums[0:heads], onward)
            by_step = sums[heads : 2 * heads] / jax.nn.softplus(raw)
            lean_scr[b, :, here] = scale[b] * jax.nn.sigmoid(raw) * (by_step - rate * d_log)
    for away in range(1, parts):
        thin_out(away).start()
    slope_ref[:, lines, :] = lean_scr[:, :, pl.ds(pl.multiple_of(mine * rows, LANES), rows)]

    def own_store(u):
        return pltpu.make_async_copy(out_scr.at[0, u], out_view(u, mine), stored.at[0, u])

    def take_store(u, away):
        owner = lax.rem(mine + parts - away, parts)
        return pltpu.make_async_copy(take_scr.at[away, u], out_view(u, owner), stored.at[away, u])

    def keep_own(u, carry):
        out_scr[0, u] = (factor_of(u) * block_of(u, 0)).astype(BF16)
        own_store(u).start()
        return carry

    lax.fori_loop(0, units, keep_own, 0)

    def take(u, carry):
        for away in range(1, parts):
            early_out(u, away).wait_recv()
            take_scr[away, u] = (factor_of(u) * wide_scr[away, u]).astype(BF16)
            take_store(u, away).start()
        return carry

    if early > 0:
        lax.fori_loop(0, early, take, 0)

    def drain(u, carry):
        own_store(u).wait()
        for copy in wides(u):
            copy.wait_send()
        for way, (_, _, arrived, _, leaves, goal) in enumerate(ways):

            @pl.when(leaves)
            def _():
                for piece in range(HOPS):
                    chain_copy(way, u, piece, arrived, goal).wait_send()

        @pl.when(has_less)
        def _():
            edge(u).wait_send()

        @pl.when(gives)
        def _():
            for j in range(parts):
                edges(u, j).wait_send()

        return carry

    lax.fori_loop(0, units, drain, 0)

    def drain_early(u, carry):
        for away in range(1, parts):
            early_out(u, away).wait_send()
            take_store(u, away).wait()
        return carry

    def drain_late(u, carry):
        for away in range(1, parts):
            wide_out(u, away).wait()
        return carry

    if early > 0:
        lax.fori_loop(0, early, drain_early, 0)
    lax.fori_loop(early, units, drain_late, 0)
    for spot in range(len(mates)):
        score_copy(spot).wait_send()
    for away in range(1, parts):
        thin_out(away).wait()
    for b in range(2):
        for copy in thins(b):
            copy.wait_send()
    for away in range(1, planes):
        far_copy(away).wait_send()

    @pl.when(gives)
    def _():
        for j in range(parts):
            edge_marks(j).wait_send()


def early_units(units, parts, planes):
    return max(0, min(EARLY, units - planes)) if parts > 1 else 0


def everything(x_in, target, b_in, c_in, dt_raw, resets, rate, conv_w, label, axes, size, width):
    parts = lax.axis_size(axes[1])
    rows = x_in.shape[1]
    tokens = parts * rows
    chans, states, heads = x_in.shape[2] // parts, b_in.shape[2] // parts, dt_raw.shape[1] // parts
    units = 2 * (chans // UNIT)
    count = tokens // BLOCK
    edge = 2 * count + 8
    planes = lax.axis_size(axes[0])
    ring = min(units, planes)
    slots = planes + parts * lax.axis_size(axes[2])
    early = max(1, early_units(units, parts, planes))
    vmem = pl.BlockSpec(memory_space=pltpu.VMEM)
    dma = pltpu.SemaphoreType.DMA

    def v(shape, kind=F32):
        return pltpu.VMEM(shape, kind)

    return pl.pallas_call(
        functools.partial(kernel, axes, size, width),
        out_shape=(
            jax.ShapeDtypeStruct((1, 1), F32),
            jax.ShapeDtypeStruct(x_in.shape, BF16),
            jax.ShapeDtypeStruct(dt_raw.shape, F32),
        ),
        in_specs=[pl.BlockSpec(memory_space=pl.ANY)] * 5 + [vmem] * 3 + [pl.BlockSpec(memory_space=pltpu.SMEM)],
        out_specs=(pl.BlockSpec(memory_space=pltpu.SMEM), pl.BlockSpec(memory_space=pl.ANY), vmem),
        scratch_shapes=[
            v((units, tokens + HALO, UNIT), BF16),
            v((units, tokens, UNIT), BF16),
            v((2, tokens, states), BF16),
            v((2, tokens, states), BF16),
            v((2, heads, tokens)),
            v((2, 8, rows + tokens)),
            v((2, tokens, LANES)),
            v((2, count, BLOCK, 3 * BLOCK), BF16),
            v((2, count, BLOCK, 3 * BLOCK), BF16),
            v((2, count, BLOCK, 2 * DSTATE), BF16),
            v((2, count, BLOCK, 2 * DSTATE), BF16),
            v((2, count, 2 * DSTATE, 2 * BLOCK), BF16),
            v((2, count, 2 * DSTATE, 2 * BLOCK), BF16),
            v((BLOCK + HALO, UNIT)),
            v((ring, tokens, UNIT), BF16),
            v((ring, tokens, UNIT), BF16),
            v((ring, tokens, UNIT), BF16),
            v((ring, tokens, UNIT), BF16),
            v((ring, tokens, UNIT)),
            v((ring, tokens, UNIT)),
            v((ring, 2 * count + 1, DSTATE, UNIT)),
            v((ring, 2 * count + 1, DSTATE, UNIT)),
            v((units, edge, UNIT)),
            v((units, edge, UNIT)),
            v((units, edge, UNIT)),
            v((units, edge, UNIT)),
            v((2, units, DSTATE, UNIT)),
            v((units, DSTATE, UNIT)),
            v((units, DSTATE, UNIT)),
            v((TAPS, tokens + 2 * HALO, UNIT)),
            v((units, tokens + HALO, UNIT)),
            v((2, tokens, LANES)),
            v((2, 8, UNIT)),
            v((units, HALO, UNIT)),
            v((2, 8, LANES)),
            v((slots, 8, LANES)),
            v((parts, units, rows, UNIT), BF16),
            v((2, heads, tokens)),
            v((2, 8, rows)),
            v((parts, early, rows, UNIT)),
            v((parts, early, rows, UNIT), BF16),
            dma((parts, units, 2)),
            dma((parts, units, 2)),
            dma((units, 2)),
            dma((parts, 2, 4)),
            dma((parts, 2, 4)),
            dma((2, 4)),
            dma((parts, units)),
            dma((units,)),
            dma((parts,)),
            dma,
            dma((2, units, HOPS)),
            dma((2, units, HOPS)),
            dma((units,)),
            dma((units,)),
            dma((slots,)),
            dma((slots,)),
            dma((parts, units)),
            dma((parts, units)),
            dma((parts,)),
            dma((parts,)),
            dma((parts, early)),
            dma((parts, early)),
            dma((parts, units)),
        ],
        compiler_params=pltpu.CompilerParams(
            collective_id=0, has_side_effects=True, vmem_limit_bytes=60 * 1024 * 1024
        ),
        name="everything",
    )(x_in, target, b_in, c_in, dt_raw, resets, rate, conv_w, label)


def hand_kernel(pieces, grad_ref, slope_ref, grad_out, slope_out, grad_scr, slope_scr, came, went):
    size = grad_ref.shape[1] // pieces

    def views(b, i):
        here = pl.ds(i * size, size)
        return grad_ref.at[b, here], grad_scr.at[b, here], grad_out.at[b, here]

    chain = [views(b, i) for b in range(2) for i in range(pieces)] + [(slope_ref, slope_scr, slope_out)]
    reads = [pltpu.make_async_copy(a, m, came.at[i]) for i, (a, m, _) in enumerate(chain)]
    writes = [pltpu.make_async_copy(m, c, went.at[i]) for i, (_, m, c) in enumerate(chain)]
    for copy in reads:
        copy.start()
    for read, write in zip(reads, writes):
        read.wait()
        write.start()
    for copy in writes:
        copy.wait()


def hand_over(grad, slope):
    pieces = max(1, grad.shape[1] // (2 * HALO))
    anywhere = pl.BlockSpec(memory_space=pl.ANY)
    dma = pltpu.SemaphoreType.DMA((2 * pieces + 1,))
    return pl.pallas_call(
        functools.partial(hand_kernel, pieces),
        out_shape=(jax.ShapeDtypeStruct(grad.shape, grad.dtype), jax.ShapeDtypeStruct(slope.shape, slope.dtype)),
        in_specs=[anywhere] * 2,
        out_specs=(anywhere,) * 2,
        scratch_shapes=[pltpu.VMEM(grad.shape, grad.dtype), pltpu.VMEM(slope.shape, slope.dtype), dma, dma],
        name="hand_over",
    )(grad, slope)


def body(outer, inner, x_in, target, b_in, c_in, dt_raw, resets, decay_rate, conv_w, label):
    rows = x_in.shape[1]
    width = x_in.shape[2] // dt_raw.shape[1]
    size = rows * lax.axis_size(outer) * lax.axis_size(inner) * x_in.shape[2] * lax.axis_size("head")
    axes = (outer, inner, "head")
    loss, grad, slope = everything(
        x_in, target, b_in, c_in, dt_raw, resets, decay_rate[None], conv_w, label, axes, size, width
    )
    grad, slope = hand_over(grad, slope)
    return (loss[0, 0], grad, slope)


def solution(mesh):
    def program(*arrays):
        ways, across = mesh.shape["seq"], mesh.shape["head"]
        groups = arrays[2].shape[2] // DSTATE // across
        parts = math.gcd(groups, ways)
        devices = mesh.devices.reshape(ways // parts, parts, across)
        finer = Mesh(devices, ("outer", "inner", "head"))
        seq = ("outer", "inner")
        in_specs = (
            P(None, seq, "head"),
            P(None, seq, "head"),
            P(None, seq, "head"),
            P(None, seq, "head"),
            P(None, "head", seq),
            P(None, seq),
            P("head"),
            P(None, "head"),
            P(),
        )
        out_specs = (P(), P(None, seq, "head"), P(None, "head", seq))
        inner = functools.partial(body, "outer", "inner")
        mapped = jax.shard_map(inner, mesh=finer, in_specs=in_specs, out_specs=out_specs, check_vma=False)
        return mapped(*arrays)

    return program
```
